32 devices in a mesh: dp: 8 (over z, y), tensor: 4 (over x, core).
Axes of the slice: x: 2, y: 2, z: 4, core: 2. Of those that a mesh axis runs over, the one named last changes fastest.
Arguments:
- tokens: bfloat16 [32768, 768], P(('dp', 'tensor')), may hold values from -6 to 6
- doc_lengths: int32 [32, 16], P('dp'), may hold values from 1 to 512, 1024 in all within a row
- w_query: bfloat16 [768, 768], P('dp', 'tensor'), may hold values from -0.21875 to 0.21875
- w_key: bfloat16 [768, 768], P('dp', 'tensor'), may hold values from -0.21875 to 0.21875
- w_value: bfloat16 [768, 768], P('dp', 'tensor'), may hold values from -0.21875 to 0.21875
- w_out: bfloat16 [768, 768], P('tensor', 'dp'), may hold values from -1.25 to 1.25
- w_up: bfloat16 [768, 3072], P('dp', 'tensor'), may hold values from -0.21875 to 0.21875
- w_down: bfloat16 [3072, 768], P('tensor', 'dp'), may hold values from -0.109375 to 0.109375
- b_query: bfloat16 [12, 64], P('tensor', 'dp'), may hold values from -3 to 3
- b_value: bfloat16 [12, 64], P('tensor', 'dp'), may hold values from -3 to 3
- b_up: bfloat16 [24, 128], P('tensor', 'dp'), may hold values from -3 to 3
- b_out: float32 [768], P(('dp', 'tensor')), may hold values from -3 to 3
- b_down: float32 [768], P(('dp', 'tensor')), may hold values from -3 to 3
- gain_one: float32 [768], P(('dp', 'tensor')), may hold values from 0.1 to 1.9
- shift_one: float32 [768], P(('dp', 'tensor')), may hold values from -3 to 3
- gain_two: float32 [768], P(('dp', 'tensor')), may hold values from 0.1 to 1.9
- shift_two: float32 [768], P(('dp', 'tensor')), may hold values from -3 to 3
- cotangent: bfloat16 [32768, 768], P(('dp', 'tensor')), may hold values from -6 to 6
Outputs:
- layer_out: bfloat16 [32768, 768], P(('dp', 'tensor'))
- grad_tokens: bfloat16 [32768, 768], P(('dp', 'tensor'))
- grad_w_query: float32 [768, 768], P('dp', 'tensor')
- grad_w_key: float32 [768, 768], P('dp', 'tensor')
- grad_w_value: float32 [768, 768], P('dp', 'tensor')
- grad_w_out: float32 [768, 768], P('tensor', 'dp')
- grad_w_up: float32 [768, 3072], P('dp', 'tensor')
- grad_w_down: float32 [3072, 768], P('tensor', 'dp')
- grad_b_query: float32 [12, 64], P('tensor', 'dp')
- grad_b_value: float32 [12, 64], P('tensor', 'dp')
- grad_b_up: float32 [24, 128], P('tensor', 'dp')
- grad_b_out: float32 [768], P(('dp', 'tensor'))
- grad_b_down: float32 [768], P(('dp', 'tensor'))
- grad_gain_one: float32 [768], P(('dp', 'tensor'))
- grad_shift_one: float32 [768], P(('dp', 'tensor'))
- grad_gain_two: float32 [768], P(('dp', 'tensor'))
- grad_shift_two: float32 [768], P(('dp', 'tensor'))
The draws below stay inside these ranges and needn't reach their ends.
Inputs may be any that keep to these rules, and one draw needn't show every extreme that they name: `doc_lengths`: each row holds the 16 document lengths of one sequence in order and sums to 1024.
All inputs are finite; a program needn't handle non-finite values.
Results may differ from the reference program's by a relative error of at most 0.02.
Values may be sent and summed in bfloat16 or wider, within the bound.
No kernel may reach another device: no remote copies, remote signals or barrier semaphores. Data moves between devices by JAX's collectives and lax.ppermute only.
A program may use at most 192 MiB of HBM per device.

```python
import math
import jax
import jax.numpy as jnp
import numpy as np
from jax import lax

D = 768
HEADS = 12
HD = 64
FF = 3072
LEN = 1024
DOCS = 16
SEQS = 4
NSEQ = 32
TOKENS = 32768


def steps_of(rng, shape, cuts, low, top_value):
    def one(position, blocks):
        draws = jax.random.uniform(jax.random.fold_in(jax.random.fold_in(rng, 6), position), (blocks,), jnp.float32, low / len(cuts), top_value / len(cuts))
        return jnp.repeat(jnp.exp(draws), shape[position] // blocks).reshape((-1,) + (1,) * (len(shape) - position - 1))

    gain = one(*cuts[0])
    for cut in cuts[1:]:
        gain = gain * one(*cut)
    return gain


def length_profile(number_of, total, most, skew):
    weights = [(1 << 20) // math.isqrt(grade ** skew) + 1 for grade in range(2, number_of + 1)]
    spare, given = total - most - (number_of - 1), [1] * (number_of - 1)
    while spare > 0:
        candidates = [i for i in range(number_of - 1) if given[i] < most]
        mass, remaining = sum([weights[i] for i in candidates]), spare
        for i in candidates:
            more = min(most - given[i], max(1, remaining * weights[i] // mass), spare)
            given[i] = given[i] + more
            spare = spare - more
    return np.array([most] + given)


def uneven(key, number_of, total, limit, skew):
    if number_of == 2:
        one = jax.random.randint(key, (), max(1, total - limit), min(limit, total - 1) + 1)
        return jnp.stack([one, total - one])
    tallies = jnp.asarray(length_profile(number_of, total, limit, skew), jnp.int32)
    couples = (number_of - 1) // 2
    donor, taker = tallies[1:1 + 2 * couples:2], tallies[2:2 + 2 * couples:2]
    slack = jnp.minimum(donor - 1, limit - taker)
    moved = jax.random.randint(jax.random.fold_in(key, 1), (couples,), 0, 1 << 20) % (slack + 1)
    tallies = tallies.at[1:1 + 2 * couples:2].set(donor - moved).at[2:2 + 2 * couples:2].set(taker + moved)
    return tallies[jax.random.permutation(jax.random.fold_in(key, 2), number_of)]


def noise(rng, dims, width, limit, shards=(), kind=jnp.bfloat16):
    entries = jax.random.normal(rng, dims, jnp.float32) * width
    if len(shards) > 0:
        entries = steps_of(rng, dims, shards, -0.22, 0.18) * entries
    return jnp.clip(entries, min=-limit, max=limit).astype(kind)


def setup_inputs(seed: int = 0) -> dict:
    splits = jax.random.split(jax.random.key(seed), 19)
    tokens = noise(splits[0], (TOKENS, D), 1.0, 6.0, ((0, 32),))
    doc_lengths = jax.vmap(lambda own: uneven(own, DOCS, LEN, LEN // 2, 2))(jax.random.split(splits[1], NSEQ)).reshape((NSEQ, DOCS)).astype(jnp.int32)
    w_query = noise(splits[2], (D, D), D ** -0.5, 0.21875, ((0, 8), (1, 4)))
    w_key = noise(splits[3], (D, D), D ** -0.5, 0.21875, ((0, 8), (1, 4)))
    w_value = noise(splits[4], (D, D), D ** -0.5, 0.21875, ((0, 8), (1, 4)))
    w_out = noise(splits[5], (D, D), (D // 32) ** -0.5, 1.25, ((0, 4), (1, 8)))
    w_up = noise(splits[6], (D, FF), D ** -0.5, 0.21875, ((0, 8), (1, 4)))
    w_down = noise(splits[7], (FF, D), FF ** -0.5, 0.109375, ((0, 4), (1, 8)))
    b_query = noise(splits[8], (HEADS, HD), 0.5, 3.0, ((0, 4), (1, 8)))
    b_value = noise(splits[9], (HEADS, HD), 0.5, 3.0, ((0, 4), (1, 8)))
    b_up = noise(splits[10], (FF // 128, 128), 0.5, 3.0, ((0, 4), (1, 8)))
    b_out = noise(splits[11], (D,), 0.5, 3.0, ((0, 32),), jnp.float32)
    b_down = noise(splits[12], (D,), 0.5, 3.0, ((0, 32),), jnp.float32)
    gain_one = jnp.clip(1.0 + 0.18 * jax.random.normal(splits[13], (D,), jnp.float32), 0.1, 1.9)
    shift_one = noise(splits[14], (D,), 0.5, 3.0, ((0, 32),), jnp.float32)
    gain_two = jnp.clip(1.0 + 0.18 * jax.random.normal(splits[15], (D,), jnp.float32), 0.1, 1.9)
    shift_two = noise(splits[16], (D,), 0.5, 3.0, ((0, 32),), jnp.float32)
    cotangent = noise(splits[17], (TOKENS, D), 1.0, 6.0, ((0, 32),))
    return {"tokens": tokens, "doc_lengths": doc_lengths, "w_query": w_query, "w_key": w_key, "w_value": w_value, "w_out": w_out, "w_up": w_up, "w_down": w_down, "b_query": b_query, "b_value": b_value, "b_up": b_up, "b_out": b_out, "b_down": b_down, "gain_one": gain_one, "shift_one": shift_one, "gain_two": gain_two, "shift_two": shift_two, "cotangent": cotangent}


epsilon = 1e-06
root_half = 0.7071067811865476
masked_value = -1e+30
highest = lax.Precision.HIGHEST

@jax.custom_vjp
def low(v):
    return lax.optimization_barrier(v.astype(jnp.bfloat16)).astype(jnp.float32)

@jax.custom_vjp
def low_back(v):
    return v

def low_keep(v):
    return (low(v), None)

def low_pass(kept, grad):
    return (grad,)

def back_keep(v):
    return (v, None)

def back_low(kept, grad):
    return (low(grad),)
low.defvjp(low_keep, low_pass)
low_back.defvjp(back_keep, back_low)

def layer_norm(values, norm_gain, norm_shift):
    average = lax.optimization_barrier(jnp.mean(values, axis=-1, keepdims=True))
    centred = values - average
    variance = lax.optimization_barrier(jnp.mean(centred * centred, axis=-1, keepdims=True))
    return centred * lax.rsqrt(variance + epsilon) * norm_gain + norm_shift

def gelu_exact(values):
    return values * (0.5 * (1.0 + lax.erf(values * root_half)))

def segment_ids(doc_lengths):
    bounds = jnp.cumsum(doc_lengths, axis=-1)
    places = jnp.arange(LEN, dtype=jnp.int32)
    return lax.optimization_barrier(jnp.sum((bounds[:, None, :] <= places[None, :, None]).astype(jnp.int32), axis=-1))

def attend_group(inputs):
    queries, keys_all, values_all, segments = inputs
    scale = queries.shape[-1] ** (-0.5)
    scores = jnp.einsum('sqhd,skhd->shqk', queries, keys_all, precision=highest) * scale
    allowed = segments[:, None, :, None] == segments[:, None, None, :]
    scores = low_back(jnp.where(allowed, scores, masked_value))
    row_top = lax.optimization_barrier(jnp.max(scores, axis=-1, keepdims=True))
    weights = jnp.exp(scores - row_top)
    probability = weights / lax.optimization_barrier(jnp.sum(weights, axis=-1, keepdims=True))
    mixture = jnp.einsum('shqk,skhd->sqhd', low(probability), values_all, precision=highest)
    return low_back(low(mixture))

def forward(tokens, w_query, w_key, w_value, w_out, w_up, w_down, b_query, b_value, b_up, b_out, b_down, gain_one, shift_one, gain_two, shift_two, segments):
    tokens_low = low(tokens)
    queries = low_back(low(jnp.dot(tokens_low, w_query, precision=highest) + b_query.reshape(-1)))
    keys_all = low_back(low(jnp.dot(tokens_low, w_key, precision=highest)))
    values_all = low_back(low(jnp.dot(tokens_low, w_value, precision=highest) + b_value.reshape(-1)))
    grouped = (NSEQ // SEQS, SEQS, LEN, HEADS, HD)
    mixture = lax.map(jax.checkpoint(attend_group), (queries.reshape(grouped), keys_all.reshape(grouped), values_all.reshape(grouped), segments.reshape(NSEQ // SEQS, SEQS, LEN)))
    mixture = mixture.reshape(TOKENS, D)
    branch_one = low_back(jnp.dot(mixture, w_out, precision=highest))
    first = layer_norm(branch_one + b_out + tokens, gain_one, shift_one)
    up_pre = low_back(jnp.dot(low(first), w_up, precision=highest) + b_up.reshape(-1))
    activated = low(gelu_exact(up_pre))
    branch_two = low_back(jnp.dot(activated, w_down, precision=highest))
    return layer_norm(branch_two + b_down + first, gain_two, shift_two)

def reference(tokens, doc_lengths, w_query, w_key, w_value, w_out, w_up, w_down, b_query, b_value, b_up, b_out, b_down, gain_one, shift_one, gain_two, shift_two, cotangent):
    segments = segment_ids(doc_lengths)
    float_args = tuple((item.astype(jnp.float32) for item in (tokens, w_query, w_key, w_value, w_out, w_up, w_down, b_query, b_value, b_up, b_out, b_down, gain_one, shift_one, gain_two, shift_two)))

    def wrapped(*parameters):
        return forward(*parameters, segments)
    result, pullback = jax.vjp(wrapped, *float_args)
    gradients = pullback(cotangent.astype(jnp.float32))
    return (result.astype(jnp.bfloat16), gradients[0].astype(jnp.bfloat16), gradients[1], gradients[2], gradients[3], gradients[4], gradients[5], gradients[6], gradients[7], gradients[8], gradients[9], gradients[10], gradients[11], gradients[12], gradients[13], gradients[14], gradients[15])
```

```python
import functools

import jax
import jax.numpy as jnp
from jax import lax
from jax.experimental import pallas as pl
from jax.experimental.pallas import tpu as pltpu
from jax.sharding import PartitionSpec as P

HD = 64
BLOCK = 256
EXTRA = 16

epsilon = 1e-06
root_half = 0.7071067811865476
inv_root_tau = 0.3989422804014327
masked_value = -1e30
bf16 = jnp.bfloat16
f32 = jnp.float32


def contract(a, b, dims, out=f32):
    return lax.dot_general(a, b, (dims, ((), ())), preferred_element_type=f32).astype(out)


def ring_order(size):
    return list(range(0, size, 2)) + list(range(size - 1, 0, -2)) if size > 1 else [0]


class Links:
    def __init__(self, dp, tensor):
        self.dp, self.tensor = dp, tensor
        order = ring_order(dp)
        self.order = jnp.array(order, jnp.int32)
        place = [0] * dp
        for position, member in enumerate(order):
            place[member] = position
        self.forward = [(order[i], order[(i + 1) % dp]) for i in range(dp)]
        self.backward = [(b, a) for a, b in self.forward]
        self.me = lax.axis_index("dp")
        self.position = jnp.array(place, jnp.int32)[self.me]
        self.ahead = dp // 2
        self.behind = dp - 1 - self.ahead

    def member(self, offset):
        return self.order[(self.position + offset + self.dp) % self.dp]

    def swap_tensor(self, value, mask):
        return lax.ppermute(value, "tensor", [(i, i ^ mask) for i in range(self.tensor)])

    def gather_ring(self, value):
        rows = value.shape[-2]
        full = jnp.zeros(value.shape[:-2] + (rows * self.dp, value.shape[-1]), value.dtype)

        def put(full, piece, offset):
            start = self.member(offset) * rows
            return lax.dynamic_update_slice_in_dim(full, piece, start, axis=full.ndim - 2)

        full = put(full, value, 0)
        up, down = value, value
        for step in range(1, self.ahead + 1):
            up = lax.ppermute(up, "dp", self.forward)
            full = put(full, up, -step)
            if step <= self.behind:
                down = lax.ppermute(down, "dp", self.backward)
                full = put(full, down, step)
        return full

    def scatter_ring(self, full):
        rows = full.shape[-2] // self.dp

        def part(offset):
            start = self.member(offset) * rows
            return lax.dynamic_slice_in_dim(full, start, rows, axis=full.ndim - 2).astype(f32)

        up = part(self.ahead).astype(bf16)
        down = part(-self.behind).astype(bf16)
        total = part(0)
        for step in range(1, self.ahead + 1):
            up = lax.ppermute(up, "dp", self.forward)
            left = self.ahead - step
            if left:
                up = (up.astype(f32) + part(left)).astype(bf16)
            else:
                total = total + up.astype(f32)
            if step <= self.behind:
                down = lax.ppermute(down, "dp", self.backward)
                left = self.behind - step
                if left:
                    down = (down.astype(f32) + part(-left)).astype(bf16)
                else:
                    total = total + down.astype(f32)
        return total

    def gather_wide(self, value):
        own = self.gather_ring(value)
        across = self.swap_tensor(own, 2)
        return (own, self.swap_tensor(own, 1), across, self.swap_tensor(across, 1))

    def gather_early(self, value):
        pair = jnp.stack([value, self.swap_tensor(value, 2)])
        pair = self.gather_ring(pair)
        other = self.swap_tensor(pair, 1)
        return (pair[0], other[0], pair[1], other[1])

    def pair_sum(self, pieces):
        one = self.swap_tensor(pieces[1].astype(bf16), 1)
        three = self.swap_tensor(pieces[3].astype(bf16), 1)
        return (pieces[0].astype(f32) + one.astype(f32), pieces[2].astype(f32) + three.astype(f32))

    def scatter_early(self, pieces):
        own, across = self.pair_sum(pieces)
        across = self.swap_tensor(across.astype(bf16), 2)
        return self.scatter_ring(own + across.astype(f32))

    def scatter_late(self, pieces):
        own, across = self.pair_sum(pieces)
        pair = self.scatter_ring(jnp.stack([own, across]).astype(bf16))
        return pair[0] + self.swap_tensor(pair[1].astype(bf16), 2).astype(f32)

    def relative(self, value):
        mine = lax.axis_index("tensor")
        low = (mine & 1) == 1
        high = (mine & 2) == 2
        value = jnp.where(low, value[:, [1, 0, 3, 2]], value)
        return jnp.where(high, value[:, [2, 3, 0, 1]], value)

    def gather_small(self, value):
        full = value[None]
        bit = 1
        while bit < self.dp:
            other = lax.ppermute(full, "dp", [(i, i ^ bit) for i in range(self.dp)])
            upper = (self.me & bit) != 0
            full = jnp.where(
                upper, jnp.concatenate([other, full]), jnp.concatenate([full, other])
            )
            bit *= 2
        across = self.swap_tensor(full, 2)
        one = self.swap_tensor(full, 1)
        three = self.swap_tensor(across, 1)
        return jnp.stack([full, one, across, three], axis=1)

    def scatter_small(self, value):
        one = self.swap_tensor(value[:, 1], 1)
        three = self.swap_tensor(value[:, 3], 1)
        own, across = value[:, 0] + one, value[:, 2] + three
        full = own + self.swap_tensor(across, 2)
        bit = self.dp // 2
        while bit:
            upper = (self.me & bit) != 0
            low, high = full[:bit], full[bit:]
            kept = jnp.where(upper, high, low)
            sent = jnp.where(upper, low, high)
            full = kept + lax.ppermute(sent, "dp", [(i, i ^ bit) for i in range(self.dp)])
            bit //= 2
        return full[0]


def attend_kernel(first_ref, last_ref, qkv_ref, seg_row_ref, seg_col_ref, out_ref, log_ref, keys, values):
    length = qkv_ref.shape[1]
    heads = qkv_ref.shape[0] // (3 * HD)
    width = heads * HD
    tail = jnp.where(lax.broadcasted_iota(jnp.int32, (EXTRA, length), 0) == 0, 1.0, 0.0).astype(bf16)
    for head in range(heads):
        rows = slice(width + head * HD, width + (head + 1) * HD)
        keys[head] = qkv_ref[rows, :].astype(f32).T.astype(bf16)
        values[head, 0:HD, :] = qkv_ref[2 * width + head * HD : 2 * width + (head + 1) * HD, :]
        values[head, HD : HD + EXTRA, :] = tail

    def one_block(block, _):
        start = pl.multiple_of(block * BLOCK, BLOCK)
        seg_query = seg_row_ref[:, pl.ds(start, BLOCK)]
        queries = [
            qkv_ref[head * HD : (head + 1) * HD, pl.ds(start, BLOCK)] * 0.125 for head in range(heads)
        ]

        def one_key(key, carry):
            offset = pl.multiple_of(key * BLOCK, BLOCK)
            allowed = seg_col_ref[pl.ds(offset, BLOCK), :] == seg_query
            result = []
            for head in range(heads):
                top, total = carry[head]
                scores = contract(keys[head, pl.ds(offset, BLOCK), :], queries[head], ((1,), (0,)))
                scores = jnp.where(allowed, scores, masked_value)
                now = jnp.maximum(top, jnp.max(scores, axis=0, keepdims=True))
                weights = jnp.exp(scores - now).astype(bf16)
                total = total * jnp.exp(top - now) + contract(
                    values[head, :, pl.ds(offset, BLOCK)], weights, ((1,), (0,))
                )
                result.append((now, total))
            return tuple(result)

        start_value = tuple(
            (
                jnp.full((1, BLOCK), masked_value, f32),
                jnp.zeros((HD + EXTRA, BLOCK), f32),
            )
            for _ in range(heads)
        )
        done = lax.fori_loop(first_ref[block], last_ref[block] + 1, one_key, start_value)
        for head in range(heads):
            top, total = done[head]
            mass = total[HD : HD + 1, :]
            out_ref[head * HD : (head + 1) * HD, pl.ds(start, BLOCK)] = (total[:HD] / mass).astype(bf16)
            log_ref[head : head + 1, pl.ds(start, BLOCK)] = top + jnp.log(mass)
        return 0

    lax.fori_loop(0, length // BLOCK, one_block, 0)


def attend(qkv, seg_row, seg_col, first, last):
    width, length = qkv.shape
    heads = width // (3 * HD)
    full = lambda *shape: pl.BlockSpec(shape, lambda i, *_: (0,) * len(shape))
    return pl.pallas_call(
        attend_kernel,
        out_shape=(
            jax.ShapeDtypeStruct((heads * HD, length), bf16),
            jax.ShapeDtypeStruct((8, length), f32),
        ),
        grid_spec=pltpu.PrefetchScalarGridSpec(
            num_scalar_prefetch=2,
            grid=(1,),
            in_specs=[full(width, length), full(1, length), full(length, 1)],
            out_specs=(full(heads * HD, length), full(8, length)),
            scratch_shapes=[
                pltpu.VMEM((heads, length, HD), bf16),
                pltpu.VMEM((heads, HD + EXTRA, length), bf16),
            ],
        ),
        cost_estimate=pl.CostEstimate(
            flops=4 * heads * length * length * HD,
            bytes_accessed=4 * width * length,
            transcendentals=heads * length * length,
        ),
        name="attend",
    )(first, last, qkv, seg_row, seg_col)


def attend_back_kernel(
    first_ref, last_ref, qkv_ref, out_ref, log_ref, grad_ref, seg_row_ref, seg_col_ref, result_ref, keys, values, delta, grad_query
):
    length = qkv_ref.shape[1]
    heads = qkv_ref.shape[0] // (3 * HD)
    width = heads * HD
    for head in range(heads):
        own = slice(head * HD, (head + 1) * HD)
        keys[head] = qkv_ref[width + head * HD : width + (head + 1) * HD, :].astype(f32).T.astype(bf16)
        values[head] = qkv_ref[2 * width + head * HD : 2 * width + (head + 1) * HD, :].astype(f32).T.astype(bf16)
        delta[head : head + 1, :] = jnp.sum(
            out_ref[own, :].astype(f32) * grad_ref[own, :].astype(f32), axis=0, keepdims=True
        )
    grad_query[...] = jnp.zeros_like(grad_query)

    def one_key(block, _):
        offset = pl.multiple_of(block * BLOCK, BLOCK)
        seg_key = seg_col_ref[pl.ds(offset, BLOCK), :]

        def one_query(query, carry):
            start = pl.multiple_of(query * BLOCK, BLOCK)
            lanes = pl.ds(start, BLOCK)
            allowed = seg_key == seg_row_ref[:, lanes]
            result = []
            for head in range(heads):
                grad_key, grad_value = carry[head]
                own = slice(head * HD, (head + 1) * HD)
                queries = qkv_ref[own, lanes] * 0.125
                grads = grad_ref[own, lanes]
                scores = contract(keys[head, pl.ds(offset, BLOCK), :], queries, ((1,), (0,)))
                scores = jnp.where(allowed, scores, masked_value)
                weights = jnp.exp(scores - log_ref[head : head + 1, lanes])
                grad_prob = contract(values[head, pl.ds(offset, BLOCK), :], grads, ((1,), (0,)))
                grad_scores = (weights * (grad_prob - delta[head : head + 1, lanes])).astype(bf16)
                grad_value = grad_value + contract(grads, weights.astype(bf16), ((1,), (1,)))
                grad_key = grad_key + contract(queries, grad_scores, ((1,), (1,)))
                key_cols = qkv_ref[width + head * HD : width + (head + 1) * HD, pl.ds(offset, BLOCK)]
                grad_query[own, lanes] += contract(key_cols, grad_scores, ((1,), (0,)))
                result.append((grad_key, grad_value))
            return tuple(result)

        zero = jnp.zeros((HD, BLOCK), f32)
        done = lax.fori_loop(
            first_ref[block], last_ref[block] + 1, one_query, tuple((zero, zero) for _ in range(heads))
        )
        for head in range(heads):
            grad_key, grad_value = done[head]
            rows = width + head * HD
            result_ref[rows : rows + HD, pl.ds(offset, BLOCK)] = grad_key.astype(bf16)
            result_ref[width + rows : width + rows + HD, pl.ds(offset, BLOCK)] = grad_value.astype(bf16)
        return 0

    lax.fori_loop(0, length // BLOCK, one_key, 0)
    result_ref[0:width, :] = (grad_query[...] * 0.125).astype(bf16)


def attend_back(qkv, out, logs, grad, seg_row, seg_col, first, last):
    width, length = qkv.shape
    heads = width // (3 * HD)
    full = lambda *shape: pl.BlockSpec(shape, lambda i, *_: (0,) * len(shape))
    return pl.pallas_call(
        attend_back_kernel,
        out_shape=jax.ShapeDtypeStruct((width, length), bf16),
        grid_spec=pltpu.PrefetchScalarGridSpec(
            num_scalar_prefetch=2,
            grid=(1,),
            in_specs=[
                full(width, length),
                full(heads * HD, length),
                full(8, length),
                full(heads * HD, length),
                full(1, length),
                full(length, 1),
            ],
            out_specs=full(width, length),
            scratch_shapes=[
                pltpu.VMEM((heads, length, HD), bf16),
                pltpu.VMEM((heads, length, HD), bf16),
                pltpu.VMEM((8, length), f32),
                pltpu.VMEM((heads * HD, length), f32),
            ],
        ),
        cost_estimate=pl.CostEstimate(
            flops=10 * heads * length * length * HD,
            bytes_accessed=6 * width * length,
            transcendentals=heads * length * length,
        ),
        name="attend_back",
    )(first, last, qkv, out, logs, grad, seg_row, seg_col)


def normalize(values, norm_gain, norm_shift):
    average = jnp.mean(values, axis=-1, keepdims=True)
    centred = values - average
    variance = jnp.mean(centred * centred, axis=-1, keepdims=True)
    inv_scale = lax.rsqrt(variance + epsilon)
    unit_rows = centred * inv_scale
    return (unit_rows * norm_gain + norm_shift, unit_rows, inv_scale)


def normalize_back(grad_out, unit_rows, inv_scale, norm_gain):
    grad_unit = grad_out * norm_gain
    middle = grad_unit - jnp.mean(grad_unit, axis=-1, keepdims=True)
    middle = middle - unit_rows * jnp.mean(grad_unit * unit_rows, axis=-1, keepdims=True)
    return inv_scale * middle


def gelu_parts(up_pre):
    normal_cdf = 0.5 * (1.0 + lax.erf(up_pre * root_half))
    return (
        up_pre * normal_cdf,
        normal_cdf + up_pre * inv_root_tau * jnp.exp(-0.5 * up_pre * up_pre),
    )


def per_device(
    tokens,
    doc_lengths,
    w_query,
    w_key,
    w_value,
    w_out,
    w_up,
    w_down,
    b_query,
    b_value,
    b_up,
    b_out,
    b_down,
    gain_one,
    shift_one,
    gain_two,
    shift_two,
    cotangent,
):
    dp, tensor = lax.axis_size("dp"), lax.axis_size("tensor")
    length, model = tokens.shape
    group = w_query.shape[1]
    hidden = w_up.shape[1]
    links = Links(dp, tensor)
    sequence = lax.axis_index("tensor")

    lengths = lax.dynamic_slice_in_dim(doc_lengths, sequence, 1, axis=0)[0]
    bounds = jnp.cumsum(lengths)
    places = jnp.arange(length, dtype=jnp.int32)
    segment = jnp.sum((bounds[None, :] <= places[:, None]).astype(jnp.int32), axis=-1)
    seg_row, seg_col = segment[None, :], segment[:, None]
    blocks = segment.reshape(-1, BLOCK)
    low, high = blocks[:, 0], blocks[:, -1]
    meets = (low[:, None] <= high[None, :]) & (low[None, :] <= high[:, None])
    count = low.shape[0]
    index = jnp.arange(count, dtype=jnp.int32)
    first = jnp.min(jnp.where(meets, index[None, :], count), axis=1)
    last = jnp.max(jnp.where(meets, index[None, :], -1), axis=1)

    vectors = (b_out, b_down, gain_one, shift_one, gain_two, shift_two)
    share = b_out.shape[0]
    small = jnp.concatenate(
        list(vectors) + [v.astype(f32).reshape(-1) for v in (b_query, b_value, b_up)]
    )
    used = small.shape[0]
    small = jnp.pad(small, (0, -used % 128))
    small = links.gather_small(small)
    flat = links.relative(small)[:, :, : 6 * share].reshape(dp * tensor, 6, share)
    flat = flat.transpose(1, 0, 2).reshape(6, model)
    bias_out, bias_down, norm_gain_one, norm_shift_one, norm_gain_two, norm_shift_two = flat
    heads = b_query.shape[0]
    taken = 6 * share

    def columns(rows, per):
        nonlocal taken
        part = small[:, :, taken : taken + rows * per].reshape(dp, tensor, rows, per)
        taken += rows * per
        return part.transpose(1, 2, 0, 3).reshape(tensor, -1)

    bias_query = columns(heads, b_query.shape[1])
    bias_value = columns(heads, b_value.shape[1])
    bias_up = columns(b_up.shape[0], b_up.shape[1])

    attn_w = links.gather_early(jnp.concatenate([w_query, w_key, w_value, w_out.T], axis=1))
    up_w = links.gather_wide(w_up)
    down_w = links.gather_early(w_down.T)

    qkv, mixture, logs = [], [], []
    for j in range(tensor):
        bias = jnp.concatenate([bias_query[j], jnp.zeros((group,), f32), bias_value[j]])
        made = contract(attn_w[j][:, : 3 * group], tokens, ((0,), (1,))) + bias[:, None]
        qkv.append(made.astype(bf16))
        mixed, log = attend(qkv[j], seg_row, seg_col, first, last)
        mixture.append(mixed)
        logs.append(log)
    attn = bias_out + tokens.astype(f32)
    for j in range(tensor):
        attn = attn + contract(mixture[j], attn_w[j][:, 3 * group :], ((0,), (1,)))
    first_out, unit_one, scale_one = normalize(attn, norm_gain_one, norm_shift_one)
    first_low = first_out.astype(bf16)
    activated, slopes = [], []
    for j in range(tensor):
        up_pre = contract(first_low, up_w[j], ((1,), (0,))) + bias_up[j]
        act, slope = gelu_parts(up_pre)
        activated.append(act.astype(bf16))
        slopes.append(slope.astype(bf16))
    residual = bias_down + first_out
    for j in range(tensor):
        residual = residual + contract(activated[j], down_w[j], ((1,), (1,)))
    result, unit_two, scale_two = normalize(residual, norm_gain_two, norm_shift_two)
    grad_out = cotangent.astype(f32)
    grad_two = normalize_back(grad_out, unit_two, scale_two, norm_gain_two)
    grad_gain_two = jnp.sum(grad_out * unit_two, axis=0)
    grad_shift_two = jnp.sum(grad_out, axis=0)
    grad_bias_down = jnp.sum(grad_two, axis=0)
    grad_two_low = grad_two.astype(bf16)
    grad_down = [contract(grad_two_low, activated[j], ((0,), (0,)), bf16) for j in range(tensor)]
    grad_down = links.scatter_late(grad_down)
    grad_up, grad_w_up, grad_bias_up = [], [], []
    grad_first = grad_two
    for j in range(tensor):
        made = contract(grad_two_low, down_w[j], ((1,), (0,))) * slopes[j].astype(f32)
        grad_up.append(made.astype(bf16))
        grad_bias_up.append(jnp.sum(grad_up[j].astype(f32), axis=0))
        grad_w_up.append(contract(first_low, grad_up[j], ((0,), (0,)), bf16))
        grad_first = grad_first + contract(grad_up[j], up_w[j], ((1,), (1,)))
    grad_w_up = links.scatter_early(grad_w_up)
    grad_one = normalize_back(grad_first, unit_one, scale_one, norm_gain_one)
    grad_gain_one = jnp.sum(grad_first * unit_one, axis=0)
    grad_shift_one = jnp.sum(grad_first, axis=0)
    grad_bias_out = jnp.sum(grad_one, axis=0)
    grad_one_low = grad_one.astype(bf16)
    grad_attn, grad_bias_query, grad_bias_value = [], [], []
    grad_input = grad_one
    for j in range(tensor):
        grad_mix = contract(attn_w[j][:, 3 * group :], grad_one_low, ((0,), (1,)), bf16)
        grad_qkv = attend_back(qkv[j], mixture[j], logs[j], grad_mix, seg_row, seg_col, first, last)
        sums = jnp.sum(grad_qkv.astype(f32), axis=1)
        grad_bias_query.append(sums[:group])
        grad_bias_value.append(sums[2 * group :])
        grad_attn.append(
            jnp.concatenate(
                [
                    contract(tokens, grad_qkv, ((0,), (1,)), bf16),
                    contract(grad_one_low, mixture[j], ((0,), (1,)), bf16),
                ],
                axis=1,
            )
        )
        grad_input = grad_input + contract(grad_qkv, attn_w[j][:, : 3 * group], ((0,), (1,)))
    grad_attn = links.scatter_late(grad_attn)

    sums = jnp.stack(
        [grad_bias_out, grad_bias_down, grad_gain_one, grad_shift_one, grad_gain_two, grad_shift_two]
    )
    sums = sums.reshape(6, dp, tensor, share).transpose(1, 2, 0, 3).reshape(dp, tensor, 6 * share)
    sums = links.relative(sums)

    def spread(pieces, rows, per):
        stacked = jnp.stack(pieces).reshape(tensor, rows, dp, per)
        return stacked.transpose(2, 0, 1, 3).reshape(dp, tensor, rows * per)

    shapes = [b_query.shape, b_value.shape, b_up.shape]
    sums = jnp.concatenate(
        [sums]
        + [
            spread(pieces, *shape)
            for pieces, shape in zip((grad_bias_query, grad_bias_value, grad_bias_up), shapes)
        ],
        axis=2,
    )
    sums = jnp.pad(sums, ((0, 0), (0, 0), (0, -used % 128)))
    sums = links.scatter_small(sums)
    vector_sums = [sums[i * share : (i + 1) * share] for i in range(6)]
    at = 6 * share
    tables = []
    for rows, per in shapes:
        tables.append(sums[at : at + rows * per].reshape(rows, per))
        at += rows * per
    return (
        result.astype(bf16),
        grad_input.astype(bf16),
        grad_attn[:, :group],
        grad_attn[:, group : 2 * group],
        grad_attn[:, 2 * group : 3 * group],
        grad_attn[:, 3 * group :].T,
        grad_w_up,
        grad_down.T,
        *tables,
        *vector_sums,
    )


def solution(mesh):
    both = P(("dp", "tensor"))
    rows = P(("dp", "tensor"), None)
    down = P("tensor", "dp")
    wide = P("dp", "tensor")
    weights = (wide, wide, wide, down, wide, down, down, down, down)
    return jax.shard_map(
        per_device,
        mesh=mesh,
        in_specs=(rows, P("dp", None)) + weights + (both,) * 6 + (rows,),
        out_specs=(rows, rows) + weights + (both,) * 6,
        check_vma=False,
    )
```

```python
import functools

import jax
import jax.numpy as jnp
from jax import lax
from jax.experimental import pallas as pl
from jax.experimental.pallas import tpu as pltpu
from jax.sharding import PartitionSpec as P

HD = 64
BLOCK = 256
EXTRA = 16
STEP = 128
SIDE = 8
TAIL = 16

epsilon = 1e-06
root_half = 0.7071067811865476
inv_root_tau = 0.3989422804014327
masked_value = -1e30
bf16 = jnp.bfloat16
f32 = jnp.float32


def contract(a, b, dims, out=f32):
    return lax.dot_general(a, b, (dims, ((), ())), preferred_element_type=f32).astype(out)


def ring_order(size):
    return list(range(0, size, 2)) + list(range(size - 1, 0, -2)) if size > 1 else [0]


class Links:
    def __init__(self, dp, tensor):
        self.dp, self.tensor = dp, tensor
        order = ring_order(dp)
        self.order = jnp.array(order, jnp.int32)
        place = [0] * dp
        for position, member in enumerate(order):
            place[member] = position
        self.forward = [(order[i], order[(i + 1) % dp]) for i in range(dp)]
        self.backward = [(b, a) for a, b in self.forward]
        self.me = lax.axis_index("dp")
        self.position = jnp.array(place, jnp.int32)[self.me]
        self.ahead = dp // 2
        self.behind = dp - 1 - self.ahead
        offsets = jnp.arange(-self.ahead, self.behind + 1, dtype=jnp.int32)
        self.members = self.order[(self.position + offsets + dp) % dp]

    def swap(self, value, mask):
        return lax.ppermute(value, "tensor", [(i, i ^ mask) for i in range(self.tensor)])


def tie(*holders):
    flat, tree = jax.tree.flatten([holder.live for holder in holders])
    flat = lax.optimization_barrier(tuple(flat))
    for holder, live in zip(holders, jax.tree.unflatten(tree, flat)):
        holder.live = live


class Box:
    def __init__(self, *live):
        self.live = list(live)


class GatherRing:
    def __init__(self, links, value):
        self.links = links
        self.live = [value, value]
        self.pieces = {0: value}
        self.count = 0

    def step(self):
        links = self.links
        self.count += 1
        up, down = self.live
        up = lax.ppermute(up, "dp", links.forward)
        self.pieces[-self.count] = up
        if self.count <= links.behind:
            down = lax.ppermute(down, "dp", links.backward)
            self.pieces[self.count] = down
        self.live = [up, down]

    def full(self, widths, rows):
        links = self.links
        pieces = [self.pieces[offset] for offset in range(-links.ahead, links.behind + 1)]
        return assemble(links.members, pieces, widths, rows)


class ScatterRing:
    def __init__(self, links, source):
        self.links = links
        self.source = source
        self.count = 0
        self.total = None
        self.live = ring_first(links, source)

    def step(self):
        links = self.links
        self.count += 1
        up, down = self.live
        up = lax.ppermute(up, "dp", links.forward)
        if self.count <= links.behind:
            down = lax.ppermute(down, "dp", links.backward)
        left_up, left_down = links.ahead - self.count, links.behind - self.count
        if left_up == 0:
            self.total = ring_last(links, self.source, up, down)
        elif left_down > 0:
            up, down = ring_add(links, self.source, (left_up, -left_down), (up, down))
        else:
            (up,) = ring_add(links, self.source, (left_up,), (up,))
        self.live = [up, down]


VMEM = pl.BlockSpec(memory_space=pltpu.VMEM)
SMEM = pl.BlockSpec(memory_space=pltpu.SMEM)


def ring_kernel(members_ref, *refs, count, dtype, fold):
    parts, arrived, outs = refs[:count], refs[count:-count], refs[-count:]
    if fold:
        total = parts[0][0].astype(f32)
        for one in arrived:
            total = total + one[...].astype(f32)
        outs[0][...] = total.astype(dtype)
    else:
        for index in range(count):
            made = parts[index][0]
            if arrived:
                made = (made.astype(f32) + arrived[index][...].astype(f32)).astype(dtype)
            outs[index][...] = made


def ring_call(links, source, offsets, arrived, dtype, fold=False):
    _, rows, columns = source.shape
    whole = pl.BlockSpec((rows, columns), lambda i, m: (0, 0))

    def part(offset):
        index = (offset + links.ahead) % links.dp
        return pl.BlockSpec((1, rows, columns), lambda i, m: (m[index], 0, 0))

    size = rows * columns
    return pl.pallas_call(
        functools.partial(ring_kernel, count=len(offsets), dtype=dtype, fold=fold),
        out_shape=[jax.ShapeDtypeStruct((rows, columns), dtype) for _ in offsets],
        grid_spec=pltpu.PrefetchScalarGridSpec(
            num_scalar_prefetch=1,
            grid=(1,),
            in_specs=[part(offset) for offset in offsets] + [whole] * len(arrived),
            out_specs=[whole] * len(offsets),
        ),
        compiler_params=pltpu.CompilerParams(vmem_limit_bytes=8 << 20),
        cost_estimate=pl.CostEstimate(
            flops=size * 2, bytes_accessed=6 * size * len(offsets), transcendentals=0
        ),
        name="ring_sum",
    )(links.members, *([source] * len(offsets)), *arrived)


def ring_first(links, source):
    return list(ring_call(links, source, (links.ahead, -links.behind), (), bf16))


def ring_add(links, source, offsets, arrived):
    return ring_call(links, source, offsets, arrived, bf16)


def ring_last(links, source, up, down):
    return ring_call(links, source, (0,), (up, down), f32, fold=True)[0]


def assemble_kernel(members_ref, *refs, count, widths, rows):
    pieces, outs, side_ref, sum_ref = refs[:count], refs[count:-2], refs[-2], refs[-1]
    total = None
    for index in range(count):
        start = pl.multiple_of(members_ref[index] * rows, rows)
        at = 0
        for out, width in zip(outs, widths):
            out[pl.ds(start, rows), :] = pieces[index][0:rows, at : at + width]
            at += width
        side = pieces[index][rows : rows + SIDE, :].astype(f32)
        side_ref[pl.ds(pl.multiple_of(members_ref[index] * SIDE, SIDE), SIDE), :] = side
        total = side if total is None else total + side
    sum_ref[...] = total


def assemble(members, pieces, widths, rows):
    count = len(pieces)
    wide = pieces[0].shape[1]
    if rows % 16:
        stacked = jnp.stack(pieces)
        back = jnp.zeros((count,), jnp.int32).at[members].set(jnp.arange(count, dtype=jnp.int32))
        stacked = jnp.take(stacked, back, axis=0)
        full = stacked[:, :rows].reshape(count * rows, -1)
        outs, at = [], 0
        for width in widths:
            outs.append(full[:, at : at + width])
            at += width
        side = stacked[:, rows:].astype(f32)
        return outs + [side.reshape(count * SIDE, wide), jnp.sum(side, axis=0)]
    total = count * pieces[0].size * 2
    return pl.pallas_call(
        functools.partial(assemble_kernel, count=count, widths=widths, rows=rows),
        out_shape=[jax.ShapeDtypeStruct((count * rows, width), bf16) for width in widths]
        + [jax.ShapeDtypeStruct((count * SIDE, wide), f32), jax.ShapeDtypeStruct((SIDE, wide), f32)],
        in_specs=[SMEM] + [VMEM] * count,
        out_specs=[VMEM] * (len(widths) + 2),
        compiler_params=pltpu.CompilerParams(vmem_limit_bytes=4 << 20),
        cost_estimate=pl.CostEstimate(flops=0, bytes_accessed=2 * total, transcendentals=0),
        name="assemble",
    )(members, *pieces)


def placed(table, me, dp):
    count, per = table.shape
    size = per * dp
    one_hot = lax.broadcasted_iota(jnp.int32, (per, size), 1) == (
        lax.broadcasted_iota(jnp.int32, (per, size), 0) + me * per
    )
    spread = contract(table, one_hot.astype(f32).astype(bf16), ((1,), (0,)), bf16)
    return [spread[row : row + 1] for row in range(count)]


def pack_kernel(me_ref, query_ref, key_ref, value_ref, b_query_ref, b_value_ref, out_ref, *, dp):
    rows, group = query_ref.shape
    out_ref[0:rows, 0:group] = query_ref[...]
    out_ref[0:rows, group : 2 * group] = key_ref[...]
    out_ref[0:rows, 2 * group :] = value_ref[...]
    me = me_ref[0]
    zero = jnp.zeros((1, group), bf16)
    row = jnp.concatenate(
        placed(b_query_ref[...], me, dp) + [zero] + placed(b_value_ref[...], me, dp), axis=1
    ).astype(f32)
    first = lax.broadcasted_iota(jnp.int32, (SIDE, 3 * group), 0) == 0
    out_ref[rows:, :] = jnp.where(first, row, 0.0).astype(bf16)


def pack(links, query, key, value, b_query, b_value):
    rows, group = query.shape
    if rows % 16:
        row = jnp.concatenate(
            placed(b_query, links.me, links.dp)
            + [jnp.zeros((1, group), bf16)]
            + placed(b_value, links.me, links.dp),
            axis=1,
        )
        side = jnp.pad(row, ((0, SIDE - 1), (0, 0)))
        return jnp.concatenate([jnp.concatenate([query, key, value], axis=1), side])
    return pl.pallas_call(
        functools.partial(pack_kernel, dp=links.dp),
        out_shape=jax.ShapeDtypeStruct((rows + SIDE, 3 * group), bf16),
        in_specs=[SMEM] + [VMEM] * 5,
        out_specs=VMEM,
        compiler_params=pltpu.CompilerParams(vmem_limit_bytes=2 << 20),
        name="pack",
    )(links.me.reshape(1), query, key, value, b_query, b_value)


def windows(low, high, block, length):
    begin = low.reshape(-1, block)[:, 0] // STEP * STEP
    end = high.reshape(-1, block)[:, -1]
    count = (end - begin + block - 1) // block
    return jnp.stack([jnp.minimum(begin, length - count * block), count])


def fill_bias(bias, begin, low, high, size):
    keys = lax.broadcasted_iota(jnp.int32, (size, low.shape[1]), 0) + begin
    bias[0:size, :] = jnp.where((keys >= low) & (keys < high), 0.0, masked_value)


def attend_kernel(
    window_ref, tokens_ref, weight_ref, bias_ref, span_ref, out_ref, log_ref, qkv_ref, keys, values, bias, hold, *, block
):
    length = qkv_ref.shape[1]
    heads = qkv_ref.shape[0] // (3 * HD)
    width = heads * HD
    made = contract(tokens_ref[...], weight_ref[...], ((1,), (0,))) + bias_ref[0:1, :]
    qkv_ref[...] = made.astype(bf16).T
    tail = jnp.where(lax.broadcasted_iota(jnp.int32, (EXTRA, length), 0) == 0, 1.0, 0.0).astype(bf16)
    for head in range(heads):
        keys[head] = qkv_ref[width + head * HD : width + (head + 1) * HD, :].T
        values[head, 0:HD, :] = qkv_ref[2 * width + head * HD : 2 * width + (head + 1) * HD, :]
        values[head, HD : HD + EXTRA, :] = tail

    def one_block(index, _):
        lanes = pl.ds(pl.multiple_of(index * block, block), block)
        begin = pl.multiple_of(window_ref[0, index], STEP)

        def with_count(count):
            fill_bias(bias, begin, span_ref[0:1, lanes], span_ref[1:2, lanes], count * block)
            tops = []
            for head in range(heads):
                queries = qkv_ref[head * HD : (head + 1) * HD, lanes] * 0.125
                top = None
                for piece in range(count):
                    rows = slice(piece * block, (piece + 1) * block)
                    own = pl.ds(begin + piece * block, block)
                    scores = contract(keys[head, own, :], queries, ((1,), (0,))) + bias[rows, :]
                    hold[head, rows, :] = scores
                    most = jnp.max(scores.reshape(block // 8, 8, block), axis=0)
                    top = most if top is None else jnp.maximum(top, most)
                tops.append(jnp.max(top, axis=0, keepdims=True))
            for head in range(heads):
                total = None
                for piece in range(count):
                    rows = slice(piece * block, (piece + 1) * block)
                    own = pl.ds(begin + piece * block, block)
                    weights = jnp.exp(hold[head, rows, :] - tops[head]).astype(bf16)
                    made = contract(values[head, :, own], weights, ((1,), (0,)))
                    total = made if total is None else total + made
                mass = total[HD : HD + 1, :]
                out_ref[head * HD : (head + 1) * HD, lanes] = (total[:HD] / mass).astype(bf16)
                log_ref[head : head + 1, lanes] = tops[head] + jnp.log(mass)

        for count in range(1, length // block + 1):
            pl.when(window_ref[1, index] == count)(functools.partial(with_count, count))
        return 0

    lax.fori_loop(0, length // block, one_block, 0)


def attend_back_kernel(
    window_ref, qkv_ref, span_ref, out_ref, log_ref, grad_ref, result_ref, keys, values, bias, grad_key, grad_value, *, block
):
    length = qkv_ref.shape[1]
    heads = qkv_ref.shape[0] // (3 * HD)
    width = heads * HD
    for head in range(heads):
        keys[head] = qkv_ref[width + head * HD : width + (head + 1) * HD, :].T
        values[head] = qkv_ref[2 * width + head * HD : 2 * width + (head + 1) * HD, :].T
    grad_key[...] = jnp.zeros_like(grad_key)
    grad_value[...] = jnp.zeros_like(grad_value)

    def one_block(index, _):
        lanes = pl.ds(pl.multiple_of(index * block, block), block)
        begin = pl.multiple_of(window_ref[0, index], STEP)

        def with_count(count):
            size = count * block
            window = pl.ds(begin, size)
            fill_bias(bias, begin, span_ref[0:1, lanes], span_ref[1:2, lanes], size)
            for head in range(heads):
                own = slice(head * HD, (head + 1) * HD)
                queries = qkv_ref[own, lanes] * 0.125
                grads = grad_ref[own, lanes]
                delta = jnp.sum(
                    out_ref[own, lanes].astype(f32) * grads.astype(f32), axis=0, keepdims=True
                )
                scores = contract(keys[head, window, :], queries, ((1,), (0,))) + bias[0:size, :]
                weights = jnp.exp(scores - log_ref[head : head + 1, lanes])
                grad_prob = contract(values[head, window, :], grads, ((1,), (0,)))
                grad_scores = (weights * (grad_prob - delta)).astype(bf16)
                grad_value[own, window] += contract(grads, weights.astype(bf16), ((1,), (1,)))
                grad_key[own, window] += contract(queries, grad_scores, ((1,), (1,)))
                key_cols = qkv_ref[width + head * HD : width + (head + 1) * HD, window]
                made = contract(key_cols, grad_scores, ((1,), (0,)))
                result_ref[own, lanes] = (made * 0.125).astype(bf16)

        for count in range(1, length // block + 1):
            pl.when(window_ref[1, index] == count)(functools.partial(with_count, count))
        return 0

    lax.fori_loop(0, length // block, one_block, 0)
    result_ref[width : 2 * width, :] = grad_key[...].astype(bf16)
    result_ref[2 * width :, :] = grad_value[...].astype(bf16)


def attend(tokens, weight, bias, window, span):
    length, model = tokens.shape
    width = weight.shape[1]
    heads = width // (3 * HD)
    return pl.pallas_call(
        functools.partial(attend_kernel, block=BLOCK),
        out_shape=(
            jax.ShapeDtypeStruct((heads * HD, length), bf16),
            jax.ShapeDtypeStruct((8, length), f32),
            jax.ShapeDtypeStruct((width, length), bf16),
        ),
        in_specs=[SMEM] + [VMEM] * 4,
        out_specs=(VMEM,) * 3,
        scratch_shapes=[
            pltpu.VMEM((heads, length, HD), bf16),
            pltpu.VMEM((heads, HD + EXTRA, length), bf16),
            pltpu.VMEM((length, BLOCK), f32),
            pltpu.VMEM((heads, length, BLOCK), f32),
        ],
        compiler_params=pltpu.CompilerParams(vmem_limit_bytes=24 << 20),
        cost_estimate=pl.CostEstimate(
            flops=4 * heads * length * length * HD + 2 * length * model * width,
            bytes_accessed=4 * width * length,
            transcendentals=heads * length * length,
        ),
        name="attend",
    )(window, tokens, weight, bias, span)


def attend_back(qkv, out, logs, grad, window, span):
    width, length = qkv.shape
    heads = width // (3 * HD)
    return pl.pallas_call(
        functools.partial(attend_back_kernel, block=BLOCK),
        out_shape=jax.ShapeDtypeStruct((width, length), bf16),
        in_specs=[SMEM] + [VMEM] * 5,
        out_specs=VMEM,
        scratch_shapes=[
            pltpu.VMEM((heads, length, HD), bf16),
            pltpu.VMEM((heads, length, HD), bf16),
            pltpu.VMEM((length, BLOCK), f32),
            pltpu.VMEM((heads * HD, length), f32),
            pltpu.VMEM((heads * HD, length), f32),
        ],
        compiler_params=pltpu.CompilerParams(vmem_limit_bytes=16 << 20),
        cost_estimate=pl.CostEstimate(
            flops=10 * heads * length * length * HD,
            bytes_accessed=6 * width * length,
            transcendentals=heads * length * length,
        ),
        name="attend_back",
    )(window, qkv, span, out, logs, grad)


def grad_weight_kernel(tokens_ref, grad_ref, one_ref, mixture_ref, *refs):
    more, out_ref = refs[:-1], refs[-1]
    up_ref, vectors_ref = more[0], more[1]
    dp, full, columns = out_ref.shape
    rows = full - TAIL
    wide = grad_ref.shape[0]
    group = wide // 3
    made = contract(tokens_ref[...], grad_ref[...], ((0,), (1,)))
    out_low = contract(one_ref[...], mixture_ref[...], ((0,), (1,)))
    ones = jnp.ones((TAIL, grad_ref.shape[1]), bf16)
    lane = contract(ones, grad_ref[...], ((1,), (1,)))
    line = lax.broadcasted_iota(jnp.int32, (TAIL, columns), 0)
    bias_row = jnp.concatenate([lane, jnp.zeros((TAIL, columns - wide), f32)], axis=1)
    side = jnp.where(line == 0, bias_row, 0.0) + jnp.where(line == 1, up_ref[0:1, :], 0.0)
    lower = jnp.concatenate([jnp.zeros((TAIL - 8, columns), f32), vectors_ref[...]], axis=0)
    side = side + lower
    for index in range(dp):
        own = slice(index * rows, (index + 1) * rows)
        left, right, low = made[own], out_low[own], side
        if len(more) > 2:
            left = left + more[2][index, 0:rows, 0:wide].astype(f32)
            right = right + more[2][index, 0:rows, wide:].astype(f32)
            low = low + more[2][index, rows:, :].astype(f32)
        out_ref[index, 0:rows, 0:wide] = left.astype(bf16)
        out_ref[index, 0:rows, wide:] = right.astype(bf16)
        out_ref[index, rows:, :] = low.astype(bf16)


def grad_weight(dp, tokens, grad, one, mixture, up_row, vectors, arrived=None):
    length, model = tokens.shape
    wide, group = grad.shape[0], mixture.shape[0]
    more = [] if arrived is None else [arrived]
    return pl.pallas_call(
        grad_weight_kernel,
        out_shape=jax.ShapeDtypeStruct((dp, model // dp + TAIL, wide + group), bf16),
        in_specs=[VMEM] * (6 + len(more)),
        out_specs=VMEM,
        compiler_params=pltpu.CompilerParams(vmem_limit_bytes=24 << 20),
        cost_estimate=pl.CostEstimate(
            flops=2 * length * model * (wide + group),
            bytes_accessed=2 * (length + model) * (wide + group + model),
            transcendentals=0,
        ),
        name="grad_weight",
    )(tokens, grad, one, mixture, up_row, vectors, *more)


def normalize(values, norm_gain, norm_shift):
    average = jnp.mean(values, axis=-1, keepdims=True)
    centred = values - average
    variance = jnp.mean(centred * centred, axis=-1, keepdims=True)
    inv_scale = lax.rsqrt(variance + epsilon)
    unit_rows = centred * inv_scale
    return (unit_rows * norm_gain + norm_shift, unit_rows, inv_scale)


def normalize_back(grad_out, unit_rows, inv_scale, norm_gain):
    grad_unit = grad_out * norm_gain
    middle = grad_unit - jnp.mean(grad_unit, axis=-1, keepdims=True)
    middle = middle - unit_rows * jnp.mean(grad_unit * unit_rows, axis=-1, keepdims=True)
    return inv_scale * middle


def gelu_parts(up_pre):
    normal_cdf = 0.5 * (1.0 + lax.erf(up_pre * root_half))
    return (
        up_pre * normal_cdf,
        normal_cdf + up_pre * inv_root_tau * jnp.exp(-0.5 * up_pre * up_pre),
    )


def per_device(
    tokens,
    doc_lengths,
    w_query,
    w_key,
    w_value,
    w_out,
    w_up,
    w_down,
    b_query,
    b_value,
    b_up,
    b_out,
    b_down,
    gain_one,
    shift_one,
    gain_two,
    shift_two,
    cotangent,
):
    dp, tensor = lax.axis_size("dp"), lax.axis_size("tensor")
    length, model = tokens.shape
    rows = model // dp
    group = w_query.shape[1]
    links = Links(dp, tensor)
    swap = links.swap

    share = b_out.shape[0]
    me = links.me
    vectors = jnp.stack([b_out, b_down, gain_one, shift_one, gain_two, shift_two])
    parts = []
    for _ in range(3):
        part = lax.reduce_precision(vectors, 8, 7)
        parts.append(part.astype(bf16))
        vectors = vectors - part
    side = jnp.pad(jnp.concatenate(parts, axis=1), ((0, SIDE - 6), (0, group - 3 * share)))

    ring_attn = GatherRing(links, pack(links, w_query, w_key, w_value, b_query, b_value))
    late_out = jnp.concatenate([w_out.T, side])
    late = Box(late_out, w_down.T)
    work = Box(tokens)

    ring_attn.step()
    late.live = [swap(late_out, 2), late.live[1]]
    early = Box(doc_lengths)
    tie(ring_attn, late, early)
    lengths = lax.dynamic_slice_in_dim(early.live[0], lax.axis_index("tensor"), 1, axis=0)[0]
    ends = jnp.sum(jnp.where(jnp.tri(lengths.shape[0], dtype=bool), lengths[None, :], 0), axis=1)
    places = jnp.arange(length, dtype=jnp.int32)
    inside = (places[None, :] >= (ends - lengths)[:, None]) & (places[None, :] < ends[:, None])
    low = jnp.sum(jnp.where(inside, (ends - lengths)[:, None], 0), axis=0)
    high = jnp.sum(jnp.where(inside, ends[:, None], 0), axis=0)
    span = jnp.stack([low, high])
    ring_attn.step()
    late.live = [late.live[0], swap(late.live[1], 2)]
    tie(ring_attn, late)
    window = windows(low, high, BLOCK, length)
    up_row = jnp.concatenate(placed(b_up, me, dp), axis=1)
    up_side = jnp.pad(up_row, ((0, SIDE - 1), (0, 0)))
    ring_up = GatherRing(
        links,
        jnp.concatenate([late_out, late.live[0], jnp.concatenate([w_up, up_side])], axis=1),
    )
    down_blocks = jnp.concatenate([w_down.T, late.live[1]], axis=1)
    ring_down = GatherRing(links, jnp.pad(down_blocks, ((0, SIDE), (0, 0))))
    for _ in range(links.ahead - 2):
        ring_attn.step()
        tie(ring_attn)
    attn_own, _, bias_own = ring_attn.full((3 * group,), rows)

    attn_w, attn_b = [attn_own, None, None, None], [bias_own, None, None, None]
    qkv, mixture, logs = [None] * 4, [None] * 4, [None] * 4

    def attend_group(j):
        mixture[j], logs[j], qkv[j] = attend(work.live[0], attn_w[j], attn_b[j], window, span)
        return Box(mixture[j])

    def core_swap(j):
        attn_w[j ^ 1] = swap(attn_w[j], 1)
        attn_b[j ^ 1] = swap(attn_b[j], 1)

    tie(ring_attn, ring_up, work)
    far = Box(swap(attn_w[0], 2), swap(attn_b[0], 2))
    core_swap(0)
    ring_up.step()
    done = attend_group(0)
    tie(ring_up, work, done)
    ring_up.step()
    done = attend_group(1)
    tie(ring_up, work, done)
    ring_up.step()
    attn_w[2], attn_b[2] = far.live
    for _ in range(links.ahead - 3):
        ring_up.step()
    tie(ring_up, work, ring_down)
    core_swap(2)
    ring_down.step()
    done = attend_group(2)
    hidden = w_up.shape[1]
    out_own, out_across, up_own, side_all, side_sum = ring_up.full((group, group, hidden), rows)
    tie(ring_down, work, done)
    up_w = [up_own, swap(up_own, 1), None, None]
    far = Box(swap(up_own, 2), swap(side_sum, 2))
    out_w = [out_own, swap(out_own, 1), out_across, swap(out_across, 1)]
    side_all = side_all[:, : 2 * group]
    side_core = swap(side_all, 1)
    up_b = [side_sum, swap(side_sum, 1), None, None]
    ring_down.step()
    done = attend_group(3)
    tie(ring_down, work, done)

    flat = jnp.stack([side_all, side_core]).reshape(2, dp, SIDE, 2, group)[:, :, :6, :, : 3 * share]
    flat = flat.reshape(2, dp, 6, 2, 3, share)
    flat = flat[..., 0, :] + flat[..., 1, :] + flat[..., 2, :]
    flat = flat.transpose(2, 1, 3, 0, 4).reshape(6, dp, tensor, share)
    mine = lax.axis_index("tensor")
    flat = jnp.where((mine & 1) == 1, flat[:, :, jnp.array([1, 0, 3, 2])], flat)
    flat = jnp.where((mine & 2) == 2, flat[:, :, jnp.array([2, 3, 0, 1])], flat)
    bias_out, bias_down, norm_gain_one, norm_shift_one, norm_gain_two, norm_shift_two = flat.reshape(
        6, model
    )
    ring_down.step()
    attn = bias_out + work.live[0].astype(f32)
    for j in range(tensor):
        attn = attn + contract(mixture[j], out_w[j], ((0,), (1,)))
    first_out, unit_one, scale_one = normalize(attn, norm_gain_one, norm_shift_one)
    first_low = first_out.astype(bf16)
    activated, slopes = [None] * 4, [None] * 4

    def up_group(j):
        up_pre = contract(work.live[0], up_w[j], ((1,), (0,))) + up_b[j][0:1, 2 * group :]
        act, slope = gelu_parts(up_pre)
        activated[j], slopes[j] = act.astype(bf16), slope.astype(bf16)
        return Box(activated[j])

    work = Box(first_low)
    done = up_group(0)
    tie(ring_down, work, done)
    for _ in range(links.ahead - 3):
        ring_down.step()
    done = up_group(1)
    tie(ring_down, work, done)
    up_w[2], up_b[2] = far.live
    up_w[3], up_b[3] = swap(up_w[2], 1), swap(up_b[2], 1)
    down_own, down_across, _, _ = ring_down.full((hidden, hidden), rows)
    down_w = [down_own, swap(down_own, 1), down_across, swap(down_across, 1)]
    done = [up_group(2), up_group(3)]
    residual = bias_down + first_out
    for j in range(tensor):
        residual = residual + contract(activated[j], down_w[j], ((1,), (1,)))
    result, unit_two, scale_two = normalize(residual, norm_gain_two, norm_shift_two)
    grad_out = cotangent.astype(f32)
    grad_two = normalize_back(grad_out, unit_two, scale_two, norm_gain_two)
    grad_gain_two = jnp.sum(grad_out * unit_two, axis=0)
    grad_shift_two = jnp.sum(grad_out, axis=0)
    grad_bias_down = jnp.sum(grad_two, axis=0)
    work = Box(grad_two.astype(bf16))

    def add(a, b):
        return (a.astype(f32) + b.astype(f32)).astype(bf16)

    def blocks(value):
        return value.reshape(dp, rows, value.shape[-1])

    def grad_down(j):
        return contract(work.live[0], activated[j], ((0,), (0,)), bf16)

    sent = Box(grad_down(3), grad_down(1))
    tie(work, sent)
    three, one = (swap(v, 1) for v in sent.live)
    two, zero = grad_down(2), grad_down(0)
    pair = Box(add(zero, one), add(two, three))
    tie(work, pair)
    sums_down = ScatterRing(links, jnp.concatenate([blocks(v) for v in pair.live], axis=2))
    grad_up, grad_bias_up = [None] * 4, [None] * 4

    def back_up(j):
        made = contract(work.live[0], down_w[j], ((1,), (0,))) * slopes[j].astype(f32)
        grad_up[j] = made.astype(bf16)
        grad_bias_up[j] = jnp.sum(grad_up[j].astype(f32), axis=0, keepdims=True)
        return Box(grad_up[j])

    for j in (3, 1, 2, 0):
        sums_down.step()
        done = back_up(j)
        tie(work, done, sums_down)
    for _ in range(links.ahead - 4):
        sums_down.step()

    def grad_w_up(j):
        return contract(work.live[0], grad_up[j], ((0,), (0,)), bf16)

    end_down = Box(swap(sums_down.total[:, hidden:].astype(bf16), 2))
    work = Box(first_low)
    sent = Box(grad_w_up(3), grad_w_up(1))
    tie(work, sent, end_down)
    three, one = (swap(v, 1) for v in sent.live)
    two, zero = grad_w_up(2), grad_w_up(0)
    pair = Box(add(zero, one), add(two, three), grad_up[0])
    tie(work, pair)
    own_up, across_up, grad_up[0] = pair.live
    half = model // 2
    far_low = Box(swap(across_up[:half], 2))
    grad_first = grad_two
    for j in range(tensor):
        grad_first = grad_first + contract(grad_up[j], up_w[j], ((1,), (1,)))
    grad_one = normalize_back(grad_first, unit_one, scale_one, norm_gain_one)
    grad_gain_one = jnp.sum(grad_first * unit_one, axis=0)
    grad_shift_one = jnp.sum(grad_first, axis=0)
    grad_bias_out = jnp.sum(grad_one, axis=0)
    work = Box(grad_one.astype(bf16))
    far_high = Box(across_up[half:])
    tie(work, far_low, far_high)
    far_high.live = [swap(far_high.live[0], 2)]

    zero_row = jnp.zeros_like(grad_bias_out)
    sums = jnp.stack(
        [
            grad_bias_out,
            grad_bias_down,
            grad_gain_one,
            grad_shift_one,
            grad_gain_two,
            grad_shift_two,
            zero_row,
            zero_row,
        ]
    )
    grad_qkv = [None] * 4

    def back_group(j, arrived=None):
        grad_mix = contract(out_w[j][:model], work.live[0], ((0,), (1,)), bf16)
        grad_qkv[j] = attend_back(qkv[j], mixture[j], logs[j], grad_mix, window, span)
        return grad_weight(
            dp, tokens, grad_qkv[j], work.live[0], mixture[j], grad_bias_up[j], sums, arrived
        )

    three = Box(back_group(3))
    tie(work, three, far_high)
    sums_up = ScatterRing(
        links, blocks(add(own_up, jnp.concatenate(far_low.live + far_high.live)))
    )
    recv = swap(three.live[0], 1)
    sums_up.step()
    two = Box(back_group(2, recv))
    tie(work, two, sums_up)
    split = dp // 2
    far_low = Box(swap(two.live[0][:split], 2))
    sums_up.step()
    one = Box(back_group(1))
    far_high = Box(two.live[0][split:])
    tie(work, one, sums_up, far_low, far_high)
    far_high.live = [swap(far_high.live[0], 2)]
    recv = swap(one.live[0], 1)
    sums_up.step()
    zero = Box(back_group(0, recv))
    tie(work, zero, sums_up, far_high)
    sums_attn = ScatterRing(
        links, add(zero.live[0], jnp.concatenate(far_low.live + far_high.live))
    )
    grad_input = grad_one
    for j in range(tensor):
        sums_attn.step()
        if sums_up.count < links.ahead:
            sums_up.step()
        grad_input = grad_input + contract(grad_qkv[j], attn_w[j], ((0,), (1,)))
        holder = Box(grad_input)
        tie(holder, sums_attn, sums_up)
        grad_input = holder.live[0]
    for ring in (sums_attn, sums_up):
        while ring.count < links.ahead:
            ring.step()
    grad_attn = sums_attn.total
    grad_down_own = sums_down.total[:, :hidden] + end_down.live[0].astype(f32)

    side = grad_attn[rows:]
    outs = []
    for row, at, shape in (
        (0, 0, b_query.shape),
        (0, 2 * group, b_value.shape),
        (1, 0, b_up.shape),
    ):
        count, per = shape
        held = side[row, at : at + count * per * dp].reshape(count, per * dp)
        outs.append(lax.dynamic_slice_in_dim(held, me * per, per, axis=1))
    own = (me * tensor + mine) * share
    held = lax.dynamic_slice_in_dim(side[TAIL - 8 : TAIL - 2], own, share, axis=1)
    grad_attn = grad_attn[:rows]
    return (
        result.astype(bf16),
        grad_input.astype(bf16),
        grad_attn[:, :group],
        grad_attn[:, group : 2 * group],
        grad_attn[:, 2 * group : 3 * group],
        grad_attn[:, 3 * group :].T,
        sums_up.total,
        grad_down_own.T,
        *outs,
        *[held[i] for i in range(6)],
    )


def solution(mesh):
    both = P(("dp", "tensor"))
    rows = P(("dp", "tensor"), None)
    down = P("tensor", "dp")
    wide = P("dp", "tensor")
    weights = (wide, wide, wide, down, wide, down, down, down, down)
    return jax.shard_map(
        per_device,
        mesh=mesh,
        in_specs=(rows, P("dp", None)) + weights + (both,) * 6 + (rows,),
        out_specs=(rows, rows) + weights + (both,) * 6,
        check_vma=False,
    )
```

```python
import functools

import jax
import jax.numpy as jnp
import numpy as np
from jax import lax
from jax.experimental import pallas as pl
from jax.experimental.pallas import tpu as pltpu
from jax.sharding import PartitionSpec as P

HD = 64
BLOCK = 256
EXTRA = 16
STEP = 128
SIDE = 8
TAIL = 16

epsilon = 1e-06
root_half = 0.7071067811865476
inv_root_tau = 0.3989422804014327
masked_value = -1e30
bf16 = jnp.bfloat16
f32 = jnp.float32


def contract(a, b, dims, out=f32):
    return lax.dot_general(a, b, (dims, ((), ())), preferred_element_type=f32).astype(out)


def ring_order(size):
    return list(range(0, size, 2)) + list(range(size - 1, 0, -2)) if size > 1 else [0]


class Links:
    def __init__(self, dp, tensor):
        self.dp, self.tensor = dp, tensor
        order = ring_order(dp)
        self.order = jnp.array(order, jnp.int32)
        place = [0] * dp
        for position, member in enumerate(order):
            place[member] = position
        self.forward = [(order[i], order[(i + 1) % dp]) for i in range(dp)]
        self.backward = [(b, a) for a, b in self.forward]
        self.me = lax.axis_index("dp")
        self.position = jnp.array(place, jnp.int32)[self.me]
        self.ahead = dp // 2
        self.behind = dp - 1 - self.ahead
        offsets = jnp.arange(-self.ahead, self.behind + 1, dtype=jnp.int32)
        self.members = self.order[(self.position + offsets + dp) % dp]

    def swap(self, value, mask):
        return lax.ppermute(value, "tensor", [(i, i ^ mask) for i in range(self.tensor)])


def tie(*holders):
    flat, tree = jax.tree.flatten([holder.live for holder in holders])
    flat = lax.optimization_barrier(tuple(flat))
    for holder, live in zip(holders, jax.tree.unflatten(tree, flat)):
        holder.live = live


class Box:
    def __init__(self, *live):
        self.live = list(live)


class GatherRing:
    def __init__(self, links, value):
        self.links = links
        self.live = [value, value]
        self.pieces = {0: value}
        self.count = 0

    def step(self):
        links = self.links
        self.count += 1
        up, down = self.live
        up = lax.ppermute(up, "dp", links.forward)
        self.pieces[-self.count] = up
        if self.count <= links.behind:
            down = lax.ppermute(down, "dp", links.backward)
            self.pieces[self.count] = down
        self.live = [up, down]

    def full(self, plan, rows):
        links = self.links
        pieces = [self.pieces[offset] for offset in range(-links.ahead, links.behind + 1)]
        return assemble(links.members, pieces, plan, rows)


class ScatterRing:
    def __init__(self, links, groups):
        self.links = links
        self.groups = groups
        self.count = 0
        self.total = None
        self.live = ring_call(links, groups, (links.ahead, -links.behind), (), bf16)

    def step(self):
        links = self.links
        self.count += 1
        up, down = self.live
        up = lax.ppermute(up, "dp", links.forward)
        if self.count <= links.behind:
            down = lax.ppermute(down, "dp", links.backward)
        left_up, left_down = links.ahead - self.count, links.behind - self.count
        if left_up == 0:
            (self.total,) = ring_call(links, self.groups, (0,), (up, down), f32)
        elif left_down > 0:
            up, down = ring_call(links, self.groups, (left_up, -left_down), (up, down), bf16)
        else:
            (up,) = ring_call(links, self.groups, (left_up,), (up,), bf16)
        self.live = [up, down]


VMEM = pl.BlockSpec(memory_space=pltpu.VMEM)
SMEM = pl.BlockSpec(memory_space=pltpu.SMEM)


def ring_kernel(members_ref, *refs, counts, sends, dtype):
    size = sum(counts)
    parts, arrived, outs = refs[: size * sends], refs[size * sends : -sends], refs[-sends:]
    share = len(arrived) // sends
    for index in range(sends):
        at, column = index * size, 0
        for count in counts:
            width = parts[at].shape[-1]
            made = parts[at][0].astype(f32)
            for more in range(1, count):
                made = made + parts[at + more][0].astype(f32)
            for one in arrived[index * share : (index + 1) * share]:
                made = made + one[:, column : column + width].astype(f32)
            outs[index][:, column : column + width] = made.astype(dtype)
            at += count
            column += width


def ring_call(links, groups, offsets, arrived, dtype):
    rows = groups[0][0].shape[1]
    columns = sum(group[0].shape[2] for group in groups)
    whole = pl.BlockSpec((rows, columns), lambda i, m: (0, 0))
    sources = [source for group in groups for source in group]

    def part(source, offset):
        index = (offset + links.ahead) % links.dp
        return pl.BlockSpec((1, rows, source.shape[2]), lambda i, m: (m[index], 0, 0))

    size = rows * columns
    return list(
        pl.pallas_call(
            functools.partial(
                ring_kernel,
                counts=[len(group) for group in groups],
                sends=len(offsets),
                dtype=dtype,
            ),
            out_shape=[jax.ShapeDtypeStruct((rows, columns), dtype) for _ in offsets],
            grid_spec=pltpu.PrefetchScalarGridSpec(
                num_scalar_prefetch=1,
                grid=(1,),
                in_specs=[part(source, offset) for offset in offsets for source in sources]
                + [whole] * len(arrived),
                out_specs=[whole] * len(offsets),
            ),
            compiler_params=pltpu.CompilerParams(vmem_limit_bytes=12 << 20),
            cost_estimate=pl.CostEstimate(
                flops=size * 2, bytes_accessed=6 * size * len(offsets), transcendentals=0
            ),
            name="ring_sum",
        )(links.members, *(sources * len(offsets)), *arrived)
    )


def whole(*shape):
    return pl.BlockSpec(shape, lambda *_: (0,) * len(shape))


def like(*arrays):
    return [whole(*array.shape) for array in arrays]


def assemble_kernel(members_ref, *refs, count, plan, rows):
    pieces, outs = refs[:count], refs[count:]
    sides = pieces[0].shape[0] > rows
    total = None
    for index in range(count):
        start = pl.multiple_of(members_ref[index] * rows, rows)
        for out, (at, width, _) in zip(outs, plan):
            out[pl.ds(start, rows), :] = pieces[index][0:rows, at : at + width]
        if sides:
            side = pieces[index][rows:, :].astype(f32)
            total = side if total is None else total + side
    for out, (at, width, kept) in zip(outs, plan):
        if kept is not None:
            out[count * rows :, :] = jnp.broadcast_to(
                total[kept : kept + 1, at : at + width], (SIDE, width)
            ).astype(bf16)
    if sides:
        outs[-1][...] = total


def assemble(members, pieces, plan, rows):
    count = len(pieces)
    full, wide = pieces[0].shape
    if rows % 16:
        stacked = jnp.stack(pieces)
        back = jnp.zeros((count,), jnp.int32).at[members].set(jnp.arange(count, dtype=jnp.int32))
        stacked = jnp.take(stacked, back, axis=0)
        weights = stacked[:, :rows].reshape(count * rows, -1)
        total = jnp.sum(stacked[:, rows:].astype(f32), axis=0)
        outs = []
        for at, width, kept in plan:
            out = weights[:, at : at + width]
            if kept is not None:
                row = jnp.broadcast_to(total[kept : kept + 1, at : at + width], (SIDE, width))
                out = jnp.concatenate([out, row.astype(bf16)])
            outs.append(out)
        return outs + ([total] if full > rows else [])
    shapes = [
        jax.ShapeDtypeStruct((count * rows + (0 if kept is None else SIDE), width), bf16)
        for _, width, kept in plan
    ]
    if full > rows:
        shapes.append(jax.ShapeDtypeStruct((full - rows, wide), f32))
    return pl.pallas_call(
        functools.partial(assemble_kernel, count=count, plan=plan, rows=rows),
        grid=(1,),
        out_shape=shapes,
        in_specs=[SMEM] + like(*pieces),
        out_specs=like(*shapes),
        compiler_params=pltpu.CompilerParams(vmem_limit_bytes=16 << 20),
        cost_estimate=pl.CostEstimate(
            flops=0, bytes_accessed=4 * count * full * wide, transcendentals=0
        ),
        name="assemble",
    )(members, *pieces)


def one_hot(first, rows, size):
    hit = lax.broadcasted_iota(jnp.int32, (rows, size), 1) == (
        lax.broadcasted_iota(jnp.int32, (rows, size), 0) + first
    )
    return jnp.where(hit, 1.0, 0.0).astype(bf16)


def placed(table, me, dp):
    count, per = table.shape
    spread = contract(table, one_hot(me * per, per, per * dp), ((1,), (0,)))
    return [spread[row : row + 1] for row in range(count)]


def only_row(row, at):
    line = lax.broadcasted_iota(jnp.int32, (SIDE, row.shape[1]), 0)
    return jnp.where(line == at, row, 0.0)


def pack_kernel(me_ref, query_ref, key_ref, value_ref, b_query_ref, b_value_ref, out_ref, *, dp):
    rows, group = query_ref.shape
    out_ref[0:rows, 0:group] = query_ref[...]
    out_ref[0:rows, group : 2 * group] = key_ref[...]
    out_ref[0:rows, 2 * group :] = value_ref[...]
    me = me_ref[0]
    row = jnp.concatenate(
        placed(b_query_ref[...], me, dp)
        + [jnp.zeros((1, group), f32)]
        + placed(b_value_ref[...], me, dp),
        axis=1,
    )
    out_ref[rows:, :] = only_row(row, 0).astype(bf16)


def pack_late_kernel(me_ref, w_out_ref, w_down_ref, vectors_ref, out_ref, down_ref, *, dp):
    rows, hidden = w_down_ref.shape[1], w_down_ref.shape[0]
    out_ref[...] = w_out_ref[...].T
    down_ref[0:rows, :] = w_down_ref[...].T
    left = vectors_ref[...]
    share = left.shape[1]
    place = one_hot(me_ref[0] * share, share, share * dp)
    spread = []
    for _ in range(3):
        part = left.astype(bf16)
        left = left - part.astype(f32)
        spread.append(contract(part, place, ((1,), (0,))))
    row = jnp.concatenate(spread, axis=1)
    blank = jnp.zeros((SIDE, hidden - row.shape[1]), f32)
    down_ref[rows:, :] = jnp.concatenate([row, blank], axis=1).astype(bf16)


def pack_up_kernel(
    me_ref, out_ref, far_out_ref, w_up_ref, down_ref, far_down_ref, b_up_ref, up_ref, pair_ref, *, dp
):
    rows, hidden = w_up_ref.shape
    group = out_ref.shape[1]
    up_ref[0:rows, 0:group] = out_ref[...]
    up_ref[0:rows, group : 2 * group] = far_out_ref[...]
    up_ref[0:rows, 2 * group :] = w_up_ref[...]
    pair_ref[:, 0:hidden] = down_ref[0:rows, :]
    pair_ref[:, hidden:] = far_down_ref[0:rows, :]
    near = down_ref[rows:, 0 : 3 * group].astype(f32)
    far = far_down_ref[rows:, 0 : 3 * group].astype(f32)
    bias = jnp.concatenate(
        [jnp.zeros((1, 2 * group), f32)] + placed(b_up_ref[...], me_ref[0], dp), axis=1
    )
    side = jnp.concatenate([near, far], axis=1) + only_row(bias, 6)
    up_ref[rows:, :] = side.astype(bf16)


def small_call(kernel, name, links, shapes, *operands):
    return pl.pallas_call(
        functools.partial(kernel, dp=links.dp),
        grid=(1,),
        out_shape=shapes,
        in_specs=[SMEM] + like(*operands),
        out_specs=like(*shapes),
        compiler_params=pltpu.CompilerParams(vmem_limit_bytes=8 << 20),
        name=name,
    )(links.me.reshape(1), *operands)


def windows(low, high, block, length):
    begin = low.reshape(-1, block)[:, 0] // STEP * STEP
    end = high.reshape(-1, block)[:, -1]
    count = (end - begin + block - 1) // block
    return jnp.stack([jnp.minimum(begin, length - count * block), count])


def fill_bias(bias, begin, low, high, size):
    keys = lax.broadcasted_iota(jnp.int32, (size, low.shape[1]), 0) + begin
    bias[0:size, :] = jnp.where((keys >= low) & (keys < high), 0.0, masked_value)


def attend_kernel(
    window_ref, tokens_ref, weight_ref, span_ref, out_ref, log_ref, qkv_ref, keys, values, bias, hold, *, block
):
    length = qkv_ref.shape[1]
    heads = qkv_ref.shape[0] // (3 * HD)
    width = heads * HD
    model = tokens_ref.shape[1]
    made = contract(tokens_ref[...], weight_ref[0:model, :], ((1,), (0,)))
    made = made + weight_ref[model : model + 1, :].astype(f32)
    qkv_ref[...] = made.astype(bf16).T
    tail = jnp.where(lax.broadcasted_iota(jnp.int32, (EXTRA, length), 0) == 0, 1.0, 0.0).astype(bf16)
    for head in range(heads):
        keys[head] = qkv_ref[width + head * HD : width + (head + 1) * HD, :].T
        values[head, 0:HD, :] = qkv_ref[2 * width + head * HD : 2 * width + (head + 1) * HD, :]
        values[head, HD : HD + EXTRA, :] = tail

    def one_block(index, _):
        lanes = pl.ds(pl.multiple_of(index * block, block), block)
        begin = pl.multiple_of(window_ref[0, index], STEP)

        def with_count(count):
            fill_bias(bias, begin, span_ref[0:1, lanes], span_ref[1:2, lanes], count * block)
            tops = []
            for head in range(heads):
                queries = qkv_ref[head * HD : (head + 1) * HD, lanes] * 0.125
                top = None
                for piece in range(count):
                    rows = slice(piece * block, (piece + 1) * block)
                    own = pl.ds(begin + piece * block, block)
                    scores = contract(keys[head, own, :], queries, ((1,), (0,))) + bias[rows, :]
                    hold[head, rows, :] = scores
                    most = jnp.max(scores.reshape(block // 8, 8, block), axis=0)
                    top = most if top is None else jnp.maximum(top, most)
                tops.append(jnp.max(top, axis=0, keepdims=True))
            for head in range(heads):
                total = None
                for piece in range(count):
                    rows = slice(piece * block, (piece + 1) * block)
                    own = pl.ds(begin + piece * block, block)
                    weights = jnp.exp(hold[head, rows, :] - tops[head]).astype(bf16)
                    made = contract(values[head, :, own], weights, ((1,), (0,)))
                    total = made if total is None else total + made
                mass = total[HD : HD + 1, :]
                out_ref[head * HD : (head + 1) * HD, lanes] = (total[:HD] / mass).astype(bf16)
                log_ref[head : head + 1, lanes] = tops[head] + jnp.log(mass)

        for count in range(1, length // block + 1):
            pl.when(window_ref[1, index] == count)(functools.partial(with_count, count))
        return 0

    lax.fori_loop(0, length // block, one_block, 0)


def attend_back_kernel(
    window_ref, qkv_ref, span_ref, out_ref, log_ref, weight_ref, one_ref, result_ref, keys, values, bias, grad_key, grad_value, grad_ref, *, block
):
    length = qkv_ref.shape[1]
    grad_ref[...] = contract(weight_ref[...], one_ref[...], ((0,), (1,)), bf16)
    heads = qkv_ref.shape[0] // (3 * HD)
    width = heads * HD
    for head in range(heads):
        keys[head] = qkv_ref[width + head * HD : width + (head + 1) * HD, :].T
        values[head] = qkv_ref[2 * width + head * HD : 2 * width + (head + 1) * HD, :].T
    grad_key[...] = jnp.zeros_like(grad_key)
    grad_value[...] = jnp.zeros_like(grad_value)

    def one_block(index, _):
        lanes = pl.ds(pl.multiple_of(index * block, block), block)
        begin = pl.multiple_of(window_ref[0, index], STEP)

        def with_count(count):
            size = count * block
            window = pl.ds(begin, size)
            fill_bias(bias, begin, span_ref[0:1, lanes], span_ref[1:2, lanes], size)
            for head in range(heads):
                own = slice(head * HD, (head + 1) * HD)
                queries = qkv_ref[own, lanes] * 0.125
                grads = grad_ref[own, lanes]
                delta = jnp.sum(
                    out_ref[own, lanes].astype(f32) * grads.astype(f32), axis=0, keepdims=True
                )
                scores = contract(keys[head, window, :], queries, ((1,), (0,))) + bias[0:size, :]
                weights = jnp.exp(scores - log_ref[head : head + 1, lanes])
                grad_prob = contract(values[head, window, :], grads, ((1,), (0,)))
                grad_scores = (weights * (grad_prob - delta)).astype(bf16)
                grad_value[own, window] += contract(grads, weights.astype(bf16), ((1,), (1,)))
                grad_key[own, window] += contract(queries, grad_scores, ((1,), (1,)))
                key_cols = qkv_ref[width + head * HD : width + (head + 1) * HD, window]
                made = contract(key_cols, grad_scores, ((1,), (0,)))
                result_ref[own, lanes] = (made * 0.125).astype(bf16)

        for count in range(1, length // block + 1):
            pl.when(window_ref[1, index] == count)(functools.partial(with_count, count))
        return 0

    lax.fori_loop(0, length // block, one_block, 0)
    result_ref[width : 2 * width, :] = grad_key[...].astype(bf16)
    result_ref[2 * width :, :] = grad_value[...].astype(bf16)


def attend(tokens, weight, window, span):
    length, model = tokens.shape
    width = weight.shape[1]
    heads = width // (3 * HD)
    return pl.pallas_call(
        functools.partial(attend_kernel, block=BLOCK),
        out_shape=(
            jax.ShapeDtypeStruct((heads * HD, length), bf16),
            jax.ShapeDtypeStruct((8, length), f32),
            jax.ShapeDtypeStruct((width, length), bf16),
        ),
        grid=(1,),
        in_specs=[SMEM] + like(tokens, weight, span),
        out_specs=(whole(heads * HD, length), whole(8, length), whole(width, length)),
        scratch_shapes=[
            pltpu.VMEM((heads, length, HD), bf16),
            pltpu.VMEM((heads, HD + EXTRA, length), bf16),
            pltpu.VMEM((length, BLOCK), f32),
            pltpu.VMEM((heads, length, BLOCK), f32),
        ],
        compiler_params=pltpu.CompilerParams(vmem_limit_bytes=24 << 20),
        cost_estimate=pl.CostEstimate(
            flops=4 * heads * length * length * HD + 2 * length * model * width,
            bytes_accessed=4 * width * length,
            transcendentals=heads * length * length,
        ),
        name="attend",
    )(window, tokens, weight, span)


def attend_back(qkv, out, logs, weight, one, window, span):
    width, length = qkv.shape
    heads = width // (3 * HD)
    return pl.pallas_call(
        functools.partial(attend_back_kernel, block=BLOCK),
        out_shape=jax.ShapeDtypeStruct((width, length), bf16),
        in_specs=[SMEM] + [VMEM] * 6,
        out_specs=VMEM,
        scratch_shapes=[
            pltpu.VMEM((heads, length, HD), bf16),
            pltpu.VMEM((heads, length, HD), bf16),
            pltpu.VMEM((length, BLOCK), f32),
            pltpu.VMEM((heads * HD, length), f32),
            pltpu.VMEM((heads * HD, length), f32),
            pltpu.VMEM((heads * HD, length), bf16),
        ],
        compiler_params=pltpu.CompilerParams(vmem_limit_bytes=16 << 20),
        cost_estimate=pl.CostEstimate(
            flops=10 * heads * length * length * HD,
            bytes_accessed=6 * width * length,
            transcendentals=heads * length * length,
        ),
        name="attend_back",
    )(window, qkv, span, out, logs, weight, one)


def grad_weight_kernel(tokens_ref, grad_ref, one_ref, mixture_ref, *refs):
    more, out_ref = refs[2:-1], refs[-1]
    up_ref, vectors_ref = refs[0], refs[1]
    dp, full, columns = out_ref.shape
    rows = full - TAIL
    wide = grad_ref.shape[0]
    group = wide // 3
    made = contract(tokens_ref[...], grad_ref[...], ((0,), (1,)))
    out_low = contract(one_ref[...], mixture_ref[...], ((0,), (1,)))
    ones = jnp.ones((TAIL, grad_ref.shape[1]), bf16)
    lane = contract(ones, grad_ref[...], ((1,), (1,)))
    line = lax.broadcasted_iota(jnp.int32, (TAIL, columns), 0)
    bias_row = jnp.concatenate([lane, jnp.zeros((TAIL, columns - wide), f32)], axis=1)
    side = jnp.where(line == 0, bias_row, 0.0) + jnp.where(line == 1, up_ref[0:1, :], 0.0)
    lower = jnp.concatenate([jnp.zeros((TAIL - 8, columns), f32), vectors_ref[...]], axis=0)
    side = side + lower
    for index in range(dp):
        own = slice(index * rows, (index + 1) * rows)
        left, right, low = made[own], out_low[own], side
        if more:
            left = left + more[0][index, 0:rows, 0:wide].astype(f32)
            right = right + more[0][index, 0:rows, wide:].astype(f32)
            low = low + more[0][index, rows:, :].astype(f32)
        out_ref[index, 0:rows, 0:wide] = left.astype(bf16)
        out_ref[index, 0:rows, wide:] = right.astype(bf16)
        out_ref[index, rows:, :] = low.astype(bf16)


def grad_weight(dp, tokens, grad, one, mixture, up_row, vectors, arrived=None):
    length, model = tokens.shape
    wide, group = grad.shape[0], mixture.shape[0]
    more = [] if arrived is None else [arrived]
    return pl.pallas_call(
        grad_weight_kernel,
        out_shape=jax.ShapeDtypeStruct((dp, model // dp + TAIL, wide + group), bf16),
        in_specs=[VMEM] * (6 + len(more)),
        out_specs=VMEM,
        compiler_params=pltpu.CompilerParams(vmem_limit_bytes=24 << 20),
        cost_estimate=pl.CostEstimate(
            flops=2 * length * model * (wide + group),
            bytes_accessed=2 * (length + model) * (wide + group + model),
            transcendentals=0,
        ),
        name="grad_weight",
    )(tokens, grad, one, mixture, up_row, vectors, *more)


def normalize(values):
    average = jnp.mean(values, axis=-1, keepdims=True)
    centred = values - average
    variance = jnp.mean(centred * centred, axis=-1, keepdims=True)
    inv_scale = lax.rsqrt(variance + epsilon)
    return centred * inv_scale, inv_scale


def normalize_back(grad_out, unit_rows, inv_scale, norm_gain):
    grad_unit = grad_out * norm_gain
    middle = grad_unit - jnp.mean(grad_unit, axis=-1, keepdims=True)
    middle = middle - unit_rows * jnp.mean(grad_unit * unit_rows, axis=-1, keepdims=True)
    return inv_scale * middle


def gelu_parts(up_pre):
    normal_cdf = 0.5 * (1.0 + lax.erf(up_pre * root_half))
    return (
        up_pre * normal_cdf,
        normal_cdf + up_pre * inv_root_tau * jnp.exp(-0.5 * up_pre * up_pre),
    )


def tiled(kernel, name, steps, operands, tiles, shapes, flops, limit=40):
    def spec(array, tile):
        if tile is None:
            return whole(*array.shape)
        block = list(array.shape)
        block[tile] //= steps
        if tile:
            return pl.BlockSpec(tuple(block), lambda i: (0, i))
        return pl.BlockSpec(tuple(block), lambda i: (i, 0))

    shapes, out_tiles = [x for x, _ in shapes], [x for _, x in shapes]
    moved = sum(x.size * x.dtype.itemsize for x in list(operands) + shapes)
    return pl.pallas_call(
        kernel,
        grid=(steps,),
        out_shape=shapes,
        in_specs=[spec(x, t) for x, t in zip(operands, tiles)],
        out_specs=[spec(x, t) for x, t in zip(shapes, out_tiles)],
        compiler_params=pltpu.CompilerParams(vmem_limit_bytes=limit << 20),
        cost_estimate=pl.CostEstimate(flops=flops, bytes_accessed=moved, transcendentals=0),
        name=name,
    )(*operands)


def shape(*size, dtype=f32):
    return jax.ShapeDtypeStruct(size, dtype)


def vectors_kernel(lane_ref, near_ref, far_ref, out_ref):
    model = out_ref.shape[1]
    size = near_ref.shape[1] // 6
    total = jnp.zeros((SIDE, model), f32)
    lanes = lax.broadcasted_iota(jnp.int32, (size, model), 1)
    for j in range(4):
        held = near_ref if j % 2 == 0 else far_ref
        first = (j // 2) * 3 * size
        place = jnp.where(lanes == lane_ref[:, j : j + 1], 1.0, 0.0).astype(bf16)
        for part in range(3):
            at = first + part * size
            total = total + contract(held[:, at : at + size].astype(bf16), place, ((1,), (0,)))
    out_ref[...] = total


def out_kernel(m0, m1, m2, m3, w0, w1, w2, w3, vectors, tokens, low_ref, unit_ref, scale_ref):
    total = vectors[0:1, :] + tokens[...].astype(f32)
    for mixture, weight in ((m0, w0), (m1, w1), (m2, w2), (m3, w3)):
        total = total + contract(mixture[...], weight[...], ((0,), (1,)))
    unit, scale = normalize(total)
    unit_ref[...] = unit
    scale_ref[...] = scale
    low_ref[...] = (unit * vectors[2:3, :] + vectors[3:4, :]).astype(bf16)


def up_kernel(low, weight, act_ref, slope_ref):
    model = low.shape[1]
    up_pre = contract(low[...], weight[0:model, :], ((1,), (0,)))
    act, slope = gelu_parts(up_pre + weight[model : model + 1, :].astype(f32))
    act_ref[...] = act.astype(bf16)
    slope_ref[...] = slope.astype(bf16)


def column_sums(ref, rows):
    line = lax.broadcasted_iota(jnp.int32, ref.shape, 0)
    made = jnp.zeros(ref.shape, f32)
    for at, values in rows:
        made = made + jnp.where(line == at, jnp.sum(values, axis=0, keepdims=True), 0.0)

    @pl.when(pl.program_id(0) == 0)
    def _():
        ref[...] = made

    @pl.when(pl.program_id(0) > 0)
    def _():
        ref[...] += made


def down_kernel(
    a0, a1, a2, a3, w0, w1, w2, w3, vectors, unit_ref, cotangent, result_ref, grad_ref, low_ref, sums_ref
):
    total = vectors[1:2, :] + unit_ref[...] * vectors[2:3, :] + vectors[3:4, :]
    for act, weight in ((a0, w0), (a1, w1), (a2, w2), (a3, w3)):
        total = total + contract(act[...], weight[...], ((1,), (1,)))
    unit, scale = normalize(total)
    result_ref[...] = (unit * vectors[4:5, :] + vectors[5:6, :]).astype(bf16)
    grad_out = cotangent[...].astype(f32)
    grad = normalize_back(grad_out, unit, scale, vectors[4:5, :])
    grad_ref[...] = grad
    low_ref[...] = grad.astype(bf16)
    column_sums(sums_ref, ((1, grad), (4, grad_out * unit), (5, grad_out)))


def slope_kernel(low, weight, slope, grad_ref, sums_ref):
    made = contract(low[...], weight[...], ((1,), (0,))) * slope[...].astype(f32)
    made = made.astype(bf16)
    grad_ref[...] = made
    column_sums(sums_ref, ((0, made.astype(f32)),))


def first_kernel(
    g0, g1, g2, g3, w0, w1, w2, w3, vectors, two, unit_ref, scale, sums_two, grad_ref, low_ref, sums_ref
):
    total = two[...]
    model = total.shape[1]
    for grad, weight in ((g0, w0), (g1, w1), (g2, w2), (g3, w3)):
        total = total + contract(grad[...], weight[0:model, :], ((1,), (1,)))
    unit = unit_ref[...]
    grad = normalize_back(total, unit, scale[...], vectors[2:3, :])
    grad_ref[...] = grad
    low_ref[...] = grad.astype(bf16)
    column_sums(sums_ref, ((0, grad), (2, total * unit), (3, total)))

    @pl.when(pl.program_id(0) == 0)
    def _():
        sums_ref[...] += sums_two[...]


def per_device(
    tokens,
    doc_lengths,
    w_query,
    w_key,
    w_value,
    w_out,
    w_up,
    w_down,
    b_query,
    b_value,
    b_up,
    b_out,
    b_down,
    gain_one,
    shift_one,
    gain_two,
    shift_two,
    cotangent,
):
    dp, tensor = lax.axis_size("dp"), lax.axis_size("tensor")
    length, model = tokens.shape
    rows = model // dp
    group = w_query.shape[1]
    links = Links(dp, tensor)
    swap = links.swap

    share = b_out.shape[0]
    me = links.me
    mine = lax.axis_index("tensor")
    hidden = w_up.shape[1]
    (packed,) = small_call(
        pack_kernel,
        "pack",
        links,
        [shape(rows + SIDE, 3 * group, dtype=bf16)],
        w_query,
        w_key,
        w_value,
        b_query,
        b_value,
    )
    ring_attn = GatherRing(links, packed)
    zero = jnp.zeros((share,), f32)
    vectors = jnp.stack([b_out, b_down, gain_one, shift_one, gain_two, shift_two, zero, zero])

    ring_attn.step()
    late_out, late_down = small_call(
        pack_late_kernel,
        "pack_late",
        links,
        [shape(rows, group, dtype=bf16), shape(rows + SIDE, hidden, dtype=bf16)],
        w_out,
        w_down,
        vectors,
    )
    late = Box(late_out, late_down, doc_lengths)
    tie(ring_attn, late)
    late_out, late_down, early_lengths = late.live
    ring_attn.step()
    far_late = Box(swap(late_out, 2), swap(late_down, 2))
    lengths = lax.dynamic_slice_in_dim(early_lengths, mine, 1, axis=0)[0]
    ends = jnp.sum(jnp.where(jnp.tri(lengths.shape[0], dtype=bool), lengths[None, :], 0), axis=1)
    places = jnp.arange(length, dtype=jnp.int32)
    inside = (places[None, :] >= (ends - lengths)[:, None]) & (places[None, :] < ends[:, None])
    low = jnp.sum(jnp.where(inside, (ends - lengths)[:, None], 0), axis=0)
    high = jnp.sum(jnp.where(inside, ends[:, None], 0), axis=0)
    span = Box(jnp.stack([low, high]))
    tie(ring_attn, far_late, span)
    span = span.live[0]
    ring_attn.step()
    window = windows(span[0], span[1], BLOCK, length)
    up_chunk, down_chunk = small_call(
        pack_up_kernel,
        "pack_up",
        links,
        [
            shape(rows + SIDE, 2 * group + hidden, dtype=bf16),
            shape(rows, 2 * hidden, dtype=bf16),
        ],
        late_out,
        far_late.live[0],
        w_up,
        late_down,
        far_late.live[1],
        b_up,
    )
    ring_up = GatherRing(links, up_chunk)
    ring_down = GatherRing(links, down_chunk)
    tie(ring_attn, ring_up, ring_down)
    for _ in range(links.ahead - 3):
        ring_attn.step()
    attn_own, _ = ring_attn.full([(0, 3 * group, 0)], rows)

    attn_w = [attn_own, None, None, None]
    qkv, mixture, logs = [None] * 4, [None] * 4, [None] * 4

    def attend_group(j):
        mixture[j], logs[j], qkv[j] = attend(work.live[0], attn_w[j], window, span)
        return Box(mixture[j])

    work = Box(tokens, attn_own)
    tie(ring_attn, ring_up, work)
    attn_w[0] = work.live[1]
    work = Box(work.live[0])
    far = Box(swap(attn_w[0], 2))
    attn_w[1] = swap(attn_w[0], 1)
    ring_up.step()
    done = attend_group(0)
    tie(ring_up, work, done)
    ring_up.step()
    done = attend_group(1)
    tie(ring_up, work, done)
    ring_up.step()
    tie(ring_up, work, far)
    attn_w[2] = far.live[0]
    attn_w[3] = swap(attn_w[2], 1)
    for _ in range(links.ahead - 3):
        ring_up.step()
    done = attend_group(2)
    tie(ring_up, work, done, ring_down)
    ring_down.step()
    out_own, out_across, up_own, side_near = ring_up.full(
        [(0, group, None), (group, group, None), (2 * group, hidden, 6)], rows
    )
    far = Box(swap(up_own, 2))
    out_w = [out_own, swap(out_own, 1), out_across, swap(out_across, 1)]
    side_far = swap(side_near, 1)
    done = attend_group(3)
    tie(ring_down, work, done)

    ring_down.step()
    count = np.arange(dp * share)
    base = jnp.asarray((count // share * tensor * share + count % share)[:, None], jnp.int32)
    lanes = base + (mine ^ jnp.arange(4, dtype=jnp.int32))[None, :] * share
    (vectors,) = tiled(
        vectors_kernel,
        "vectors",
        1,
        (lanes, side_near, side_far),
        (None,) * 3,
        [(shape(SIDE, model), None)],
        0,
    )
    up_w = [up_own, swap(up_own, 1), None, None]
    first_low, unit_one, scale_one = tiled(
        out_kernel,
        "attention_out",
        4,
        (*mixture, *out_w, vectors, work.live[0]),
        (1,) * 4 + (None,) * 5 + (0,),
        [(shape(length, model, dtype=bf16), 0), (shape(length, model), 0), (shape(length, 1), 0)],
        2 * length * model * model,
    )
    activated, slopes = [None] * 4, [None] * 4

    def up_group(j):
        activated[j], slopes[j] = tiled(
            up_kernel,
            "up",
            4,
            (work.live[0], up_w[j]),
            (0, None),
            [(shape(length, hidden, dtype=bf16), 0)] * 2,
            2 * length * model * hidden,
        )
        return Box(activated[j])

    work = Box(first_low)
    tie(ring_down, work)
    ring_down.step()
    done = up_group(0)
    tie(ring_down, work, done)
    for _ in range(links.ahead - 3):
        ring_down.step()
    done = up_group(1)
    tie(ring_down, work, done, far)
    up_w[2] = far.live[0]
    up_w[3] = swap(up_w[2], 1)
    down_own, down_across = ring_down.full([(0, hidden, None), (hidden, hidden, None)], rows)
    down_w = [down_own, swap(down_own, 1), down_across, swap(down_across, 1)]
    done = [up_group(2), up_group(3)]
    result, grad_two, grad_two_low, sums_two = tiled(
        down_kernel,
        "down",
        4,
        (*activated, *down_w, vectors, unit_one, cotangent),
        (0,) * 4 + (None,) * 5 + (0,) * 2,
        [
            (shape(length, model, dtype=bf16), 0),
            (shape(length, model), 0),
            (shape(length, model, dtype=bf16), 0),
            (shape(SIDE, model), None),
        ],
        8 * length * model * hidden,
    )
    work = Box(grad_two_low)

    def blocks(value):
        return value.reshape(dp, -1, value.shape[-1])

    def grad_down(j):
        return contract(work.live[0], activated[j], ((0,), (0,)), bf16)

    sent = Box(grad_down(3), grad_down(1))
    tie(work, sent)
    three, one = (swap(v, 1) for v in sent.live)
    pair = Box(grad_down(2), grad_down(0), three, one)
    tie(work, pair)
    two, zero, three, one = (blocks(v) for v in pair.live)
    sums_down = ScatterRing(links, [[zero, one], [two, three]])
    grad_up, grad_bias_up = [None] * 4, [None] * 4

    def back_up(j):
        grad_up[j], grad_bias_up[j] = tiled(
            slope_kernel,
            "back_up",
            4,
            (work.live[0], down_w[j], slopes[j]),
            (0, None, 0),
            [(shape(length, hidden, dtype=bf16), 0), (shape(SIDE, hidden), None)],
            2 * length * model * hidden,
        )
        return Box(grad_up[j])

    for j in (3, 1, 2, 0):
        sums_down.step()
        done = back_up(j)
        tie(work, done, sums_down)
    for _ in range(links.ahead - 4):
        sums_down.step()

    def grad_w_up(j):
        return contract(work.live[0], grad_up[j], ((0,), (0,)), bf16)

    end_down = Box(swap(sums_down.total[:, hidden:].astype(bf16), 2))
    work = Box(first_low)
    sent = Box(grad_w_up(3), grad_w_up(1))
    tie(work, sent, end_down)
    three, one = (swap(v, 1) for v in sent.live)
    two, zero = grad_w_up(2), grad_w_up(0)
    across = (two.astype(f32) + three.astype(f32)).astype(bf16)
    pair = Box(zero, one, across, grad_up[0])
    tie(work, pair)
    zero_up, one_up, across, grad_up[0] = pair.live
    half = model // 2
    far_low = Box(swap(across[:half], 2))
    grad_one, grad_one_low, sums = tiled(
        first_kernel,
        "back_first",
        4,
        (*grad_up, *up_w, vectors, grad_two, unit_one, scale_one, sums_two),
        (0,) * 4 + (None,) * 5 + (0,) * 3 + (None,),
        [
            (shape(length, model), 0),
            (shape(length, model, dtype=bf16), 0),
            (shape(SIDE, model), None),
        ],
        8 * length * model * hidden,
    )
    work = Box(grad_one_low)
    far_high = Box(across[half:])
    tie(work, far_low, far_high)
    far_high.live = [swap(far_high.live[0], 2)]
    grad_qkv = [None] * 4

    def back_group(j, arrived=None):
        grad_qkv[j] = attend_back(qkv[j], mixture[j], logs[j], out_w[j], work.live[0], window, span)
        return grad_weight(
            dp, tokens, grad_qkv[j], work.live[0], mixture[j], grad_bias_up[j], sums, arrived
        )

    three = Box(back_group(3))
    tie(work, three, far_high)
    far_up = jnp.concatenate(far_low.live + far_high.live)
    sums_up = ScatterRing(links, [[blocks(zero_up), blocks(one_up), blocks(far_up)]])
    recv = swap(three.live[0], 1)
    sums_up.step()
    two = Box(back_group(2, recv))
    tie(work, two, sums_up)
    split = dp // 2
    far_low = Box(swap(two.live[0][:split], 2))
    sums_up.step()
    one = Box(back_group(1))
    far_high = Box(two.live[0][split:])
    tie(work, one, sums_up, far_low, far_high)
    far_high.live = [swap(far_high.live[0], 2)]
    recv = swap(one.live[0], 1)
    sums_up.step()
    zero = Box(back_group(0, recv))
    tie(work, zero, sums_up, far_high)
    far_attn = jnp.concatenate(far_low.live + far_high.live)
    sums_attn = ScatterRing(links, [[zero.live[0], far_attn]])
    grad_input = grad_one
    for j in range(tensor):
        sums_attn.step()
        if sums_up.count < links.ahead:
            sums_up.step()
        grad_input = grad_input + contract(grad_qkv[j], attn_w[j][:model], ((0,), (1,)))
        holder = Box(grad_input)
        tie(holder, sums_attn, sums_up)
        grad_input = holder.live[0]
    for ring in (sums_attn, sums_up):
        while ring.count < links.ahead:
            ring.step()
    grad_attn = sums_attn.total
    grad_down_own = sums_down.total[:, :hidden] + end_down.live[0].astype(f32)

    side = grad_attn[rows:]
    outs = []
    for row, at, (count, per) in (
        (0, 0, b_query.shape),
        (0, 2 * group, b_value.shape),
        (1, 0, b_up.shape),
    ):
        held = side[row, at : at + count * per * dp].reshape(count, per * dp)
        outs.append(lax.dynamic_slice_in_dim(held, me * per, per, axis=1))
    own = (me * tensor + mine) * share
    held = lax.dynamic_slice_in_dim(side[TAIL - 8 : TAIL - 2], own, share, axis=1)
    grad_attn = grad_attn[:rows]
    return (
        result,
        grad_input.astype(bf16),
        grad_attn[:, :group],
        grad_attn[:, group : 2 * group],
        grad_attn[:, 2 * group : 3 * group],
        grad_attn[:, 3 * group :].T,
        sums_up.total,
        grad_down_own.T,
        *outs,
        *[held[i] for i in range(6)],
    )


def solution(mesh):
    both = P(("dp", "tensor"))
    rows = P(("dp", "tensor"), None)
    down = P("tensor", "dp")
    wide = P("dp", "tensor")
    weights = (wide, wide, wide, down, wide, down, down, down, down)
    return jax.shard_map(
        per_device,
        mesh=mesh,
        in_specs=(rows, P("dp", None)) + weights + (both,) * 6 + (rows,),
        out_specs=(rows, rows) + weights + (both,) * 6,
        check_vma=False,
    )
```

```python
import functools

import jax
import jax.numpy as jnp
import numpy as np
from jax import lax
from jax.experimental import pallas as pl
from jax.experimental.pallas import tpu as pltpu
from jax.sharding import PartitionSpec as P

HD = 64
BLOCK = 256
EXTRA = 16
STEP = 128
SIDE = 8
RING_ROOM = 2 << 20
ATTEND_ROOM = 12 << 20
TILE_ROOM = 8 << 20
TAIL = 16

epsilon = 1e-06
root_half = 0.7071067811865476
inv_root_tau = 0.3989422804014327
masked_value = -1e30
bf16 = jnp.bfloat16
f32 = jnp.float32


def contract(a, b, dims, out=f32):
    return lax.dot_general(a, b, (dims, ((), ())), preferred_element_type=f32).astype(out)


def ring_order(size):
    return list(range(0, size, 2)) + list(range(size - 1, 0, -2)) if size > 1 else [0]


class Links:
    def __init__(self, dp, tensor):
        self.dp, self.tensor = dp, tensor
        order = ring_order(dp)
        self.order = jnp.array(order, jnp.int32)
        place = [0] * dp
        for position, member in enumerate(order):
            place[member] = position
        self.forward = [(order[i], order[(i + 1) % dp]) for i in range(dp)]
        self.backward = [(b, a) for a, b in self.forward]
        self.me = lax.axis_index("dp")
        self.position = jnp.array(place, jnp.int32)[self.me]
        self.ahead = dp // 2
        self.behind = dp - 1 - self.ahead
        offsets = jnp.arange(-self.ahead, self.behind + 1, dtype=jnp.int32)
        self.members = self.order[(self.position + offsets + dp) % dp]

    def swap(self, value, mask):
        return lax.ppermute(value, "tensor", [(i, i ^ mask) for i in range(self.tensor)])


def tie(*holders):
    flat, tree = jax.tree.flatten([holder.live for holder in holders])
    flat = lax.optimization_barrier(tuple(flat))
    for holder, live in zip(holders, jax.tree.unflatten(tree, flat)):
        holder.live = live


class Box:
    def __init__(self, *live):
        self.live = list(live)


class GatherRing:
    def __init__(self, links, value):
        self.links = links
        self.live = [value, value]
        self.pieces = {0: value}
        self.count = 0

    def step(self):
        links = self.links
        self.count += 1
        up, down = self.live
        up = lax.ppermute(up, "dp", links.forward)
        self.pieces[-self.count] = up
        if self.count <= links.behind:
            down = lax.ppermute(down, "dp", links.backward)
            self.pieces[self.count] = down
        self.live = [up, down]

    def full(self, plan, rows):
        links = self.links
        pieces = [self.pieces[offset] for offset in range(-links.ahead, links.behind + 1)]
        pieces[0] = self.live[0]
        return assemble(links.members, pieces, plan, rows)


class ScatterRing:
    def __init__(self, links, groups):
        self.links = links
        self.groups = groups
        self.count = 0
        self.live = ring_call(links, groups, (links.ahead, -links.ahead), (), bf16, first=True)

    def step(self):
        links = self.links
        self.count += 1
        up, down = self.live
        up = lax.ppermute(up, "dp", links.forward)
        down = lax.ppermute(down, "dp", links.backward)
        left = links.ahead - self.count
        if left:
            up, down = ring_call(links, self.groups, (left, -left), (up, down), bf16)
        self.live = [up, down]

    def total(self):
        (made,) = ring_call(self.links, self.groups, (0,), self.live, f32)
        return made


VMEM = pl.BlockSpec(memory_space=pltpu.VMEM)
SMEM = pl.BlockSpec(memory_space=pltpu.SMEM)


def block_of(sources, member):
    if len(sources) == 1:
        return sources[0][member].astype(f32)
    low, high = sources
    half = low.shape[0]
    lower = low[jnp.minimum(member, half - 1)].astype(f32)
    return jnp.where(member < half, lower, high[jnp.maximum(member - half, 0)].astype(f32))


def ring_sums(members_ref, refs, counts, place):
    member = members_ref[place]
    at = 0
    for count in counts:
        total = None
        for pieces in count:
            made = block_of(refs[at : at + pieces], member)
            total = made if total is None else total + made
            at += pieces
        yield total


def ring_kernel(members_ref, *refs, counts, places, dtype, first):
    size, sends = sum(map(sum, counts)), len(places)
    sources, arrived, outs = refs[:size], refs[size:-sends], refs[-sends:]
    for index, place in enumerate(places):
        column = 0
        out = outs[index]
        mine = arrived if sends == 1 else arrived[index : index + 1]
        for made in ring_sums(members_ref, sources, counts, place):
            rows, width = made.shape
            own = slice(column, column + width)
            column += width
            if first:
                half = out.shape[0]
                out[:, own] = (made[:half] if index == 0 else made[rows - half :]).astype(dtype)
                continue
            whole = [one for one in mine if one.shape[0] == rows]
            for one in whole:
                made = made + one[:, own].astype(f32)
            out[:, own] = made.astype(dtype)
            for one in mine:
                if one.shape[0] < rows:
                    half = one.shape[0]
                    part = slice(0, half) if index == 0 else slice(rows - half, rows)
                    out[part, own] = (made[part] + one[:, own].astype(f32)).astype(dtype)


def flatten(groups):
    sources, counts = [], []
    for group in groups:
        pieces = [one if isinstance(one, (list, tuple)) else [one] for one in group]
        counts.append([len(one) for one in pieces])
        sources += [part for one in pieces for part in one]
    widths = [(group[0][0] if isinstance(group[0], (list, tuple)) else group[0]).shape for group in groups]
    return sources, counts, widths[0][1], sum(width[2] for width in widths)


def ring_call(links, groups, offsets, arrived, dtype, first=False):
    sources, counts, rows, columns = flatten(groups)
    size = rows * columns
    return list(
        pl.pallas_call(
            functools.partial(
                ring_kernel,
                counts=counts,
                places=[(offset + links.ahead) % links.dp for offset in offsets],
                dtype=dtype,
                first=first,
            ),
            out_shape=[
                jax.ShapeDtypeStruct((rows // 2 if first else rows, columns), dtype) for _ in offsets
            ],
            in_specs=[SMEM] + [VMEM] * (len(sources) + len(arrived)),
            out_specs=[VMEM] * len(offsets),
            compiler_params=pltpu.CompilerParams(vmem_limit_bytes=RING_ROOM),
            cost_estimate=pl.CostEstimate(
                flops=size * 2, bytes_accessed=6 * size * len(offsets), transcendentals=0
            ),
            name="ring_sum",
        )(links.members, *sources, *arrived)
    )


def finish_kernel(
    members_ref, me_ref, *refs, counts, place, tables
):
    size = sum(map(sum, counts))
    sources, arrived, outs = refs[:size], refs[size : size + 2], refs[size + 2 :]
    (total,) = ring_sums(members_ref, sources, counts, place)
    for one in arrived:
        total = total + one[...].astype(f32)
    rows, group = outs[0].shape
    for index in range(3):
        outs[index][...] = total[:rows, index * group : (index + 1) * group]
    outs[3][...] = total[:rows, 3 * group :].T
    side = total[rows:]
    wide = side.shape[1]
    for out, (line, at, per, full) in zip(outs[4:7], tables):
        turned = pltpu.roll(side, wide - me_ref[0] * per, axis=1)
        for row in range(out.shape[0]):
            start = at + row * full
            out[row : row + 1, :] = turned[line : line + 1, start : start + per]
    share = outs[7].shape[1]
    turned = pltpu.roll(side, wide - me_ref[1] * share, axis=1)
    outs[7][...] = turned[TAIL - 8 :, 0:share]


def finish(links, ring, places, shapes, tables):
    sources, counts, _, _ = flatten(ring.groups)
    return pl.pallas_call(
        functools.partial(finish_kernel, counts=counts, place=links.ahead, tables=tables),
        out_shape=shapes,
        in_specs=[SMEM] * 2 + [VMEM] * (len(sources) + 2),
        out_specs=[VMEM] * len(shapes),
        compiler_params=pltpu.CompilerParams(vmem_limit_bytes=RING_ROOM),
        name="finish",
    )(links.members, places, *sources, *ring.live)


def assemble_kernel(members_ref, *refs, count, plan, rows):
    pieces, outs = refs[:count], refs[count:]
    sides = pieces[0].shape[0] > rows
    total = None
    for index in range(count):
        start = pl.multiple_of(members_ref[index] * rows, rows)
        for out, (at, width, _) in zip(outs, plan):
            out[pl.ds(start, rows), :] = pieces[index][0:rows, at : at + width]
        if sides:
            side = pieces[index][rows:, :].astype(f32)
            total = side if total is None else total + side
    for out, (at, width, kept) in zip(outs, plan):
        if kept == "all":
            for index in range(3):
                first = count * rows + index * SIDE
                out[first : first + SIDE, :] = total[:, index * width : (index + 1) * width].astype(bf16)
        elif kept is not None:
            out[count * rows :, :] = jnp.broadcast_to(
                total[kept : kept + 1, at : at + width], (SIDE, width)
            ).astype(bf16)


def assemble(members, pieces, plan, rows):
    count = len(pieces)
    full, wide = pieces[0].shape
    if rows % 16:
        stacked = jnp.stack(pieces)
        back = jnp.zeros((count,), jnp.int32).at[members].set(jnp.arange(count, dtype=jnp.int32))
        stacked = jnp.take(stacked, back, axis=0)
        weights = stacked[:, :rows].reshape(count * rows, -1)
        total = jnp.sum(stacked[:, rows:].astype(f32), axis=0)
        outs = []
        for at, width, kept in plan:
            out = weights[:, at : at + width]
            if kept == "all":
                parts = [total[:, i * width : (i + 1) * width].astype(bf16) for i in range(3)]
                out = jnp.concatenate([out] + parts)
            elif kept is not None:
                row = jnp.broadcast_to(total[kept : kept + 1, at : at + width], (SIDE, width))
                out = jnp.concatenate([out, row.astype(bf16)])
            outs.append(out)
        return outs
    shapes = [
        jax.ShapeDtypeStruct(
            (count * rows + SIDE * {None: 0, "all": 3}.get(kept, 1), width), bf16
        )
        for _, width, kept in plan
    ]
    return pl.pallas_call(
        functools.partial(assemble_kernel, count=count, plan=plan, rows=rows),
        out_shape=shapes,
        in_specs=[SMEM] + [VMEM] * count,
        out_specs=[VMEM] * len(shapes),
        compiler_params=pltpu.CompilerParams(vmem_limit_bytes=RING_ROOM),
        cost_estimate=pl.CostEstimate(
            flops=0, bytes_accessed=4 * count * full * wide, transcendentals=0
        ),
        name="assemble",
    )(members, *pieces)


def one_hot(first, rows, size):
    hit = lax.broadcasted_iota(jnp.int32, (rows, size), 1) == (
        lax.broadcasted_iota(jnp.int32, (rows, size), 0) + first
    )
    return jnp.where(hit, 1.0, 0.0).astype(bf16)


def placed(table, me, dp):
    count, per = table.shape
    spread = contract(table, one_hot(me * per, per, per * dp), ((1,), (0,)))
    return [spread[row : row + 1] for row in range(count)]


def only_row(row, at):
    line = lax.broadcasted_iota(jnp.int32, (SIDE, row.shape[1]), 0)
    return jnp.where(line == at, row, 0.0)


def pack_kernel(me_ref, *refs, dp):
    sources, out_ref, held, sems = refs[:5], refs[5], refs[6:11], refs[11]
    copies = [
        pltpu.make_async_copy(source, target, sems.at[index])
        for index, (source, target) in enumerate(zip(sources, held))
    ]
    for copy in copies:
        copy.start()
    for copy in copies:
        copy.wait()
    query_ref, key_ref, value_ref, b_query_ref, b_value_ref = held
    rows, group = query_ref.shape
    out_ref[0:rows, 0:group] = query_ref[...]
    out_ref[0:rows, group : 2 * group] = key_ref[...]
    out_ref[0:rows, 2 * group :] = value_ref[...]
    me = me_ref[0]
    row = jnp.concatenate(
        placed(b_query_ref[...], me, dp)
        + [jnp.zeros((1, group), f32)]
        + placed(b_value_ref[...], me, dp),
        axis=1,
    )
    out_ref[rows:, :] = only_row(row, 0).astype(bf16)


def pack_late_kernel(me_ref, w_out_ref, w_down_ref, vectors_ref, out_ref, down_ref, *, dp):
    rows, hidden = w_down_ref.shape[1], w_down_ref.shape[0]
    out_ref[...] = w_out_ref[...].T
    down_ref[0:rows, :] = w_down_ref[...].T
    left = vectors_ref[...]
    share = left.shape[1]
    place = one_hot(me_ref[0] * share, share, share * dp)
    spread = []
    for _ in range(3):
        part = left.astype(bf16)
        left = left - part.astype(f32)
        spread.append(contract(part, place, ((1,), (0,))))
    row = jnp.concatenate(spread, axis=1)
    blank = jnp.zeros((SIDE, hidden - row.shape[1]), f32)
    down_ref[rows:, :] = jnp.concatenate([row, blank], axis=1).astype(bf16)


def pack_up_kernel(
    me_ref, out_ref, far_out_ref, w_up_ref, down_ref, far_down_ref, b_up_ref, up_ref, pair_ref, *, dp
):
    rows, hidden = w_up_ref.shape
    group = out_ref.shape[1]
    up_ref[0:rows, 0:group] = out_ref[...]
    up_ref[0:rows, group : 2 * group] = far_out_ref[...]
    up_ref[0:rows, 2 * group :] = w_up_ref[...]
    pair_ref[:, 0:hidden] = down_ref[0:rows, :]
    pair_ref[:, hidden:] = far_down_ref[0:rows, :]
    near = down_ref[rows:, 0 : 3 * group].astype(f32)
    far = far_down_ref[rows:, 0 : 3 * group].astype(f32)
    bias = jnp.concatenate(
        [jnp.zeros((1, 2 * group), f32)] + placed(b_up_ref[...], me_ref[0], dp), axis=1
    )
    side = jnp.concatenate([near, far], axis=1) + only_row(bias, 6)
    up_ref[rows:, :] = side.astype(bf16)


def small_call(kernel, name, links, shapes, *operands, copied=False):
    place = pl.BlockSpec(memory_space=pltpu.HBM) if copied else VMEM
    scratch = []
    if copied:
        operands = [pltpu.with_memory_space_constraint(x, pltpu.HBM) for x in operands]
        scratch = [pltpu.VMEM(x.shape, x.dtype) for x in operands]
        scratch.append(pltpu.SemaphoreType.DMA((len(operands),)))
    return pl.pallas_call(
        functools.partial(kernel, dp=links.dp),
        out_shape=shapes,
        in_specs=[SMEM] + [place] * len(operands),
        out_specs=[VMEM] * len(shapes),
        scratch_shapes=scratch,
        compiler_params=pltpu.CompilerParams(vmem_limit_bytes=RING_ROOM),
        name=name,
    )(links.me.reshape(1), *operands)


def documents_kernel(mine_ref, lengths_ref, span_ref, window_ref, *, block):
    length = span_ref.shape[1]
    count = length // block
    place = lax.broadcasted_iota(jnp.int32, (1, length), 1)
    low = high = jnp.zeros((1, length), jnp.int32)
    begins, ends = [jnp.int32(0)] * count, [jnp.int32(0)] * count
    start = jnp.int32(0)
    for document in range(lengths_ref.shape[1]):
        end = start + lengths_ref[mine_ref[0], document]
        inside = (place >= start) & (place < end)
        low, high = jnp.where(inside, start, low), jnp.where(inside, end, high)
        for index in range(count):
            first, last = index * block, (index + 1) * block - 1
            begins[index] = jnp.where((start <= first) & (first < end), start, begins[index])
            ends[index] = jnp.where((start <= last) & (last < end), end, ends[index])
        start = end
    span_ref[0:1, :] = low
    span_ref[1:2, :] = high
    for index in range(count):
        begin = lax.div(begins[index], jnp.int32(STEP)) * STEP
        blocks = lax.div(ends[index] - begin + (block - 1), jnp.int32(block))
        window_ref[0, index] = jnp.minimum(begin, length - blocks * block)
        window_ref[1, index] = blocks


def documents(mine, lengths, length, block):
    return pl.pallas_call(
        functools.partial(documents_kernel, block=block),
        out_shape=[
            jax.ShapeDtypeStruct((2, length), jnp.int32),
            jax.ShapeDtypeStruct((2, length // block), jnp.int32),
        ],
        in_specs=[SMEM, SMEM],
        out_specs=[VMEM, SMEM],
        compiler_params=pltpu.CompilerParams(vmem_limit_bytes=RING_ROOM),
        name="documents",
    )(mine.reshape(1), lengths)


def fill_bias(bias, begin, low, high, size):
    keys = lax.broadcasted_iota(jnp.int32, (size, low.shape[1]), 0) + begin
    bias[0:size, :] = jnp.where((keys >= low) & (keys < high), 0.0, masked_value)


def attend_kernel(
    window_ref, tokens_ref, weight_ref, span_ref, out_ref, log_ref, qkv_ref, keys, values, bias, hold, *, block
):
    length = qkv_ref.shape[1]
    heads = qkv_ref.shape[0] // (3 * HD)
    width = heads * HD
    model = tokens_ref.shape[1]
    made = contract(tokens_ref[...], weight_ref[0:model, :], ((1,), (0,)))
    made = made + weight_ref[model : model + 1, :].astype(f32)
    qkv_ref[...] = made.astype(bf16).T
    tail = jnp.where(lax.broadcasted_iota(jnp.int32, (EXTRA, length), 0) == 0, 1.0, 0.0).astype(bf16)
    for head in range(heads):
        keys[head] = qkv_ref[width + head * HD : width + (head + 1) * HD, :].T
        values[head, 0:HD, :] = qkv_ref[2 * width + head * HD : 2 * width + (head + 1) * HD, :]
        values[head, HD : HD + EXTRA, :] = tail

    def one_block(index, _):
        lanes = pl.ds(pl.multiple_of(index * block, block), block)
        begin = pl.multiple_of(window_ref[0, index], STEP)

        def with_count(count):
            fill_bias(bias, begin, span_ref[0:1, lanes], span_ref[1:2, lanes], count * block)
            tops = []
            for head in range(heads):
                queries = qkv_ref[head * HD : (head + 1) * HD, lanes] * 0.125
                top = None
                for piece in range(count):
                    rows = slice(piece * block, (piece + 1) * block)
                    own = pl.ds(begin + piece * block, block)
                    scores = contract(keys[head, own, :], queries, ((1,), (0,))) + bias[rows, :]
                    hold[head, rows, :] = scores
                    most = jnp.max(scores.reshape(block // 8, 8, block), axis=0)
                    top = most if top is None else jnp.maximum(top, most)
                tops.append(jnp.max(top, axis=0, keepdims=True))
            for head in range(heads):
                total = None
                for piece in range(count):
                    rows = slice(piece * block, (piece + 1) * block)
                    own = pl.ds(begin + piece * block, block)
                    weights = jnp.exp(hold[head, rows, :] - tops[head]).astype(bf16)
                    made = contract(values[head, :, own], weights, ((1,), (0,)))
                    total = made if total is None else total + made
                mass = total[HD : HD + 1, :]
                out_ref[head * HD : (head + 1) * HD, lanes] = (total[:HD] / mass).astype(bf16)
                log_ref[head : head + 1, lanes] = tops[head] + jnp.log(mass)

        for count in range(1, length // block + 1):
            pl.when(window_ref[1, index] == count)(functools.partial(with_count, count))
        return 0

    lax.fori_loop(0, length // block, one_block, 0)


def attend_back_kernel(
    window_ref, qkv_ref, span_ref, out_ref, log_ref, weight_ref, one_ref, result_ref, keys, values, bias, grad_key, grad_value, grad_ref, *, block, half
):
    length = qkv_ref.shape[1]
    model = one_ref.shape[1]
    group = grad_ref.shape[0]
    weight = weight_ref[0:model, half * group : (half + 1) * group]
    grad_ref[...] = contract(weight, one_ref[...], ((0,), (1,)), bf16)
    heads = qkv_ref.shape[0] // (3 * HD)
    width = heads * HD
    for head in range(heads):
        keys[head] = qkv_ref[width + head * HD : width + (head + 1) * HD, :].T
        values[head] = qkv_ref[2 * width + head * HD : 2 * width + (head + 1) * HD, :].T
    grad_key[...] = jnp.zeros_like(grad_key)
    grad_value[...] = jnp.zeros_like(grad_value)

    def one_block(index, _):
        lanes = pl.ds(pl.multiple_of(index * block, block), block)
        begin = pl.multiple_of(window_ref[0, index], STEP)

        def with_count(count):
            size = count * block
            window = pl.ds(begin, size)
            fill_bias(bias, begin, span_ref[0:1, lanes], span_ref[1:2, lanes], size)
            for head in range(heads):
                own = slice(head * HD, (head + 1) * HD)
                queries = qkv_ref[own, lanes] * 0.125
                grads = grad_ref[own, lanes]
                delta = jnp.sum(
                    out_ref[own, lanes].astype(f32) * grads.astype(f32), axis=0, keepdims=True
                )
                scores = contract(keys[head, window, :], queries, ((1,), (0,))) + bias[0:size, :]
                weights = jnp.exp(scores - log_ref[head : head + 1, lanes])
                grad_prob = contract(values[head, window, :], grads, ((1,), (0,)))
                grad_scores = (weights * (grad_prob - delta)).astype(bf16)
                grad_value[own, window] += contract(grads, weights.astype(bf16), ((1,), (1,)))
                grad_key[own, window] += contract(queries, grad_scores, ((1,), (1,)))
                key_cols = qkv_ref[width + head * HD : width + (head + 1) * HD, window]
                made = contract(key_cols, grad_scores, ((1,), (0,)))
                result_ref[own, lanes] = (made * 0.125).astype(bf16)

        for count in range(1, length // block + 1):
            pl.when(window_ref[1, index] == count)(functools.partial(with_count, count))
        return 0

    lax.fori_loop(0, length // block, one_block, 0)
    result_ref[width : 2 * width, :] = grad_key[...].astype(bf16)
    result_ref[2 * width :, :] = grad_value[...].astype(bf16)


def attend(tokens, weight, window, span):
    length, model = tokens.shape
    width = weight.shape[1]
    heads = width // (3 * HD)
    return pl.pallas_call(
        functools.partial(attend_kernel, block=BLOCK),
        out_shape=(
            jax.ShapeDtypeStruct((heads * HD, length), bf16),
            jax.ShapeDtypeStruct((8, length), f32),
            jax.ShapeDtypeStruct((width, length), bf16),
        ),
        in_specs=[SMEM] + [VMEM] * 3,
        out_specs=(VMEM,) * 3,
        scratch_shapes=[
            pltpu.VMEM((heads, length, HD), bf16),
            pltpu.VMEM((heads, HD + EXTRA, length), bf16),
            pltpu.VMEM((length, BLOCK), f32),
            pltpu.VMEM((heads, length, BLOCK), f32),
        ],
        compiler_params=pltpu.CompilerParams(vmem_limit_bytes=ATTEND_ROOM),
        cost_estimate=pl.CostEstimate(
            flops=4 * heads * length * length * HD + 2 * length * model * width,
            bytes_accessed=4 * width * length,
            transcendentals=heads * length * length,
        ),
        name="attend",
    )(window, tokens, weight, span)


def attend_back(qkv, out, logs, weight, half, one, window, span):
    width, length = qkv.shape
    heads = width // (3 * HD)
    return pl.pallas_call(
        functools.partial(attend_back_kernel, block=BLOCK, half=half),
        out_shape=jax.ShapeDtypeStruct((width, length), bf16),
        in_specs=[SMEM] + [VMEM] * 6,
        out_specs=VMEM,
        scratch_shapes=[
            pltpu.VMEM((heads, length, HD), bf16),
            pltpu.VMEM((heads, length, HD), bf16),
            pltpu.VMEM((length, BLOCK), f32),
            pltpu.VMEM((heads * HD, length), f32),
            pltpu.VMEM((heads * HD, length), f32),
            pltpu.VMEM((heads * HD, length), bf16),
        ],
        compiler_params=pltpu.CompilerParams(vmem_limit_bytes=ATTEND_ROOM),
        cost_estimate=pl.CostEstimate(
            flops=10 * heads * length * length * HD,
            bytes_accessed=6 * width * length,
            transcendentals=heads * length * length,
        ),
        name="attend_back",
    )(window, qkv, span, out, logs, weight, one)


def grad_weight_kernel(tokens_ref, grad_ref, one_ref, mixture_ref, *refs):
    more, out_ref = refs[2:-1], refs[-1]
    up_ref, vectors_ref = refs[0], refs[1]
    dp, full, columns = out_ref.shape
    rows = full - TAIL
    wide = grad_ref.shape[0]
    group = wide // 3
    made = contract(tokens_ref[...], grad_ref[...], ((0,), (1,)))
    out_low = contract(one_ref[...], mixture_ref[...], ((0,), (1,)))
    ones = jnp.ones((TAIL, grad_ref.shape[1]), bf16)
    lane = contract(ones, grad_ref[...], ((1,), (1,)))
    line = lax.broadcasted_iota(jnp.int32, (TAIL, columns), 0)
    bias_row = jnp.concatenate([lane, jnp.zeros((TAIL, columns - wide), f32)], axis=1)
    side = jnp.where(line == 0, bias_row, 0.0) + jnp.where(line == 1, up_ref[0:1, :], 0.0)
    lower = jnp.concatenate([jnp.zeros((TAIL - 8, columns), f32), vectors_ref[...]], axis=0)
    side = side + lower
    for index in range(dp):
        own = slice(index * rows, (index + 1) * rows)
        left, right, low = made[own], out_low[own], side
        for number, held in enumerate(more):
            half = held.shape[0]
            if half < dp and index // half != number + 2 - len(more):
                continue
            left = left + held[index % half, 0:rows, 0:wide].astype(f32)
            right = right + held[index % half, 0:rows, wide:].astype(f32)
            low = low + held[index % half, rows:, :].astype(f32)
        out_ref[index, 0:rows, 0:wide] = left.astype(bf16)
        out_ref[index, 0:rows, wide:] = right.astype(bf16)
        out_ref[index, rows:, :] = low.astype(bf16)


def grad_weight(dp, tokens, grad, one, mixture, up_row, vectors, more):
    length, model = tokens.shape
    wide, group = grad.shape[0], mixture.shape[0]
    return pl.pallas_call(
        grad_weight_kernel,
        out_shape=jax.ShapeDtypeStruct((dp, model // dp + TAIL, wide + group), bf16),
        in_specs=[VMEM] * (6 + len(more)),
        out_specs=VMEM,
        compiler_params=pltpu.CompilerParams(vmem_limit_bytes=ATTEND_ROOM),
        cost_estimate=pl.CostEstimate(
            flops=2 * length * model * (wide + group),
            bytes_accessed=2 * (length + model) * (wide + group + model),
            transcendentals=0,
        ),
        name="grad_weight",
    )(tokens, grad, one, mixture, up_row, vectors, *more)


def normalize(values):
    average = jnp.mean(values, axis=-1, keepdims=True)
    centred = values - average
    variance = jnp.mean(centred * centred, axis=-1, keepdims=True)
    inv_scale = lax.rsqrt(variance + epsilon)
    return centred * inv_scale, inv_scale


def normalize_back(grad_out, unit_rows, inv_scale, norm_gain):
    grad_unit = grad_out * norm_gain
    middle = grad_unit - jnp.mean(grad_unit, axis=-1, keepdims=True)
    middle = middle - unit_rows * jnp.mean(grad_unit * unit_rows, axis=-1, keepdims=True)
    return inv_scale * middle


def gelu_parts(up_pre):
    normal_cdf = 0.5 * (1.0 + lax.erf(up_pre * root_half))
    return (
        up_pre * normal_cdf,
        normal_cdf + up_pre * inv_root_tau * jnp.exp(-0.5 * up_pre * up_pre),
    )


def tile_kernel(*refs, kernel, steps, tiles):
    def step(index, _):
        views = []
        for ref, tile in zip(refs, tiles):
            if tile is None or steps == 1:
                views.append(ref)
                continue
            size = ref.shape[tile] // steps
            own = pl.ds(pl.multiple_of(index * size, size), size)
            views.append(ref.at[own, :] if tile == 0 else ref.at[:, own])
        kernel(index, *views)
        return 0

    lax.fori_loop(0, steps, step, 0)


def tiled(kernel, name, steps, operands, tiles, shapes, flops):
    shapes, out_tiles = [x for x, _ in shapes], [x for _, x in shapes]
    moved = sum(x.size * x.dtype.itemsize for x in list(operands) + shapes)
    return pl.pallas_call(
        functools.partial(
            tile_kernel, kernel=kernel, steps=steps, tiles=tuple(tiles) + tuple(out_tiles)
        ),
        out_shape=shapes,
        in_specs=[VMEM] * len(operands),
        out_specs=[VMEM] * len(shapes),
        compiler_params=pltpu.CompilerParams(vmem_limit_bytes=TILE_ROOM),
        cost_estimate=pl.CostEstimate(flops=flops, bytes_accessed=moved, transcendentals=0),
        name=name,
    )(*operands)


def shape(*size, dtype=f32):
    return jax.ShapeDtypeStruct(size, dtype)


def vectors_kernel(step, lane_ref, near_ref, far_ref, out_ref):
    model = out_ref.shape[1]
    wide = near_ref.shape[1]
    size = wide // 2
    total = jnp.zeros((SIDE, model), f32)
    lanes = lax.broadcasted_iota(jnp.int32, (size, model), 1)
    for j in range(4):
        held = near_ref if j % 2 == 0 else far_ref
        first = (j // 2) * 3 * size
        place = jnp.where(lanes == lane_ref[:, j : j + 1], 1.0, 0.0).astype(bf16)
        for part in range(3):
            at = first + part * size
            line = model + at // wide * SIDE
            part = held[line : line + SIDE, at % wide : at % wide + size]
            total = total + contract(part, place, ((1,), (0,)))
    out_ref[...] = total


def out_kernel(step, m0, m1, m2, m3, near, far, vectors, tokens, low_ref, unit_ref, scale_ref):
    total = vectors[0:1, :] + tokens[...].astype(f32)
    model, group = total.shape[1], m0.shape[0]
    for index, mixture in enumerate((m0, m1, m2, m3)):
        held = near if index % 2 == 0 else far
        weight = held[0:model, index // 2 * group : (index // 2 + 1) * group]
        total = total + contract(mixture[...], weight, ((0,), (1,)))
    unit, scale = normalize(total)
    unit_ref[...] = unit
    scale_ref[...] = scale
    low_ref[...] = (unit * vectors[2:3, :] + vectors[3:4, :]).astype(bf16)


def up_kernel(step, low, weight, act_ref, slope_ref):
    model = low.shape[1]
    up_pre = contract(low[...], weight[0:model, :], ((1,), (0,)))
    act, slope = gelu_parts(up_pre + weight[model : model + 1, :].astype(f32))
    act_ref[...] = act.astype(bf16)
    slope_ref[...] = slope.astype(bf16)


def column_sums(step, ref, rows, start=0.0):
    line = lax.broadcasted_iota(jnp.int32, ref.shape, 0)
    made = jnp.zeros(ref.shape, f32)
    for at, values in rows:
        made = made + jnp.where(line == at, jnp.sum(values, axis=0, keepdims=True), 0.0)

    @pl.when(step == 0)
    def _():
        ref[...] = made + start

    @pl.when(step > 0)
    def _():
        ref[...] += made


def down_kernel(
    step, a0, a1, a2, a3, w0, w1, w2, w3, vectors, unit_ref, cotangent, result_ref, grad_ref, low_ref, sums_ref
):
    total = vectors[1:2, :] + unit_ref[...] * vectors[2:3, :] + vectors[3:4, :]
    for act, weight in ((a0, w0), (a1, w1), (a2, w2), (a3, w3)):
        total = total + contract(act[...], weight[...], ((1,), (1,)))
    unit, scale = normalize(total)
    result_ref[...] = (unit * vectors[4:5, :] + vectors[5:6, :]).astype(bf16)
    grad_out = cotangent[...].astype(f32)
    grad = normalize_back(grad_out, unit, scale, vectors[4:5, :])
    grad_ref[...] = grad
    low_ref[...] = grad.astype(bf16)
    column_sums(step, sums_ref, ((1, grad), (4, grad_out * unit), (5, grad_out)))


def slope_kernel(step, low, weight, slope, grad_ref, sums_ref):
    made = contract(low[...], weight[...], ((1,), (0,))) * slope[...].astype(f32)
    made = made.astype(bf16)
    grad_ref[...] = made
    column_sums(step, sums_ref, ((0, made.astype(f32)),))


def first_kernel(
    step, g0, g1, g2, g3, w0, w1, w2, w3, vectors, two, unit_ref, scale, sums_two, grad_ref, low_ref, sums_ref
):
    total = two[...]
    model = total.shape[1]
    for grad, weight in ((g0, w0), (g1, w1), (g2, w2), (g3, w3)):
        total = total + contract(grad[...], weight[0:model, :], ((1,), (1,)))
    unit = unit_ref[...]
    grad = normalize_back(total, unit, scale[...], vectors[2:3, :])
    grad_ref[...] = grad
    low_ref[...] = grad.astype(bf16)
    column_sums(step, sums_ref, ((0, grad), (2, total * unit), (3, total)), sums_two[...])


def per_device(
    tokens,
    doc_lengths,
    w_query,
    w_key,
    w_value,
    w_out,
    w_up,
    w_down,
    b_query,
    b_value,
    b_up,
    b_out,
    b_down,
    gain_one,
    shift_one,
    gain_two,
    shift_two,
    cotangent,
):
    dp, tensor = lax.axis_size("dp"), lax.axis_size("tensor")
    length, model = tokens.shape
    rows = model // dp
    group = w_query.shape[1]
    links = Links(dp, tensor)
    swap = links.swap

    share = b_out.shape[0]
    me = links.me
    mine = lax.axis_index("tensor")
    hidden = w_up.shape[1]
    (packed,) = small_call(
        pack_kernel,
        "pack",
        links,
        [shape(rows + SIDE, 3 * group, dtype=bf16)],
        w_query,
        w_key,
        w_value,
        b_query,
        b_value,
        copied=True,
    )
    ring_attn = GatherRing(links, packed)
    zero = jnp.zeros((share,), f32)
    vectors = jnp.stack([b_out, b_down, gain_one, shift_one, gain_two, shift_two, zero, zero])

    ring_attn.step()
    late_out, late_down = small_call(
        pack_late_kernel,
        "pack_late",
        links,
        [shape(rows, group, dtype=bf16), shape(rows + SIDE, hidden, dtype=bf16)],
        w_out,
        w_down,
        vectors,
    )
    late = Box(late_out, late_down, doc_lengths)
    tie(ring_attn, late)
    late_out, late_down, early_lengths = late.live
    ring_attn.step()
    far_late = Box(swap(late_out, 2), swap(late_down, 2))
    span, window = documents(mine, early_lengths, length, BLOCK)
    done = Box(span)
    tie(ring_attn, done)
    span = done.live[0]
    ring_attn.step()
    tie(ring_attn, far_late)
    up_chunk, down_chunk = small_call(
        pack_up_kernel,
        "pack_up",
        links,
        [
            shape(rows + SIDE, 2 * group + hidden, dtype=bf16),
            shape(rows, 2 * hidden, dtype=bf16),
        ],
        late_out,
        far_late.live[0],
        w_up,
        late_down,
        far_late.live[1],
        b_up,
    )
    ring_up = GatherRing(links, up_chunk)
    ring_down = GatherRing(links, down_chunk)
    for _ in range(links.ahead - 3):
        ring_attn.step()
    (attn_own,) = ring_attn.full([(0, 3 * group, 0)], rows)

    attn_w = [attn_own, None, None, None]
    qkv, mixture, logs = [None] * 4, [None] * 4, [None] * 4

    def attend_group(j):
        mixture[j], logs[j], qkv[j] = attend(work.live[0], attn_w[j], window, span)
        return Box(mixture[j])

    work = Box(tokens, attn_own)
    tie(ring_attn, ring_up, work)
    attn_w[0] = work.live[1]
    work = Box(work.live[0])
    far = Box(swap(attn_w[0], 2))
    attn_w[1] = swap(attn_w[0], 1)
    ring_up.step()
    done = attend_group(0)
    tie(ring_up, work, done)
    ring_up.step()
    done = attend_group(1)
    tie(ring_up, work, done)
    ring_up.step()
    tie(ring_up, work, far)
    attn_w[2] = far.live[0]
    attn_w[3] = swap(attn_w[2], 1)
    for _ in range(links.ahead - 3):
        ring_up.step()
    done = attend_group(2)
    tie(ring_up, work, done, ring_down)
    ring_down.step()
    out_near, up_own = ring_up.full([(0, 2 * group, "all"), (2 * group, hidden, 6)], rows)
    out_far = swap(out_near, 1)
    cuts = [0, model // 3, 2 * model // 3, up_own.shape[0]]
    held, across_up = Box(up_own), []

    def up_across():
        low, high = cuts[len(across_up) : len(across_up) + 2]
        across_up.append(Box(swap(held.live[0][low:high], 2)))
        return across_up[-1]

    moved = up_across()
    done = attend_group(3)
    tie(ring_down, work, done, held, moved)

    ring_down.step()
    moved = up_across()
    count = np.arange(dp * share)
    base = jnp.asarray((count // share * tensor * share + count % share)[:, None], jnp.int32)
    lanes = base + (mine ^ jnp.arange(4, dtype=jnp.int32))[None, :] * share
    (vectors,) = tiled(
        vectors_kernel,
        "vectors",
        1,
        (lanes, out_near, out_far),
        (None,) * 3,
        [(shape(SIDE, model), None)],
        0,
    )
    up_w = [up_own, None, None, None]
    first_low, unit_one, scale_one = tiled(
        out_kernel,
        "attention_out",
        4,
        (*mixture, out_near, out_far, vectors, work.live[0]),
        (1,) * 4 + (None,) * 3 + (0,),
        [(shape(length, model, dtype=bf16), 0), (shape(length, model), 0), (shape(length, 1), 0)],
        2 * length * model * model,
    )
    activated, slopes = [None] * 4, [None] * 4

    def up_group(j):
        activated[j], slopes[j] = tiled(
            up_kernel,
            "up",
            4,
            (work.live[0], up_w[j]),
            (0, None),
            [(shape(length, hidden, dtype=bf16), 0)] * 2,
            2 * length * model * hidden,
        )
        return Box(activated[j])

    work = Box(first_low)
    tie(ring_down, work, held, moved)
    up_w[0] = held.live[0]
    moved = up_across()
    up_w[1] = swap(up_w[0], 1)
    ring_down.step()
    done = up_group(0)
    tie(ring_down, work, done, moved)
    for _ in range(links.ahead - 3):
        ring_down.step()
    up_w[2] = jnp.concatenate([box.live[0] for box in across_up])
    up_w[3] = swap(up_w[2], 1)
    done = up_group(1)
    tie(ring_down, work, done)
    down_own, down_across = ring_down.full([(0, hidden, None), (hidden, hidden, None)], rows)
    down_w = [down_own, swap(down_own, 1), down_across, swap(down_across, 1)]
    done = [up_group(2), up_group(3)]
    result, grad_two, grad_two_low, sums_two = tiled(
        down_kernel,
        "down",
        4,
        (*activated, *down_w, vectors, unit_one, cotangent),
        (0,) * 4 + (None,) * 5 + (0,) * 2,
        [
            (shape(length, model, dtype=bf16), 0),
            (shape(length, model), 0),
            (shape(length, model, dtype=bf16), 0),
            (shape(SIDE, model), None),
        ],
        8 * length * model * hidden,
    )
    work = Box(grad_two_low)

    def blocks(value):
        return value.reshape(-1, rows, value.shape[-1])

    def grad_down(j):
        return contract(work.live[0], activated[j], ((0,), (0,)), bf16)

    sent = Box(grad_down(3), grad_down(1))
    tie(work, sent)
    three, one = (swap(v, 1) for v in sent.live)
    pair = Box(grad_down(2), grad_down(0), three, one)
    tie(work, pair)
    two, zero, three, one = (blocks(v) for v in pair.live)
    sums_down = ScatterRing(links, [[zero, one], [two, three]])
    grad_up, grad_bias_up = [None] * 4, [None] * 4

    def back_up(j):
        grad_up[j], grad_bias_up[j] = tiled(
            slope_kernel,
            "back_up",
            4,
            (work.live[0], down_w[j], slopes[j]),
            (0, None, 0),
            [(shape(length, hidden, dtype=bf16), 0), (shape(SIDE, hidden), None)],
            2 * length * model * hidden,
        )
        return Box(grad_up[j])

    def grad_w_up(j):
        return contract(work.live[0], grad_up[j], ((0,), (0,)), bf16)

    sums_down.step()
    done = Box(*[back_up(j).live[0] for j in (3, 1, 2, 0)])
    tie(work, done, sums_down)
    for j, made in zip((3, 1, 2, 0), done.live):
        grad_up[j] = made
    work = Box(first_low)
    sums_down.step()
    three = Box(swap(grad_w_up(3), 1))
    one_up, two, zero_up = grad_w_up(1), grad_w_up(2), grad_w_up(0)
    kept = Box(one_up, two, zero_up)
    tie(work, three, kept, sums_down)
    one_up, two, zero_up = kept.live
    across = (two.astype(f32) + three.live[0].astype(f32)).astype(bf16)
    half = model // 2
    far_low, far_high = Box(swap(across[:half], 2)), Box(across[half:])
    one_up = Box(swap(one_up, 1))
    sums_down.step()
    grad_one, grad_one_low, sums = tiled(
        first_kernel,
        "back_first",
        4,
        (*grad_up, *up_w, vectors, grad_two, unit_one, scale_one, sums_two),
        (0,) * 4 + (None,) * 5 + (0,) * 3 + (None,),
        [
            (shape(length, model), 0),
            (shape(length, model, dtype=bf16), 0),
            (shape(SIDE, model), None),
        ],
        8 * length * model * hidden,
    )
    work = Box(grad_one_low)
    tie(work, one_up, sums_down, far_low)
    far_high.live = [swap(far_high.live[0], 2)]
    for _ in range(links.ahead - 3):
        sums_down.step()
    grad_qkv = [None] * 4

    def back_attention(j):
        grad_qkv[j] = attend_back(
            qkv[j],
            mixture[j],
            logs[j],
            out_near if j % 2 == 0 else out_far,
            j // 2,
            work.live[0],
            window,
            span,
        )
        return Box(grad_qkv[j])

    def back_group(j, *arrived):
        return grad_weight(
            dp, tokens, grad_qkv[j], work.live[0], mixture[j], grad_bias_up[j], sums, arrived
        )

    done = back_attention(3)
    tie(work, done, far_high, sums_down)
    grad_qkv[3] = done.live[0]
    pieces = [[blocks(far_low.live[0]), blocks(far_high.live[0])]]
    sums_up = ScatterRing(links, [[blocks(zero_up), blocks(one_up.live[0])] + pieces])
    sums_up.step()
    down_total = sums_down.total()
    end_down = Box(swap(down_total[:, hidden:].astype(bf16), 2))
    three = Box(back_group(3))
    tie(work, three, sums_up)
    recv = Box(swap(three.live[0], 1))
    sums_up.step()
    done = back_attention(2)
    tie(work, done, recv, sums_up, end_down)
    grad_qkv[2] = done.live[0]
    sums_up.step()
    two = Box(back_group(2, recv.live[0]))
    tie(work, two, sums_up)
    split = dp // 2
    far_low = Box(swap(two.live[0][:split], 2))
    far_high = Box(two.live[0][split:])
    for _ in range(links.ahead - 3):
        sums_up.step()
    done = back_attention(1)
    tie(work, done, sums_up, far_low)
    grad_qkv[1] = done.live[0]
    far_high.live = [swap(far_high.live[0], 2)]
    one = Box(back_group(1))
    tie(work, one)
    recv = Box(swap(one.live[0], 1))
    done = back_attention(0)
    tie(work, done, recv, far_high)
    grad_qkv[0] = done.live[0]
    zero = Box(back_group(0, recv.live[0], far_low.live[0], far_high.live[0]), grad_qkv)
    tie(work, zero)
    sums_attn = ScatterRing(links, [[zero.live[0]]])
    grad_qkv = zero.live[1]
    grad_input = grad_one
    for j in range(tensor):
        sums_attn.step()
        grad_input = grad_input + contract(grad_qkv[j], attn_w[j][:model], ((0,), (1,)))
        holder = Box(grad_input)
        tie(holder, sums_attn)
        grad_input = holder.live[0]
    while sums_attn.count < links.ahead:
        sums_attn.step()
    grad_down_own = down_total[:, :hidden] + end_down.live[0].astype(f32)
    full = dp * b_query.shape[1]
    full_up = dp * b_up.shape[1]
    *made, held = finish(
        links,
        sums_attn,
        jnp.stack([me, me * tensor + mine]),
        [shape(rows, group)] * 3
        + [shape(group, rows)]
        + [shape(*table.shape) for table in (b_query, b_value, b_up)]
        + [shape(SIDE, share)],
        (
            (0, 0, b_query.shape[1], full),
            (0, 2 * group, b_value.shape[1], full),
            (1, 0, b_up.shape[1], full_up),
        ),
    )
    return (
        result,
        grad_input.astype(bf16),
        *made[:4],
        sums_up.total(),
        grad_down_own.T,
        *made[4:],
        *[held[i] for i in range(6)],
    )


def solution(mesh):
    both = P(("dp", "tensor"))
    rows = P(("dp", "tensor"), None)
    down = P("tensor", "dp")
    wide = P("dp", "tensor")
    weights = (wide, wide, wide, down, wide, down, down, down, down)
    return jax.shard_map(
        per_device,
        mesh=mesh,
        in_specs=(rows, P("dp", None)) + weights + (both,) * 6 + (rows,),
        out_specs=(rows, rows) + weights + (both,) * 6,
        check_vma=False,
    )
```

```python
import functools

import jax
import jax.numpy as jnp
import numpy as np
from jax import lax
from jax.experimental import pallas as pl
from jax.experimental.pallas import tpu as pltpu
from jax.sharding import PartitionSpec as P

HD = 64
BLOCK = 256
EXTRA = 16
STEP = 128
SIDE = 8
RING_ROOM = 2 << 20
ATTEND_ROOM = 12 << 20
TILE_ROOM = 8 << 20
TAIL = 16

epsilon = 1e-06
root_half = 0.7071067811865476
inv_root_tau = 0.3989422804014327
masked_value = -1e30
bf16 = jnp.bfloat16
f32 = jnp.float32


def contract(a, b, dims, out=f32):
    return lax.dot_general(a, b, (dims, ((), ())), preferred_element_type=f32).astype(out)


def ring_order(size):
    return list(range(0, size, 2)) + list(range(size - 1, 0, -2)) if size > 1 else [0]


class Links:
    def __init__(self, dp, tensor):
        self.dp, self.tensor = dp, tensor
        order = ring_order(dp)
        self.order = jnp.array(order, jnp.int32)
        place = [0] * dp
        for position, member in enumerate(order):
            place[member] = position
        self.forward = [(order[i], order[(i + 1) % dp]) for i in range(dp)]
        self.backward = [(b, a) for a, b in self.forward]
        self.me = lax.axis_index("dp")
        self.position = jnp.array(place, jnp.int32)[self.me]
        self.ahead = dp // 2
        self.behind = dp - 1 - self.ahead
        offsets = jnp.arange(-self.ahead, self.behind + 1, dtype=jnp.int32)
        self.members = self.order[(self.position + offsets + dp) % dp]

    def swap(self, value, mask):
        return lax.ppermute(value, "tensor", [(i, i ^ mask) for i in range(self.tensor)])


def tie(*holders):
    flat, tree = jax.tree.flatten([holder.live for holder in holders])
    flat = lax.optimization_barrier(tuple(flat))
    for holder, live in zip(holders, jax.tree.unflatten(tree, flat)):
        holder.live = live


class Box:
    def __init__(self, *live):
        self.live = list(live)


class GatherRing:
    def __init__(self, links, value):
        self.links = links
        self.live = [value, value]
        self.pieces = {0: value}
        self.count = 0

    def step(self):
        links = self.links
        self.count += 1
        up, down = self.live
        half = up.shape[0] // 32 * 16
        if self.count == links.ahead and half:
            up, down = up[:half], down[half:]
            up = lax.ppermute(up, "dp", links.forward)
            self.live = [up, lax.ppermute(down, "dp", links.backward)]
            return
        up = lax.ppermute(up, "dp", links.forward)
        self.pieces[-self.count] = up
        if self.count <= links.behind:
            down = lax.ppermute(down, "dp", links.backward)
            self.pieces[self.count] = down
        self.live = [up, down]

    def full(self, plan, rows):
        links = self.links
        pieces = [self.pieces[offset] for offset in range(1 - links.ahead, links.behind + 1)]
        halves = self.live if self.live[0].shape[0] < self.pieces[0].shape[0] else self.live[:1]
        return assemble(links.members, halves + pieces, plan, rows)


class ScatterRing:
    def __init__(self, links, groups):
        self.links = links
        self.groups = groups
        self.count = 0
        self.live = ring_call(links, groups, (links.ahead, -links.ahead), (), bf16, first=True)

    def step(self):
        links = self.links
        self.count += 1
        up, down = self.live
        up = lax.ppermute(up, "dp", links.forward)
        down = lax.ppermute(down, "dp", links.backward)
        left = links.ahead - self.count
        if left:
            up, down = ring_call(links, self.groups, (left, -left), (up, down), bf16)
        self.live = [up, down]

    def total(self):
        sources, counts, rows, _ = flatten(self.groups)
        widths = [group[0].shape[2] for group in self.groups]
        return pl.pallas_call(
            functools.partial(total_kernel, counts=counts, place=self.links.ahead),
            out_shape=[
                jax.ShapeDtypeStruct((rows, width), f32 if index == 0 else bf16)
                for index, width in enumerate(widths)
            ],
            in_specs=[SMEM] + [VMEM] * (len(sources) + 2),
            out_specs=[VMEM] * len(widths),
            compiler_params=pltpu.CompilerParams(vmem_limit_bytes=RING_ROOM),
            name="ring_total",
        )(self.links.members, *sources, *self.live)


VMEM = pl.BlockSpec(memory_space=pltpu.VMEM)
SMEM = pl.BlockSpec(memory_space=pltpu.SMEM)


def block_of(sources, member):
    if len(sources) == 1:
        return sources[0][member].astype(f32)
    low, high = sources
    half = low.shape[0]
    lower = low[jnp.minimum(member, half - 1)].astype(f32)
    return jnp.where(member < half, lower, high[jnp.maximum(member - half, 0)].astype(f32))


def ring_sums(members_ref, refs, counts, place):
    member = members_ref[place]
    at = 0
    for count in counts:
        total = None
        for pieces in count:
            made = block_of(refs[at : at + pieces], member)
            total = made if total is None else total + made
            at += pieces
        yield total


def ring_kernel(members_ref, *refs, counts, places, dtype, first):
    size, sends = sum(map(sum, counts)), len(places)
    sources, arrived, outs = refs[:size], refs[size:-sends], refs[-sends:]
    for index, place in enumerate(places):
        column = 0
        out = outs[index]
        mine = arrived if sends == 1 else arrived[index : index + 1]
        for made in ring_sums(members_ref, sources, counts, place):
            rows, width = made.shape
            own = slice(column, column + width)
            column += width
            if first:
                half = out.shape[0]
                out[:, own] = (made[:half] if index == 0 else made[rows - half :]).astype(dtype)
                continue
            whole = [one for one in mine if one.shape[0] == rows]
            for one in whole:
                made = made + one[:, own].astype(f32)
            out[:, own] = made.astype(dtype)
            for one in mine:
                if one.shape[0] < rows:
                    half = one.shape[0]
                    part = slice(0, half) if index == 0 else slice(rows - half, rows)
                    out[part, own] = (made[part] + one[:, own].astype(f32)).astype(dtype)


def total_kernel(members_ref, *refs, counts, place):
    size = sum(map(sum, counts))
    sources, arrived, outs = refs[:size], refs[size : size + 2], refs[size + 2 :]
    column = 0
    for out, made in zip(outs, ring_sums(members_ref, sources, counts, place)):
        own = slice(column, column + out.shape[1])
        for one in arrived:
            made = made + one[:, own].astype(f32)
        out[...] = made.astype(out.dtype)
        column += out.shape[1]


def flatten(groups):
    sources, counts = [], []
    for group in groups:
        pieces = [one if isinstance(one, (list, tuple)) else [one] for one in group]
        counts.append([len(one) for one in pieces])
        sources += [part for one in pieces for part in one]
    widths = [(group[0][0] if isinstance(group[0], (list, tuple)) else group[0]).shape for group in groups]
    return sources, counts, widths[0][1], sum(width[2] for width in widths)


def ring_call(links, groups, offsets, arrived, dtype, first=False):
    sources, counts, rows, columns = flatten(groups)
    size = rows * columns
    return list(
        pl.pallas_call(
            functools.partial(
                ring_kernel,
                counts=counts,
                places=[(offset + links.ahead) % links.dp for offset in offsets],
                dtype=dtype,
                first=first,
            ),
            out_shape=[
                jax.ShapeDtypeStruct((rows // 2 if first else rows, columns), dtype) for _ in offsets
            ],
            in_specs=[SMEM] + [VMEM] * (len(sources) + len(arrived)),
            out_specs=[VMEM] * len(offsets),
            compiler_params=pltpu.CompilerParams(vmem_limit_bytes=RING_ROOM),
            cost_estimate=pl.CostEstimate(
                flops=size * 2, bytes_accessed=6 * size * len(offsets), transcendentals=0
            ),
            name="ring_sum",
        )(links.members, *sources, *arrived)
    )


def finish_kernel(
    members_ref, me_ref, *refs, counts, place, tables
):
    size = sum(map(sum, counts))
    sources, arrived, outs = refs[:size], refs[size : size + 2], refs[size + 2 :]
    (total,) = ring_sums(members_ref, sources, counts, place)
    for one in arrived:
        total = total + one[...].astype(f32)
    rows, group = outs[0].shape
    for index in range(3):
        outs[index][...] = total[:rows, index * group : (index + 1) * group]
    outs[3][...] = total[:rows, 3 * group :].T
    side = total[rows:]
    wide = side.shape[1]
    for out, (line, at, per, full) in zip(outs[4:7], tables):
        turned = pltpu.roll(side, wide - me_ref[0] * per, axis=1)
        for row in range(out.shape[0]):
            start = at + row * full
            out[row : row + 1, :] = turned[line : line + 1, start : start + per]
    share = outs[7].shape[1]
    turned = pltpu.roll(side, wide - me_ref[1] * share, axis=1)
    outs[7][...] = turned[TAIL - 8 :, 0:share]


def finish(links, ring, places, shapes, tables):
    sources, counts, _, _ = flatten(ring.groups)
    return pl.pallas_call(
        functools.partial(finish_kernel, counts=counts, place=links.ahead, tables=tables),
        out_shape=shapes,
        in_specs=[SMEM] * 2 + [VMEM] * (len(sources) + 2),
        out_specs=[VMEM] * len(shapes),
        compiler_params=pltpu.CompilerParams(vmem_limit_bytes=RING_ROOM),
        name="finish",
    )(links.members, places, *sources, *ring.live)


def assemble_kernel(members_ref, *refs, count, total_rows, plan, rows):
    pieces, outs = refs[:count], refs[count:]
    total, index, done = None, 0, 0
    blocks = 0
    for piece in pieces:
        first = members_ref[index] * rows + done
        own = min(piece.shape[0], rows - done)
        for out, (at, width, _) in zip(outs, plan):
            out[pl.ds(pl.multiple_of(first, 16), own), :] = piece[0:own, at : at + width]
        done += piece.shape[0]
        if done == total_rows:
            if total_rows > rows:
                side = piece[own:, :].astype(f32)
                total = side if total is None else total + side
            index, done, blocks = index + 1, 0, blocks + 1
    for out, (at, width, kept) in zip(outs, plan):
        if kept == "all":
            for index in range(3):
                first = blocks * rows + index * SIDE
                out[first : first + SIDE, :] = total[:, index * width : (index + 1) * width].astype(bf16)
        elif kept is not None:
            out[blocks * rows :, :] = jnp.broadcast_to(
                total[kept : kept + 1, at : at + width], (SIDE, width)
            ).astype(bf16)


def assemble(members, pieces, plan, rows):
    count = members.shape[0]
    full, wide = pieces[-1].shape
    if rows % 16:
        if len(pieces) > count:
            pieces = [jnp.concatenate(pieces[:2])] + pieces[2:]
        stacked = jnp.stack(pieces)
        back = jnp.zeros((count,), jnp.int32).at[members].set(jnp.arange(count, dtype=jnp.int32))
        stacked = jnp.take(stacked, back, axis=0)
        weights = stacked[:, :rows].reshape(count * rows, -1)
        total = jnp.sum(stacked[:, rows:].astype(f32), axis=0)
        outs = []
        for at, width, kept in plan:
            out = weights[:, at : at + width]
            if kept == "all":
                parts = [total[:, i * width : (i + 1) * width].astype(bf16) for i in range(3)]
                out = jnp.concatenate([out] + parts)
            elif kept is not None:
                row = jnp.broadcast_to(total[kept : kept + 1, at : at + width], (SIDE, width))
                out = jnp.concatenate([out, row.astype(bf16)])
            outs.append(out)
        return outs
    shapes = [
        jax.ShapeDtypeStruct(
            (count * rows + SIDE * {None: 0, "all": 3}.get(kept, 1), width), bf16
        )
        for _, width, kept in plan
    ]
    return pl.pallas_call(
        functools.partial(
            assemble_kernel, count=len(pieces), total_rows=full, plan=plan, rows=rows
        ),
        out_shape=shapes,
        in_specs=[SMEM] + [VMEM] * len(pieces),
        out_specs=[VMEM] * len(shapes),
        compiler_params=pltpu.CompilerParams(vmem_limit_bytes=RING_ROOM),
        cost_estimate=pl.CostEstimate(
            flops=0, bytes_accessed=4 * count * full * wide, transcendentals=0
        ),
        name="assemble",
    )(members, *pieces)


def one_hot(first, rows, size):
    hit = lax.broadcasted_iota(jnp.int32, (rows, size), 1) == (
        lax.broadcasted_iota(jnp.int32, (rows, size), 0) + first
    )
    return jnp.where(hit, 1.0, 0.0).astype(bf16)


def placed(table, me, dp):
    count, per = table.shape
    spread = contract(table, one_hot(me * per, per, per * dp), ((1,), (0,)))
    return [spread[row : row + 1] for row in range(count)]


def only_row(row, at):
    line = lax.broadcasted_iota(jnp.int32, (SIDE, row.shape[1]), 0)
    return jnp.where(line == at, row, 0.0)


def pack_kernel(me_ref, *refs, dp):
    sources, out_ref, held, sems = refs[:5], refs[5], refs[6:11], refs[11]
    copies = [
        pltpu.make_async_copy(source, target, sems.at[index])
        for index, (source, target) in enumerate(zip(sources, held))
    ]
    for copy in copies:
        copy.start()
    for copy in copies:
        copy.wait()
    query_ref, key_ref, value_ref, b_query_ref, b_value_ref = held
    rows, group = query_ref.shape
    out_ref[0:rows, 0:group] = query_ref[...]
    out_ref[0:rows, group : 2 * group] = key_ref[...]
    out_ref[0:rows, 2 * group :] = value_ref[...]
    me = me_ref[0]
    row = jnp.concatenate(
        placed(b_query_ref[...], me, dp)
        + [jnp.zeros((1, group), f32)]
        + placed(b_value_ref[...], me, dp),
        axis=1,
    )
    out_ref[rows:, :] = only_row(row, 0).astype(bf16)


def pack_late_kernel(me_ref, w_out_ref, w_down_ref, vectors_ref, out_ref, down_ref, *, dp):
    rows, hidden = w_down_ref.shape
    out_ref[...] = w_out_ref[...].T
    down_ref[0:rows, :] = w_down_ref[...]
    left = vectors_ref[...]
    share = left.shape[1]
    place = one_hot(me_ref[0] * share, share, share * dp)
    spread = []
    for _ in range(3):
        part = left.astype(bf16)
        left = left - part.astype(f32)
        spread.append(contract(part, place, ((1,), (0,))))
    row = jnp.concatenate(spread, axis=1)
    blank = jnp.zeros((SIDE, hidden - row.shape[1]), f32)
    down_ref[rows:, :] = jnp.concatenate([row, blank], axis=1).astype(bf16)


def pack_up_kernel(
    me_ref, out_ref, far_out_ref, w_up_ref, down_ref, far_down_ref, b_up_ref, up_ref, pair_ref, *, dp
):
    rows, hidden = w_up_ref.shape
    group = out_ref.shape[1]
    up_ref[0:rows, 0:group] = out_ref[...]
    up_ref[0:rows, group : 2 * group] = far_out_ref[...]
    up_ref[0:rows, 2 * group :] = w_up_ref[...]
    pair_ref[:, 0:hidden] = down_ref[0:rows, :]
    pair_ref[:, hidden:] = far_down_ref[0:rows, :]
    near = down_ref[rows:, 0 : 3 * group].astype(f32)
    far = far_down_ref[rows:, 0 : 3 * group].astype(f32)
    bias = jnp.concatenate(
        [jnp.zeros((1, 2 * group), f32)] + placed(b_up_ref[...], me_ref[0], dp), axis=1
    )
    side = jnp.concatenate([near, far], axis=1) + only_row(bias, 6)
    up_ref[rows:, :] = side.astype(bf16)


def small_call(kernel, name, links, shapes, *operands, copied=False):
    place = pl.BlockSpec(memory_space=pltpu.HBM) if copied else VMEM
    scratch = []
    if copied:
        operands = [pltpu.with_memory_space_constraint(x, pltpu.HBM) for x in operands]
        scratch = [pltpu.VMEM(x.shape, x.dtype) for x in operands]
        scratch.append(pltpu.SemaphoreType.DMA((len(operands),)))
    return pl.pallas_call(
        functools.partial(kernel, dp=links.dp),
        out_shape=shapes,
        in_specs=[SMEM] + [place] * len(operands),
        out_specs=[VMEM] * len(shapes),
        scratch_shapes=scratch,
        compiler_params=pltpu.CompilerParams(vmem_limit_bytes=RING_ROOM),
        name=name,
    )(links.me.reshape(1), *operands)


def documents_kernel(mine_ref, lengths_ref, span_ref, window_ref, *, block):
    length = span_ref.shape[1]
    count = length // block
    place = lax.broadcasted_iota(jnp.int32, (1, length), 1)
    low = high = jnp.zeros((1, length), jnp.int32)
    begins, ends = [jnp.int32(0)] * count, [jnp.int32(0)] * count
    start = jnp.int32(0)
    for document in range(lengths_ref.shape[1]):
        end = start + lengths_ref[mine_ref[0], document]
        inside = (place >= start) & (place < end)
        low, high = jnp.where(inside, start, low), jnp.where(inside, end, high)
        for index in range(count):
            first, last = index * block, (index + 1) * block - 1
            begins[index] = jnp.where((start <= first) & (first < end), start, begins[index])
            ends[index] = jnp.where((start <= last) & (last < end), end, ends[index])
        start = end
    span_ref[0:1, :] = low
    span_ref[1:2, :] = high
    for index in range(count):
        begin = lax.div(begins[index], jnp.int32(STEP)) * STEP
        blocks = lax.div(ends[index] - begin + (block - 1), jnp.int32(block))
        window_ref[0, index] = jnp.minimum(begin, length - blocks * block)
        window_ref[1, index] = blocks


def documents(mine, lengths, length, block):
    return pl.pallas_call(
        functools.partial(documents_kernel, block=block),
        out_shape=[
            jax.ShapeDtypeStruct((2, length), jnp.int32),
            jax.ShapeDtypeStruct((2, length // block), jnp.int32),
        ],
        in_specs=[SMEM, SMEM],
        out_specs=[VMEM, SMEM],
        compiler_params=pltpu.CompilerParams(vmem_limit_bytes=RING_ROOM),
        name="documents",
    )(mine.reshape(1), lengths)


def fill_bias(bias, begin, low, high, size):
    keys = lax.broadcasted_iota(jnp.int32, (size, low.shape[1]), 0) + begin
    bias[0:size, :] = jnp.where((keys >= low) & (keys < high), 0.0, masked_value)


def attend_kernel(
    window_ref, tokens_ref, weight_ref, span_ref, out_ref, log_ref, qkv_ref, keys, values, bias, hold, *, block
):
    length = qkv_ref.shape[1]
    heads = qkv_ref.shape[0] // (3 * HD)
    width = heads * HD
    model = tokens_ref.shape[1]
    made = contract(tokens_ref[...], weight_ref[0:model, :], ((1,), (0,)))
    made = made + weight_ref[model : model + 1, :].astype(f32)
    qkv_ref[...] = made.astype(bf16).T
    tail = jnp.where(lax.broadcasted_iota(jnp.int32, (EXTRA, length), 0) == 0, 1.0, 0.0).astype(bf16)
    for head in range(heads):
        keys[head] = qkv_ref[width + head * HD : width + (head + 1) * HD, :].T
        values[head, 0:HD, :] = qkv_ref[2 * width + head * HD : 2 * width + (head + 1) * HD, :]
        values[head, HD : HD + EXTRA, :] = tail

    def one_block(index, _):
        lanes = pl.ds(pl.multiple_of(index * block, block), block)
        begin = pl.multiple_of(window_ref[0, index], STEP)

        def with_count(count):
            fill_bias(bias, begin, span_ref[0:1, lanes], span_ref[1:2, lanes], count * block)
            tops = []
            for head in range(heads):
                queries = qkv_ref[head * HD : (head + 1) * HD, lanes] * 0.125
                top = None
                for piece in range(count):
                    rows = slice(piece * block, (piece + 1) * block)
                    own = pl.ds(begin + piece * block, block)
                    scores = contract(keys[head, own, :], queries, ((1,), (0,))) + bias[rows, :]
                    hold[head, rows, :] = scores
                    most = jnp.max(scores.reshape(block // 8, 8, block), axis=0)
                    top = most if top is None else jnp.maximum(top, most)
                tops.append(jnp.max(top, axis=0, keepdims=True))
            for head in range(heads):
                total = None
                for piece in range(count):
                    rows = slice(piece * block, (piece + 1) * block)
                    own = pl.ds(begin + piece * block, block)
                    weights = jnp.exp(hold[head, rows, :] - tops[head]).astype(bf16)
                    made = contract(values[head, :, own], weights, ((1,), (0,)))
                    total = made if total is None else total + made
                mass = total[HD : HD + 1, :]
                out_ref[head * HD : (head + 1) * HD, lanes] = (total[:HD] / mass).astype(bf16)
                log_ref[head : head + 1, lanes] = tops[head] + jnp.log(mass)

        for count in range(1, length // block + 1):
            pl.when(window_ref[1, index] == count)(functools.partial(with_count, count))
        return 0

    lax.fori_loop(0, length // block, one_block, 0)


def attend_back_kernel(
    window_ref, qkv_ref, span_ref, out_ref, log_ref, weight_ref, one_ref, result_ref, keys, values, bias, grad_key, grad_value, grad_ref, *, block, half
):
    length = qkv_ref.shape[1]
    model = one_ref.shape[0]
    group = grad_ref.shape[0]
    weight = weight_ref[0:model, half * group : (half + 1) * group]
    grad_ref[...] = contract(weight, one_ref[...], ((0,), (0,)), bf16)
    heads = qkv_ref.shape[0] // (3 * HD)
    width = heads * HD
    for head in range(heads):
        keys[head] = qkv_ref[width + head * HD : width + (head + 1) * HD, :].T
        values[head] = qkv_ref[2 * width + head * HD : 2 * width + (head + 1) * HD, :].T
    grad_key[...] = jnp.zeros_like(grad_key)
    grad_value[...] = jnp.zeros_like(grad_value)

    def one_block(index, _):
        lanes = pl.ds(pl.multiple_of(index * block, block), block)
        begin = pl.multiple_of(window_ref[0, index], STEP)

        def with_count(count):
            size = count * block
            window = pl.ds(begin, size)
            fill_bias(bias, begin, span_ref[0:1, lanes], span_ref[1:2, lanes], size)
            for head in range(heads):
                own = slice(head * HD, (head + 1) * HD)
                queries = qkv_ref[own, lanes] * 0.125
                grads = grad_ref[own, lanes]
                delta = jnp.sum(
                    out_ref[own, lanes].astype(f32) * grads.astype(f32), axis=0, keepdims=True
                )
                scores = contract(keys[head, window, :], queries, ((1,), (0,))) + bias[0:size, :]
                weights = jnp.exp(scores - log_ref[head : head + 1, lanes])
                grad_prob = contract(values[head, window, :], grads, ((1,), (0,)))
                grad_scores = (weights * (grad_prob - delta)).astype(bf16)
                grad_value[own, window] += contract(grads, weights.astype(bf16), ((1,), (1,)))
                grad_key[own, window] += contract(queries, grad_scores, ((1,), (1,)))
                key_cols = qkv_ref[width + head * HD : width + (head + 1) * HD, window]
                made = contract(key_cols, grad_scores, ((1,), (0,)))
                result_ref[own, lanes] = (made * 0.125).astype(bf16)

        for count in range(1, length // block + 1):
            pl.when(window_ref[1, index] == count)(functools.partial(with_count, count))
        return 0

    lax.fori_loop(0, length // block, one_block, 0)
    result_ref[width : 2 * width, :] = grad_key[...].astype(bf16)
    result_ref[2 * width :, :] = grad_value[...].astype(bf16)


def attend(tokens, weight, window, span):
    length, model = tokens.shape
    width = weight.shape[1]
    heads = width // (3 * HD)
    return pl.pallas_call(
        functools.partial(attend_kernel, block=BLOCK),
        out_shape=(
            jax.ShapeDtypeStruct((heads * HD, length), bf16),
            jax.ShapeDtypeStruct((8, length), f32),
            jax.ShapeDtypeStruct((width, length), bf16),
        ),
        in_specs=[SMEM] + [VMEM] * 3,
        out_specs=(VMEM,) * 3,
        scratch_shapes=[
            pltpu.VMEM((heads, length, HD), bf16),
            pltpu.VMEM((heads, HD + EXTRA, length), bf16),
            pltpu.VMEM((length, BLOCK), f32),
            pltpu.VMEM((heads, length, BLOCK), f32),
        ],
        compiler_params=pltpu.CompilerParams(vmem_limit_bytes=ATTEND_ROOM),
        cost_estimate=pl.CostEstimate(
            flops=4 * heads * length * length * HD + 2 * length * model * width,
            bytes_accessed=4 * width * length,
            transcendentals=heads * length * length,
        ),
        name="attend",
    )(window, tokens, weight, span)


def attend_back(qkv, out, logs, weight, half, one, window, span):
    width, length = qkv.shape
    heads = width // (3 * HD)
    return pl.pallas_call(
        functools.partial(attend_back_kernel, block=BLOCK, half=half),
        out_shape=jax.ShapeDtypeStruct((width, length), bf16),
        in_specs=[SMEM] + [VMEM] * 6,
        out_specs=VMEM,
        scratch_shapes=[
            pltpu.VMEM((heads, length, HD), bf16),
            pltpu.VMEM((heads, length, HD), bf16),
            pltpu.VMEM((length, BLOCK), f32),
            pltpu.VMEM((heads * HD, length), f32),
            pltpu.VMEM((heads * HD, length), f32),
            pltpu.VMEM((heads * HD, length), bf16),
        ],
        compiler_params=pltpu.CompilerParams(vmem_limit_bytes=ATTEND_ROOM),
        cost_estimate=pl.CostEstimate(
            flops=10 * heads * length * length * HD,
            bytes_accessed=6 * width * length,
            transcendentals=heads * length * length,
        ),
        name="attend_back",
    )(window, qkv, span, out, logs, weight, one)


def grad_weight_kernel(tokens_ref, grad_ref, one_ref, mixture_ref, *refs, starts):
    more, out_ref = refs[2:-1], refs[-1]
    up_ref, vectors_ref = refs[0], refs[1]
    dp, full, columns = out_ref.shape
    rows = full - TAIL
    wide = grad_ref.shape[0]
    group = wide // 3
    made = contract(tokens_ref[...], grad_ref[...], ((1,), (1,)))
    out_low = contract(one_ref[...], mixture_ref[...], ((1,), (1,)))
    ones = jnp.ones((TAIL, grad_ref.shape[1]), bf16)
    lane = contract(ones, grad_ref[...], ((1,), (1,)))
    line = lax.broadcasted_iota(jnp.int32, (TAIL, columns), 0)
    bias_row = jnp.concatenate([lane, jnp.zeros((TAIL, columns - wide), f32)], axis=1)
    side = jnp.where(line == 0, bias_row, 0.0) + jnp.where(line == 1, up_ref[0:1, :], 0.0)
    lower = jnp.concatenate([jnp.zeros((TAIL - 8, columns), f32), vectors_ref[...]], axis=0)
    side = side + lower
    for index in range(dp):
        own = slice(index * rows, (index + 1) * rows)
        left, right, low = made[own], out_low[own], side
        for held, start in zip(more, starts):
            at = index - start
            if not 0 <= at < held.shape[0]:
                continue
            left = left + held[at, 0:rows, 0:wide].astype(f32)
            right = right + held[at, 0:rows, wide:].astype(f32)
            low = low + held[at, rows:, :].astype(f32)
        out_ref[index, 0:rows, 0:wide] = left.astype(bf16)
        out_ref[index, 0:rows, wide:] = right.astype(bf16)
        out_ref[index, rows:, :] = low.astype(bf16)


def grad_weight(dp, tokens, grad, one, mixture, up_row, vectors, more, starts):
    model, length = tokens.shape
    wide, group = grad.shape[0], mixture.shape[0]
    return pl.pallas_call(
        functools.partial(grad_weight_kernel, starts=starts),
        out_shape=jax.ShapeDtypeStruct((dp, model // dp + TAIL, wide + group), bf16),
        in_specs=[VMEM] * (6 + len(more)),
        out_specs=VMEM,
        compiler_params=pltpu.CompilerParams(vmem_limit_bytes=ATTEND_ROOM),
        cost_estimate=pl.CostEstimate(
            flops=2 * length * model * (wide + group),
            bytes_accessed=2 * (length + model) * (wide + group + model),
            transcendentals=0,
        ),
        name="grad_weight",
    )(tokens, grad, one, mixture, up_row, vectors, *more)


def normalize(values):
    average = jnp.mean(values, axis=-1, keepdims=True)
    centred = values - average
    variance = jnp.mean(centred * centred, axis=-1, keepdims=True)
    inv_scale = lax.rsqrt(variance + epsilon)
    return centred * inv_scale, inv_scale


def normalize_back(grad_out, unit_rows, inv_scale, norm_gain):
    grad_unit = grad_out * norm_gain
    middle = grad_unit - jnp.mean(grad_unit, axis=-1, keepdims=True)
    middle = middle - unit_rows * jnp.mean(grad_unit * unit_rows, axis=-1, keepdims=True)
    return inv_scale * middle


def gelu_parts(up_pre):
    normal_cdf = 0.5 * (1.0 + lax.erf(up_pre * root_half))
    return (
        up_pre * normal_cdf,
        normal_cdf + up_pre * inv_root_tau * jnp.exp(-0.5 * up_pre * up_pre),
    )


def tile_kernel(*refs, kernel, steps, tiles):
    def step(index, _):
        views = []
        for ref, tile in zip(refs, tiles):
            if tile is None or steps == 1:
                views.append(ref)
                continue
            size = ref.shape[tile] // steps
            own = pl.ds(pl.multiple_of(index * size, size), size)
            views.append(ref.at[own, :] if tile == 0 else ref.at[:, own])
        kernel(index, *views)
        return 0

    lax.fori_loop(0, steps, step, 0)


def tiled(kernel, name, steps, operands, tiles, shapes, flops):
    shapes, out_tiles = [x for x, _ in shapes], [x for _, x in shapes]
    moved = sum(x.size * x.dtype.itemsize for x in list(operands) + shapes)
    return pl.pallas_call(
        functools.partial(
            tile_kernel, kernel=kernel, steps=steps, tiles=tuple(tiles) + tuple(out_tiles)
        ),
        out_shape=shapes,
        in_specs=[VMEM] * len(operands),
        out_specs=[VMEM] * len(shapes),
        compiler_params=pltpu.CompilerParams(vmem_limit_bytes=TILE_ROOM),
        cost_estimate=pl.CostEstimate(flops=flops, bytes_accessed=moved, transcendentals=0),
        name=name,
    )(*operands)


def shape(*size, dtype=f32):
    return jax.ShapeDtypeStruct(size, dtype)


def vectors_kernel(step, lane_ref, near_ref, far_ref, out_ref):
    model = out_ref.shape[1]
    wide = near_ref.shape[1]
    size = wide // 2
    total = jnp.zeros((SIDE, model), f32)
    lanes = lax.broadcasted_iota(jnp.int32, (size, model), 1)
    for j in range(4):
        held = near_ref if j % 2 == 0 else far_ref
        first = (j // 2) * 3 * size
        place = jnp.where(lanes == lane_ref[:, j : j + 1], 1.0, 0.0).astype(bf16)
        for part in range(3):
            at = first + part * size
            line = model + at // wide * SIDE
            part = held[line : line + SIDE, at % wide : at % wide + size]
            total = total + contract(part, place, ((1,), (0,)))
    out_ref[...] = total


def out_kernel(step, m0, m1, m2, m3, near, far, vectors, tokens, low_ref, turned_ref, unit_ref, scale_ref):
    total = vectors[0:1, :] + tokens[...].astype(f32)
    model, group = total.shape[1], m0.shape[0]
    for index, mixture in enumerate((m0, m1, m2, m3)):
        held = near if index % 2 == 0 else far
        weight = held[0:model, index // 2 * group : (index // 2 + 1) * group]
        total = total + contract(mixture[...], weight, ((0,), (1,)))
    unit, scale = normalize(total)
    unit_ref[...] = unit
    scale_ref[...] = scale
    low = (unit * vectors[2:3, :] + vectors[3:4, :]).astype(bf16)
    low_ref[...] = low
    turned_ref[...] = low.T


def up_kernel(step, low, weight, act_ref, slope_ref):
    model = low.shape[1]
    up_pre = contract(low[...], weight[0:model, :], ((1,), (0,)))
    act, slope = gelu_parts(up_pre + weight[model : model + 1, :].astype(f32))
    act_ref[...] = act.astype(bf16)
    slope_ref[...] = slope.astype(bf16)


def column_sums(step, ref, rows, start=0.0):
    line = lax.broadcasted_iota(jnp.int32, ref.shape, 0)
    made = jnp.zeros(ref.shape, f32)
    for at, values in rows:
        made = made + jnp.where(line == at, jnp.sum(values, axis=0, keepdims=True), 0.0)

    @pl.when(step == 0)
    def _():
        ref[...] = made + start

    @pl.when(step > 0)
    def _():
        ref[...] += made


def down_kernel(
    step, a0, a1, a2, a3, w0, w1, w2, w3, vectors, unit_ref, cotangent, result_ref, grad_ref, low_ref, turned_ref, sums_ref
):
    total = vectors[1:2, :] + unit_ref[...] * vectors[2:3, :] + vectors[3:4, :]
    for act, weight in ((a0, w0), (a1, w1), (a2, w2), (a3, w3)):
        total = total + contract(act[...], weight[...], ((1,), (1,)))
    unit, scale = normalize(total)
    result_ref[...] = (unit * vectors[4:5, :] + vectors[5:6, :]).astype(bf16)
    grad_out = cotangent[...].astype(f32)
    grad = normalize_back(grad_out, unit, scale, vectors[4:5, :])
    grad_ref[...] = grad
    low_ref[...] = grad.astype(bf16)
    turned_ref[...] = grad.astype(bf16).T
    column_sums(step, sums_ref, ((1, grad), (4, grad_out * unit), (5, grad_out)))


def turn_kernel(step, rows, turned_ref):
    turned_ref[...] = rows[...].T


def outer_kernel(turned_ref, right_ref, *refs, added):
    outs = refs[added:]
    at = 0
    for out in outs:
        rows = slice(at, at + out.shape[0])
        made = contract(turned_ref[rows, :], right_ref[...], ((1,), (0,)))
        if added:
            made = made + refs[0][rows, :].astype(f32)
        out[...] = made.astype(bf16)
        at = at + out.shape[0]


def outer(turned, right, cuts=None, arrived=()):
    rows, columns = turned.shape[0], right.shape[1]
    cuts = cuts or [0, rows]
    shapes = [shape(high - low, columns, dtype=bf16) for low, high in zip(cuts, cuts[1:])]
    return pl.pallas_call(
        functools.partial(outer_kernel, added=len(arrived)),
        out_shape=shapes,
        in_specs=[VMEM] * (2 + len(arrived)),
        out_specs=[VMEM] * len(shapes),
        compiler_params=pltpu.CompilerParams(vmem_limit_bytes=TILE_ROOM),
        cost_estimate=pl.CostEstimate(
            flops=2 * turned.size * columns, bytes_accessed=6 * rows * columns, transcendentals=0
        ),
        name="outer",
    )(turned, right, *arrived)


def input_kernel(step, grad, weight, total, out_ref):
    model = total.shape[1]
    made = contract(grad[...], weight[0:model, :], ((0,), (1,)))
    out_ref[...] = (total[...] + made).astype(out_ref.dtype)


def down_end_kernel(own, far, out_ref):
    out_ref[...] = own[...] + far[...].astype(f32)


def slope_kernel(step, low, weight, slope, grad_ref, sums_ref):
    made = contract(low[...], weight[...], ((1,), (0,))) * slope[...].astype(f32)
    made = made.astype(bf16)
    grad_ref[...] = made
    column_sums(step, sums_ref, ((0, made.astype(f32)),))


def first_kernel(
    step, g0, g1, g2, g3, w0, w1, w2, w3, vectors, two, unit_ref, scale, sums_two, grad_ref, turned_ref, sums_ref
):
    total = two[...]
    model = total.shape[1]
    for grad, weight in ((g0, w0), (g1, w1), (g2, w2), (g3, w3)):
        total = total + contract(grad[...], weight[0:model, :], ((1,), (1,)))
    unit = unit_ref[...]
    grad = normalize_back(total, unit, scale[...], vectors[2:3, :])
    grad_ref[...] = grad
    turned_ref[...] = grad.astype(bf16).T
    column_sums(step, sums_ref, ((0, grad), (2, total * unit), (3, total)), sums_two[...])


def per_device(
    tokens,
    doc_lengths,
    w_query,
    w_key,
    w_value,
    w_out,
    w_up,
    w_down,
    b_query,
    b_value,
    b_up,
    b_out,
    b_down,
    gain_one,
    shift_one,
    gain_two,
    shift_two,
    cotangent,
):
    dp, tensor = lax.axis_size("dp"), lax.axis_size("tensor")
    length, model = tokens.shape
    rows = model // dp
    group = w_query.shape[1]
    links = Links(dp, tensor)
    swap = links.swap

    share = b_out.shape[0]
    me = links.me
    mine = lax.axis_index("tensor")
    hidden = w_up.shape[1]
    (packed,) = small_call(
        pack_kernel,
        "pack",
        links,
        [shape(rows + SIDE, 3 * group, dtype=bf16)],
        w_query,
        w_key,
        w_value,
        b_query,
        b_value,
        copied=True,
    )
    ring_attn = GatherRing(links, packed)
    zero = jnp.zeros((share,), f32)
    vectors = jnp.stack([b_out, b_down, gain_one, shift_one, gain_two, shift_two, zero, zero])

    ring_attn.step()
    late_out, late_down = small_call(
        pack_late_kernel,
        "pack_late",
        links,
        [shape(rows, group, dtype=bf16), shape(rows + SIDE, hidden, dtype=bf16)],
        w_out,
        w_down.T,
        vectors,
    )
    late = Box(late_out, late_down, doc_lengths)
    tie(ring_attn, late)
    late_out, late_down, early_lengths = late.live
    ring_attn.step()
    far_late = Box(swap(late_out, 2), swap(late_down, 2))
    span, window = documents(mine, early_lengths, length, BLOCK)
    done = Box(span)
    tie(ring_attn, done)
    span = done.live[0]
    ring_attn.step()
    tie(ring_attn, far_late)
    up_chunk, down_chunk = small_call(
        pack_up_kernel,
        "pack_up",
        links,
        [
            shape(rows + SIDE, 2 * group + hidden, dtype=bf16),
            shape(rows, 2 * hidden, dtype=bf16),
        ],
        late_out,
        far_late.live[0],
        w_up,
        late_down,
        far_late.live[1],
        b_up,
    )
    ring_up = GatherRing(links, up_chunk)
    ring_down = GatherRing(links, down_chunk)
    for _ in range(links.ahead - 3):
        ring_attn.step()
    (attn_own,) = ring_attn.full([(0, 3 * group, 0)], rows)

    attn_w = [attn_own, None, None, None]
    qkv, mixture, logs = [None] * 4, [None] * 4, [None] * 4

    def attend_group(j):
        mixture[j], logs[j], qkv[j] = attend(work.live[0], attn_w[j], window, span)
        return Box(mixture[j])

    work = Box(tokens, attn_own)
    tie(ring_attn, ring_up, work)
    attn_w[0] = work.live[1]
    work = Box(work.live[0])
    far = Box(swap(attn_w[0], 2))
    attn_w[1] = swap(attn_w[0], 1)
    ring_up.step()
    done = attend_group(0)
    tie(ring_up, work, done)
    ring_up.step()
    done = attend_group(1)
    tie(ring_up, work, done)
    ring_up.step()
    (tokens_turned,) = tiled(
        turn_kernel, "turn", 4, (work.live[0],), (0,), [(shape(model, length, dtype=bf16), 1)], 0
    )
    turned = Box(tokens_turned)
    tie(ring_up, work, far, turned)
    tokens_turned = turned.live[0]
    attn_w[2] = far.live[0]
    attn_w[3] = swap(attn_w[2], 1)
    for _ in range(links.ahead - 3):
        ring_up.step()
    done = attend_group(2)
    tie(ring_up, work, done, ring_down)
    ring_down.step()
    out_near, up_own = ring_up.full([(0, 2 * group, "all"), (2 * group, hidden, 6)], rows)
    out_far = swap(out_near, 1)
    cuts = [0, model // 3, 2 * model // 3, up_own.shape[0]]
    held, across_up = Box(up_own), []

    def up_across():
        low, high = cuts[len(across_up) : len(across_up) + 2]
        across_up.append(Box(swap(held.live[0][low:high], 2)))
        return across_up[-1]

    moved = up_across()
    done = attend_group(3)
    tie(ring_down, work, done, held, moved)

    ring_down.step()
    moved = up_across()
    count = np.arange(dp * share)
    base = jnp.asarray((count // share * tensor * share + count % share)[:, None], jnp.int32)
    lanes = base + (mine ^ jnp.arange(4, dtype=jnp.int32))[None, :] * share
    (vectors,) = tiled(
        vectors_kernel,
        "vectors",
        1,
        (lanes, out_near, out_far),
        (None,) * 3,
        [(shape(SIDE, model), None)],
        0,
    )
    up_w = [up_own, None, None, None]
    first_low, first_turned, unit_one, scale_one = tiled(
        out_kernel,
        "attention_out",
        4,
        (*mixture, out_near, out_far, vectors, work.live[0]),
        (1,) * 4 + (None,) * 3 + (0,),
        [
            (shape(length, model, dtype=bf16), 0),
            (shape(model, length, dtype=bf16), 1),
            (shape(length, model), 0),
            (shape(length, 1), 0),
        ],
        2 * length * model * model,
    )
    activated, slopes = [None] * 4, [None] * 4

    def up_group(j):
        activated[j], slopes[j] = tiled(
            up_kernel,
            "up",
            4,
            (work.live[0], up_w[j]),
            (0, None),
            [(shape(length, hidden, dtype=bf16), 0)] * 2,
            2 * length * model * hidden,
        )
        return Box(activated[j])

    work = Box(first_low)
    tie(ring_down, work, held, moved)
    up_w[0] = held.live[0]
    moved = up_across()
    up_w[1] = swap(up_w[0], 1)
    ring_down.step()
    done = up_group(0)
    tie(ring_down, work, done, moved)
    for _ in range(links.ahead - 3):
        ring_down.step()
    up_w[2] = jnp.concatenate([box.live[0] for box in across_up])
    up_w[3] = swap(up_w[2], 1)
    done = up_group(1)
    tie(ring_down, work, done)
    down_own, down_across = ring_down.full([(0, hidden, None), (hidden, hidden, None)], rows)
    down_w = [down_own, swap(down_own, 1), down_across, swap(down_across, 1)]
    done = [up_group(2), up_group(3)]
    result, grad_two, grad_two_low, grad_two_turned, sums_two = tiled(
        down_kernel,
        "down",
        4,
        (*activated, *down_w, vectors, unit_one, cotangent),
        (0,) * 4 + (None,) * 5 + (0,) * 2,
        [
            (shape(length, model, dtype=bf16), 0),
            (shape(length, model), 0),
            (shape(length, model, dtype=bf16), 0),
            (shape(model, length, dtype=bf16), 1),
            (shape(SIDE, model), None),
        ],
        8 * length * model * hidden,
    )
    work = Box(grad_two_low)

    def blocks(value):
        return value.reshape(-1, rows, value.shape[-1])

    def grad_down(j):
        return outer(grad_two_turned, activated[j])[0]

    def grad_w_up(j, cuts=None, arrived=()):
        return outer(first_turned, grad_up[j], cuts, arrived)

    grad_up, grad_bias_up = [None] * 4, [None] * 4

    def back_up(j):
        grad_up[j], grad_bias_up[j] = tiled(
            slope_kernel,
            "back_up",
            4,
            (work.live[0], down_w[j], slopes[j]),
            (0, None, 0),
            [(shape(length, hidden, dtype=bf16), 0), (shape(SIDE, hidden), None)],
            2 * length * model * hidden,
        )

    def cuts(total):
        return [0, total * 3 // 8, total * 5 // 8, total]

    back_up(3)
    three_up = Box(*grad_w_up(3))
    tie(work, three_up)
    three_up = Box(swap(three_up.live[0], 1))
    back_up(2)
    sent = Box(grad_down(3), grad_down(1))
    tie(work, three_up, sent)
    three, one = (swap(v, 1) for v in sent.live)
    across = grad_w_up(2, cuts(model), (three_up.live[0],))
    far_up = [Box(swap(across[0], 2))]
    two, zero = grad_down(2), grad_down(0)
    pair = Box(two, zero, three, one)
    tie(work, pair)
    two, zero, three, one = (blocks(v) for v in pair.live)
    sums_down = ScatterRing(links, [[zero, one], [two, three]])
    sums_down.step()
    back_up(1)
    back_up(0)
    kept = Box(*grad_w_up(1), *grad_w_up(0), grad_up[0])
    tie(work, kept, sums_down, far_up[0])
    one_up, zero_up, grad_up[0] = kept.live
    one_up = Box(swap(one_up, 1))
    far_up.append(Box(swap(across[1], 2)))
    sums_down.step()
    grad_one, grad_one_turned, sums = tiled(
        first_kernel,
        "back_first",
        4,
        (*grad_up, *up_w, vectors, grad_two, unit_one, scale_one, sums_two),
        (0,) * 4 + (None,) * 5 + (0,) * 3 + (None,),
        [
            (shape(length, model), 0),
            (shape(model, length, dtype=bf16), 1),
            (shape(SIDE, model), None),
        ],
        8 * length * model * hidden,
    )
    work = Box(grad_one_turned)
    tie(work, one_up, sums_down, far_up[1])
    grad_qkv = [None] * 4

    def back_attention(j):
        grad_qkv[j] = attend_back(
            qkv[j],
            mixture[j],
            logs[j],
            out_near if j % 2 == 0 else out_far,
            j // 2,
            work.live[0],
            window,
            span,
        )
        return Box(grad_qkv[j])

    grad_input = Box(grad_one)

    def back_input(j):
        grad_input.live = tiled(
            input_kernel,
            "back_input",
            4,
            (grad_qkv[j], attn_w[j], grad_input.live[0]),
            (1, None, 0),
            [(shape(length, model, dtype=f32 if j else bf16), 0)],
            6 * length * model * group,
        )

    def back_group(j, arrived=(), starts=()):
        return grad_weight(
            dp,
            tokens_turned,
            grad_qkv[j],
            work.live[0],
            mixture[j],
            grad_bias_up[j],
            sums,
            arrived,
            starts,
        )

    far_up.append(Box(swap(across[2], 2)))
    sums_down.step()
    back_attention(3)
    three = Box(back_group(3))
    tie(work, three, far_up[2], sums_down)
    recv = Box(swap(three.live[0], 1))
    for _ in range(links.ahead - 3):
        sums_down.step()
    done = back_attention(2)
    tie(work, done, recv, sums_down)
    grad_qkv[2] = done.live[0]
    far = blocks(jnp.concatenate([box.live[0] for box in far_up]))
    sums_up = ScatterRing(links, [[blocks(zero_up), blocks(one_up.live[0]), far]])
    sums_up.step()
    down_total, down_far = sums_down.total()
    end_down = Box(swap(down_far, 2))
    two = Box(back_group(2, (recv.live[0],), (0,)))
    back_input(3)
    tie(work, two, sums_up, end_down, grad_input)
    split = cuts(dp)
    far_attn = [Box(swap(two.live[0][split[0] : split[1]], 2))]
    sums_up.step()
    done = back_attention(1)
    tie(work, done, sums_up, far_attn[0])
    grad_qkv[1] = done.live[0]
    far_attn.append(Box(swap(two.live[0][split[1] : split[2]], 2)))
    sums_up.step()
    one = Box(back_group(1))
    back_input(2)
    tie(work, one, far_attn[1], sums_up, grad_input)
    recv = Box(swap(one.live[0], 1))
    far_attn.append(Box(swap(two.live[0][split[2] :], 2)))
    for _ in range(links.ahead - 3):
        sums_up.step()
    done = back_attention(0)
    tie(work, done, recv, far_attn[2], sums_up)
    grad_qkv[0] = done.live[0]
    arrived = [recv.live[0]] + [box.live[0] for box in far_attn]
    (grad_down_own,) = pl.pallas_call(
        down_end_kernel,
        out_shape=[shape(rows, hidden)],
        in_specs=[VMEM] * 2,
        out_specs=[VMEM],
        compiler_params=pltpu.CompilerParams(vmem_limit_bytes=RING_ROOM),
        name="down_end",
    )(down_total, end_down.live[0])
    ends = Box(grad_down_own, *sums_up.total())
    zero = Box(back_group(0, arrived, (0, *split[:3])), grad_qkv[:2])
    tie(work, zero, ends)
    sums_attn = ScatterRing(links, [[zero.live[0]]])
    grad_qkv[:2] = zero.live[1]
    for j in (1, 0):
        sums_attn.step()
        back_input(j)
        tie(grad_input, sums_attn)
    while sums_attn.count < links.ahead:
        sums_attn.step()
    full = dp * b_query.shape[1]
    full_up = dp * b_up.shape[1]
    *made, held = finish(
        links,
        sums_attn,
        jnp.stack([me, me * tensor + mine]),
        [shape(rows, group)] * 3
        + [shape(group, rows)]
        + [shape(*table.shape) for table in (b_query, b_value, b_up)]
        + [shape(SIDE, share)],
        (
            (0, 0, b_query.shape[1], full),
            (0, 2 * group, b_value.shape[1], full),
            (1, 0, b_up.shape[1], full_up),
        ),
    )
    return (
        result,
        grad_input.live[0],
        *made[:4],
        ends.live[1],
        ends.live[0].T,
        *made[4:],
        *[held[i] for i in range(6)],
    )


def solution(mesh):
    both = P(("dp", "tensor"))
    rows = P(("dp", "tensor"), None)
    down = P("tensor", "dp")
    wide = P("dp", "tensor")
    weights = (wide, wide, wide, down, wide, down, down, down, down)
    return jax.shard_map(
        per_device,
        mesh=mesh,
        in_specs=(rows, P("dp", None)) + weights + (both,) * 6 + (rows,),
        out_specs=(rows, rows) + weights + (both,) * 6,
        check_vma=False,
    )
```

```python
import functools

import jax
import jax.numpy as jnp
import numpy as np
from jax import lax
from jax.experimental import pallas as pl
from jax.experimental.pallas import tpu as pltpu
from jax.sharding import PartitionSpec as P

HD = 64
BLOCK = 256
EXTRA = 16
STEP = 128
SIDE = 8
RING_ROOM = 2 << 20
ATTEND_ROOM = 12 << 20
TILE_ROOM = 8 << 20
TAIL = 8

epsilon = 1e-06
root_half = 0.7071067811865476
inv_root_tau = 0.3989422804014327
masked_value = -1e30
bf16 = jnp.bfloat16
f32 = jnp.float32


def contract(a, b, dims, out=f32):
    return lax.dot_general(a, b, (dims, ((), ())), preferred_element_type=f32).astype(out)


def ring_order(size):
    return list(range(0, size, 2)) + list(range(size - 1, 0, -2)) if size > 1 else [0]


class Links:
    def __init__(self, dp, tensor):
        self.dp, self.tensor = dp, tensor
        order = ring_order(dp)
        self.forward = [(order[i], order[(i + 1) % dp]) for i in range(dp)]
        self.backward = [(b, a) for a, b in self.forward]
        self.me = lax.axis_index("dp")
        self.ahead = dp // 2
        self.behind = dp - 1 - self.ahead
        offsets = jnp.arange(-self.ahead, self.behind + 1, dtype=jnp.int32)
        half = lax.shift_right_logical(self.me, 1)
        position = jnp.where((self.me & 1) == 0, half, dp - 1 - half)
        place = position + offsets
        place = jnp.where(place < 0, place + dp, jnp.where(place < dp, place, place - dp))
        self.members = jnp.where(place < (dp + 1) // 2, 2 * place, 2 * (dp - 1 - place) + 1)

    def swap(self, value, mask):
        return lax.ppermute(value, "tensor", [(i, i ^ mask) for i in range(self.tensor)])


def tie(*holders):
    flat, tree = jax.tree.flatten([holder.live for holder in holders])
    flat = lax.optimization_barrier(tuple(flat))
    for holder, live in zip(holders, jax.tree.unflatten(tree, flat)):
        holder.live = live


class Box:
    def __init__(self, *live):
        self.live = list(live)


class GatherRing:
    def __init__(self, links, value):
        self.links = links
        self.live = [value, value]
        self.pieces = {0: value}
        self.count = 0

    def step(self):
        links = self.links
        self.count += 1
        up, down = self.live
        half = up.shape[0] // 32 * 16
        if self.count == links.ahead and half:
            up, down = up[:half], down[half:]
            up = lax.ppermute(up, "dp", links.forward)
            self.live = [up, lax.ppermute(down, "dp", links.backward)]
            return
        up = lax.ppermute(up, "dp", links.forward)
        self.pieces[-self.count] = up
        if self.count <= links.behind:
            down = lax.ppermute(down, "dp", links.backward)
            self.pieces[self.count] = down
        self.live = [up, down]

    def full(self, plan, rows):
        links = self.links
        pieces = [self.pieces[offset] for offset in range(1 - links.ahead, links.behind + 1)]
        halves = self.live if self.live[0].shape[0] < self.pieces[0].shape[0] else self.live[:1]
        return assemble(links.members, halves + pieces, plan, rows)


class ScatterRing:
    def __init__(self, links, groups):
        self.links = links
        self.groups = groups
        self.count = 0
        self.live = ring_call(links, groups, (links.ahead, -links.ahead), (), bf16, first=True)

    def step(self):
        links = self.links
        self.count += 1
        up, down = self.live
        up = lax.ppermute(up, "dp", links.forward)
        down = lax.ppermute(down, "dp", links.backward)
        left = links.ahead - self.count
        if left:
            up, down = ring_call(links, self.groups, (left, -left), (up, down), bf16)
        self.live = [up, down]

    def total(self):
        sources, counts, rows, _ = flatten(self.groups)
        widths = [group[0].shape[2] for group in self.groups]
        return pl.pallas_call(
            functools.partial(total_kernel, counts=counts, place=self.links.ahead),
            out_shape=[
                jax.ShapeDtypeStruct((rows, width), f32 if index == 0 else bf16)
                for index, width in enumerate(widths)
            ],
            in_specs=[SMEM] + [VMEM] * (len(sources) + 2),
            out_specs=[VMEM] * len(widths),
            compiler_params=pltpu.CompilerParams(vmem_limit_bytes=RING_ROOM),
            name="ring_total",
        )(self.links.members, *sources, *self.live)


VMEM = pl.BlockSpec(memory_space=pltpu.VMEM)
SMEM = pl.BlockSpec(memory_space=pltpu.SMEM)


def block_of(sources, member):
    if len(sources) == 1:
        return sources[0][member].astype(f32)
    low, high = sources
    half = low.shape[0]
    lower = low[jnp.minimum(member, half - 1)].astype(f32)
    return jnp.where(member < half, lower, high[jnp.maximum(member - half, 0)].astype(f32))


def ring_sums(members_ref, refs, counts, place):
    member = members_ref[place]
    at = 0
    for count in counts:
        total = None
        for pieces in count:
            made = block_of(refs[at : at + pieces], member)
            total = made if total is None else total + made
            at += pieces
        yield total


def ring_kernel(members_ref, *refs, counts, places, dtype, first):
    size, sends = sum(map(sum, counts)), len(places)
    sources, arrived, outs = refs[:size], refs[size:-sends], refs[-sends:]
    for index, place in enumerate(places):
        column = 0
        out = outs[index]
        mine = arrived if sends == 1 else arrived[index : index + 1]
        for made in ring_sums(members_ref, sources, counts, place):
            rows, width = made.shape
            own = slice(column, column + width)
            column += width
            if first:
                half = out.shape[0]
                out[:, own] = (made[:half] if index == 0 else made[rows - half :]).astype(dtype)
                continue
            whole = [one for one in mine if one.shape[0] == rows]
            for one in whole:
                made = made + one[:, own].astype(f32)
            out[:, own] = made.astype(dtype)
            for one in mine:
                if one.shape[0] < rows:
                    half = one.shape[0]
                    part = slice(0, half) if index == 0 else slice(rows - half, rows)
                    out[part, own] = (made[part] + one[:, own].astype(f32)).astype(dtype)


def total_kernel(members_ref, *refs, counts, place):
    size = sum(map(sum, counts))
    sources, arrived, outs = refs[:size], refs[size : size + 2], refs[size + 2 :]
    column = 0
    for out, made in zip(outs, ring_sums(members_ref, sources, counts, place)):
        own = slice(column, column + out.shape[1])
        for one in arrived:
            made = made + one[:, own].astype(f32)
        out[...] = made.astype(out.dtype)
        column += out.shape[1]


def flatten(groups):
    sources, counts = [], []
    for group in groups:
        pieces = [one if isinstance(one, (list, tuple)) else [one] for one in group]
        counts.append([len(one) for one in pieces])
        sources += [part for one in pieces for part in one]
    widths = [(group[0][0] if isinstance(group[0], (list, tuple)) else group[0]).shape for group in groups]
    return sources, counts, widths[0][1], sum(width[2] for width in widths)


def ring_call(links, groups, offsets, arrived, dtype, first=False):
    sources, counts, rows, columns = flatten(groups)
    size = rows * columns
    return list(
        pl.pallas_call(
            functools.partial(
                ring_kernel,
                counts=counts,
                places=[(offset + links.ahead) % links.dp for offset in offsets],
                dtype=dtype,
                first=first,
            ),
            out_shape=[
                jax.ShapeDtypeStruct((rows // 2 if first else rows, columns), dtype) for _ in offsets
            ],
            in_specs=[SMEM] + [VMEM] * (len(sources) + len(arrived)),
            out_specs=[VMEM] * len(offsets),
            compiler_params=pltpu.CompilerParams(vmem_limit_bytes=RING_ROOM),
            cost_estimate=pl.CostEstimate(
                flops=size * 2, bytes_accessed=6 * size * len(offsets), transcendentals=0
            ),
            name="ring_sum",
        )(links.members, *sources, *arrived)
    )


def finish_kernel(
    members_ref, me_ref, *refs, counts, place, tables
):
    size = sum(map(sum, counts))
    sources, arrived, outs = refs[:size], refs[size : size + 2], refs[size + 2 :]
    (total,) = ring_sums(members_ref, sources, counts, place)
    for one in arrived:
        total = total + one[...].astype(f32)
    rows, group = outs[0].shape
    for index in range(3):
        outs[index][...] = total[:rows, index * group : (index + 1) * group]
    outs[3][...] = total[:rows, 3 * group :].T
    side = total[rows:]
    wide = side.shape[1]
    for out, (line, at, per, full) in zip(outs[4:7], tables):
        turned = pltpu.roll(side, wide - me_ref[0] * per, axis=1)
        for row in range(out.shape[0]):
            start = at + row * full
            out[row : row + 1, :] = turned[line : line + 1, start : start + per]
    share = outs[7].shape[1]
    turned = pltpu.roll(side, wide - me_ref[1] * share, axis=1)
    outs[7][...] = turned[:, 0:share]


def finish(links, ring, places, shapes, tables):
    sources, counts, _, _ = flatten(ring.groups)
    return pl.pallas_call(
        functools.partial(finish_kernel, counts=counts, place=links.ahead, tables=tables),
        out_shape=shapes,
        in_specs=[SMEM] * 2 + [VMEM] * (len(sources) + 2),
        out_specs=[VMEM] * len(shapes),
        compiler_params=pltpu.CompilerParams(vmem_limit_bytes=RING_ROOM),
        name="finish",
    )(links.members, places, *sources, *ring.live)


def assemble_kernel(members_ref, *refs, count, total_rows, plan, rows):
    pieces, outs = refs[:count], refs[count:]
    total, index, done = None, 0, 0
    blocks = 0
    for piece in pieces:
        first = members_ref[index] * rows + done
        own = min(piece.shape[0], rows - done)
        for out, (at, width, _) in zip(outs, plan):
            out[pl.ds(pl.multiple_of(first, 16), own), :] = piece[0:own, at : at + width]
        done += piece.shape[0]
        if done == total_rows:
            if total_rows > rows:
                side = piece[own:, :].astype(f32)
                total = side if total is None else total + side
            index, done, blocks = index + 1, 0, blocks + 1
    for out, (at, width, kept) in zip(outs, plan):
        if kept == "all":
            for index in range(3):
                first = blocks * rows + index * SIDE
                out[first : first + SIDE, :] = total[:, index * width : (index + 1) * width].astype(bf16)
        elif kept is not None:
            out[blocks * rows :, :] = jnp.broadcast_to(
                total[kept : kept + 1, at : at + width], (SIDE, width)
            ).astype(bf16)


def assemble(members, pieces, plan, rows):
    count = members.shape[0]
    full, wide = pieces[-1].shape
    if rows % 16:
        if len(pieces) > count:
            pieces = [jnp.concatenate(pieces[:2])] + pieces[2:]
        stacked = jnp.stack(pieces)
        back = jnp.zeros((count,), jnp.int32).at[members].set(jnp.arange(count, dtype=jnp.int32))
        stacked = jnp.take(stacked, back, axis=0)
        weights = stacked[:, :rows].reshape(count * rows, -1)
        total = jnp.sum(stacked[:, rows:].astype(f32), axis=0)
        outs = []
        for at, width, kept in plan:
            out = weights[:, at : at + width]
            if kept == "all":
                parts = [total[:, i * width : (i + 1) * width].astype(bf16) for i in range(3)]
                out = jnp.concatenate([out] + parts)
            elif kept is not None:
                row = jnp.broadcast_to(total[kept : kept + 1, at : at + width], (SIDE, width))
                out = jnp.concatenate([out, row.astype(bf16)])
            outs.append(out)
        return outs
    shapes = [
        jax.ShapeDtypeStruct(
            (count * rows + SIDE * {None: 0, "all": 3}.get(kept, 1), width), bf16
        )
        for _, width, kept in plan
    ]
    return pl.pallas_call(
        functools.partial(
            assemble_kernel, count=len(pieces), total_rows=full, plan=plan, rows=rows
        ),
        out_shape=shapes,
        in_specs=[SMEM] + [VMEM] * len(pieces),
        out_specs=[VMEM] * len(shapes),
        compiler_params=pltpu.CompilerParams(vmem_limit_bytes=RING_ROOM),
        cost_estimate=pl.CostEstimate(
            flops=0, bytes_accessed=4 * count * full * wide, transcendentals=0
        ),
        name="assemble",
    )(members, *pieces)


def one_hot(first, rows, size):
    hit = lax.broadcasted_iota(jnp.int32, (rows, size), 1) == (
        lax.broadcasted_iota(jnp.int32, (rows, size), 0) + first
    )
    return jnp.where(hit, 1.0, 0.0).astype(bf16)


def placed(table, me, dp):
    count, per = table.shape
    spread = contract(table, one_hot(me * per, per, per * dp), ((1,), (0,)))
    return [spread[row : row + 1] for row in range(count)]


def only_row(row, at):
    line = lax.broadcasted_iota(jnp.int32, (SIDE, row.shape[1]), 0)
    return jnp.where(line == at, row, 0.0)


def pack_kernel(me_ref, *refs, dp):
    sources, out_ref, held, sems = refs[:5], refs[5], refs[6:11], refs[11]
    copies = [
        pltpu.make_async_copy(source, target, sems.at[index])
        for index, (source, target) in enumerate(zip(sources, held))
    ]
    for copy in copies:
        copy.start()
    for copy in copies:
        copy.wait()
    query_ref, key_ref, value_ref, b_query_ref, b_value_ref = held
    rows, group = query_ref.shape
    out_ref[0:rows, 0:group] = query_ref[...]
    out_ref[0:rows, group : 2 * group] = key_ref[...]
    out_ref[0:rows, 2 * group :] = value_ref[...]
    me = me_ref[0]
    row = jnp.concatenate(
        placed(b_query_ref[...], me, dp)
        + [jnp.zeros((1, group), f32)]
        + placed(b_value_ref[...], me, dp),
        axis=1,
    )
    out_ref[rows:, :] = only_row(row, 0).astype(bf16)


def pack_late_kernel(me_ref, w_out_ref, w_down_ref, vectors_ref, out_ref, down_ref, *, dp):
    rows, hidden = w_down_ref.shape
    out_ref[...] = w_out_ref[...].T
    down_ref[0:rows, :] = w_down_ref[...]
    left = vectors_ref[...]
    share = left.shape[1]
    place = one_hot(me_ref[0] * share, share, share * dp)
    spread = []
    for _ in range(3):
        part = left.astype(bf16)
        left = left - part.astype(f32)
        spread.append(contract(part, place, ((1,), (0,))))
    row = jnp.concatenate(spread, axis=1)
    blank = jnp.zeros((SIDE, hidden - row.shape[1]), f32)
    down_ref[rows:, :] = jnp.concatenate([row, blank], axis=1).astype(bf16)


def pack_up_kernel(
    me_ref, out_ref, far_out_ref, w_up_ref, down_ref, far_down_ref, b_up_ref, up_ref, pair_ref, *, dp
):
    rows, hidden = w_up_ref.shape
    group = out_ref.shape[1]
    up_ref[0:rows, 0:group] = out_ref[...]
    up_ref[0:rows, group : 2 * group] = far_out_ref[...]
    up_ref[0:rows, 2 * group :] = w_up_ref[...]
    pair_ref[:, 0:hidden] = down_ref[0:rows, :]
    pair_ref[:, hidden:] = far_down_ref[0:rows, :]
    near = down_ref[rows:, 0 : 3 * group].astype(f32)
    far = far_down_ref[rows:, 0 : 3 * group].astype(f32)
    bias = jnp.concatenate(
        [jnp.zeros((1, 2 * group), f32)] + placed(b_up_ref[...], me_ref[0], dp), axis=1
    )
    side = jnp.concatenate([near, far], axis=1) + only_row(bias, 6)
    up_ref[rows:, :] = side.astype(bf16)


def small_call(kernel, name, links, shapes, *operands, copied=False):
    place = pl.BlockSpec(memory_space=pltpu.HBM) if copied else VMEM
    scratch = []
    if copied:
        operands = [pltpu.with_memory_space_constraint(x, pltpu.HBM) for x in operands]
        scratch = [pltpu.VMEM(x.shape, x.dtype) for x in operands]
        scratch.append(pltpu.SemaphoreType.DMA((len(operands),)))
    return pl.pallas_call(
        functools.partial(kernel, dp=links.dp),
        out_shape=shapes,
        in_specs=[SMEM] + [place] * len(operands),
        out_specs=[VMEM] * len(shapes),
        scratch_shapes=scratch,
        compiler_params=pltpu.CompilerParams(vmem_limit_bytes=RING_ROOM),
        name=name,
    )(links.me.reshape(1), *operands)


def documents_kernel(mine_ref, lengths_ref, span_ref, window_ref, *, block):
    length = span_ref.shape[1]
    count = length // block
    place = lax.broadcasted_iota(jnp.int32, (1, length), 1)
    low = high = jnp.zeros((1, length), jnp.int32)
    begins, ends = [jnp.int32(0)] * count, [jnp.int32(0)] * count
    start = jnp.int32(0)
    for document in range(lengths_ref.shape[1]):
        end = start + lengths_ref[mine_ref[0], document]
        inside = (place >= start) & (place < end)
        low, high = jnp.where(inside, start, low), jnp.where(inside, end, high)
        for index in range(count):
            first, last = index * block, (index + 1) * block - 1
            begins[index] = jnp.where((start <= first) & (first < end), start, begins[index])
            ends[index] = jnp.where((start <= last) & (last < end), end, ends[index])
        start = end
    span_ref[0:1, :] = low
    span_ref[1:2, :] = high
    for index in range(count):
        begin = lax.div(begins[index], jnp.int32(STEP)) * STEP
        window_ref[0, index] = begin
        window_ref[1, index] = lax.div(ends[index] - begin + (STEP - 1), jnp.int32(STEP))


def documents(mine, lengths, length, block):
    return pl.pallas_call(
        functools.partial(documents_kernel, block=block),
        out_shape=[
            jax.ShapeDtypeStruct((2, length), jnp.int32),
            jax.ShapeDtypeStruct((2, length // block), jnp.int32),
        ],
        in_specs=[SMEM, SMEM],
        out_specs=[VMEM, SMEM],
        compiler_params=pltpu.CompilerParams(vmem_limit_bytes=RING_ROOM),
        name="documents",
    )(mine.reshape(1), lengths)


def fill_bias(bias, begin, low, high, size):
    keys = lax.broadcasted_iota(jnp.int32, (size, low.shape[1]), 0) + begin
    bias[0:size, :] = jnp.where((keys >= low) & (keys < high), 0.0, masked_value)


def attend_kernel(
    window_ref, tokens_ref, weight_ref, span_ref, out_ref, log_ref, qkv_ref, keys, values, bias, hold, *, block
):
    length = qkv_ref.shape[1]
    heads = qkv_ref.shape[0] // (3 * HD)
    width = heads * HD
    model = tokens_ref.shape[1]
    made = contract(tokens_ref[...], weight_ref[0:model, :], ((1,), (0,)))
    made = made + weight_ref[model : model + 1, :].astype(f32)
    qkv_ref[...] = made.astype(bf16).T
    tail = jnp.where(lax.broadcasted_iota(jnp.int32, (EXTRA, length), 0) == 0, 1.0, 0.0).astype(bf16)
    for head in range(heads):
        keys[head] = qkv_ref[width + head * HD : width + (head + 1) * HD, :].T
        values[head, 0:HD, :] = qkv_ref[2 * width + head * HD : 2 * width + (head + 1) * HD, :]
        values[head, HD : HD + EXTRA, :] = tail

    def one_block(index, _):
        lanes = pl.ds(pl.multiple_of(index * block, block), block)
        begin = pl.multiple_of(window_ref[0, index], STEP)

        def with_count(count):
            fill_bias(bias, begin, span_ref[0:1, lanes], span_ref[1:2, lanes], count * STEP)
            parts = [(at, min(block, count * STEP - at)) for at in range(0, count * STEP, block)]
            tops = []
            for head in range(heads):
                queries = qkv_ref[head * HD : (head + 1) * HD, lanes] * 0.125
                top = None
                for at, size in parts:
                    own = pl.ds(begin + at, size)
                    scores = contract(keys[head, own, :], queries, ((1,), (0,))) + bias[at : at + size, :]
                    hold[head, at : at + size, :] = scores
                    most = jnp.max(scores.reshape(size // 8, 8, block), axis=0)
                    top = most if top is None else jnp.maximum(top, most)
                tops.append(jnp.max(top, axis=0, keepdims=True))
            for head in range(heads):
                total = None
                for at, size in parts:
                    own = pl.ds(begin + at, size)
                    weights = jnp.exp(hold[head, at : at + size, :] - tops[head]).astype(bf16)
                    made = contract(values[head, :, own], weights, ((1,), (0,)))
                    total = made if total is None else total + made
                mass = total[HD : HD + 1, :]
                out_ref[head * HD : (head + 1) * HD, lanes] = (total[:HD] / mass).astype(bf16)
                log_ref[head : head + 1, lanes] = tops[head] + jnp.log(mass)

        for count in range(1, length // STEP + 1):
            pl.when(window_ref[1, index] == count)(functools.partial(with_count, count))
        return 0

    lax.fori_loop(0, length // block, one_block, 0)


def attend_back_kernel(
    window_ref, half_ref, qkv_ref, span_ref, out_ref, log_ref, weight_ref, one_ref, result_ref, keys, values, bias, grad_key, grad_value, grad_ref, weight, *, block
):
    length = qkv_ref.shape[1]
    model = one_ref.shape[0]
    group = grad_ref.shape[0]
    for half in range(2):

        @pl.when(half_ref[0] == half)
        def _():
            weight[...] = weight_ref[0:model, half * group : (half + 1) * group]

    grad_ref[...] = contract(weight[...], one_ref[...], ((0,), (0,)), bf16)
    heads = qkv_ref.shape[0] // (3 * HD)
    width = heads * HD
    for head in range(heads):
        keys[head] = qkv_ref[width + head * HD : width + (head + 1) * HD, :].T
        values[head] = qkv_ref[2 * width + head * HD : 2 * width + (head + 1) * HD, :].T
    grad_key[...] = jnp.zeros_like(grad_key)
    grad_value[...] = jnp.zeros_like(grad_value)

    def one_block(index, _):
        lanes = pl.ds(pl.multiple_of(index * block, block), block)
        begin = pl.multiple_of(window_ref[0, index], STEP)

        def with_count(count):
            size = count * STEP
            window = pl.ds(begin, size)
            fill_bias(bias, begin, span_ref[0:1, lanes], span_ref[1:2, lanes], size)
            owns = [slice(head * HD, (head + 1) * HD) for head in range(heads)]
            queries = [qkv_ref[own, lanes] * 0.125 for own in owns]
            grads = [grad_ref[own, lanes] for own in owns]
            deltas = [
                jnp.sum(out_ref[own, lanes].astype(f32) * grad.astype(f32), axis=0, keepdims=True)
                for own, grad in zip(owns, grads)
            ]
            made = [None] * heads
            for at in range(0, size, block):
                step = min(block, size - at)
                part = pl.ds(begin + at, step)
                raw = []
                for head in range(heads):
                    scores = contract(keys[head, part, :], queries[head], ((1,), (0,)))
                    grad_prob = contract(values[head, part, :], grads[head], ((1,), (0,)))
                    raw.append((scores + bias[at : at + step, :], grad_prob))
                both = []
                for head, (scores, grad_prob) in enumerate(raw):
                    weights = jnp.exp(scores - log_ref[head : head + 1, lanes])
                    both.append((weights.astype(bf16), (weights * (grad_prob - deltas[head])).astype(bf16)))
                for head, (weights, grad_scores) in enumerate(both):
                    own = owns[head]
                    grad_value[own, part] += contract(grads[head], weights, ((1,), (1,)))
                    grad_key[own, part] += contract(queries[head], grad_scores, ((1,), (1,)))
                    key_cols = qkv_ref[width + head * HD : width + (head + 1) * HD, part]
                    more = contract(key_cols, grad_scores, ((1,), (0,)))
                    made[head] = more if made[head] is None else made[head] + more
            for head, own in enumerate(owns):
                result_ref[own, lanes] = (made[head] * 0.125).astype(bf16)

        for count in range(1, length // STEP + 1):
            pl.when(window_ref[1, index] == count)(functools.partial(with_count, count))
        return 0

    lax.fori_loop(0, length // block, one_block, 0)
    result_ref[width : 2 * width, :] = grad_key[...].astype(bf16)
    result_ref[2 * width :, :] = grad_value[...].astype(bf16)


def attend(tokens, weight, window, span):
    length, model = tokens.shape
    width = weight.shape[1]
    heads = width // (3 * HD)
    return pl.pallas_call(
        functools.partial(attend_kernel, block=BLOCK),
        out_shape=(
            jax.ShapeDtypeStruct((heads * HD, length), bf16),
            jax.ShapeDtypeStruct((8, length), f32),
            jax.ShapeDtypeStruct((width, length), bf16),
        ),
        in_specs=[SMEM] + [VMEM] * 3,
        out_specs=(VMEM,) * 3,
        scratch_shapes=[
            pltpu.VMEM((heads, length, HD), bf16),
            pltpu.VMEM((heads, HD + EXTRA, length), bf16),
            pltpu.VMEM((length, BLOCK), f32),
            pltpu.VMEM((heads, length, BLOCK), f32),
        ],
        compiler_params=pltpu.CompilerParams(vmem_limit_bytes=ATTEND_ROOM),
        cost_estimate=pl.CostEstimate(
            flops=4 * heads * length * length * HD + 2 * length * model * width,
            bytes_accessed=4 * width * length,
            transcendentals=heads * length * length,
        ),
        name="attend",
    )(window, tokens, weight, span)


def attend_back(qkv, out, logs, weight, half, one, window, span):
    width, length = qkv.shape
    heads = width // (3 * HD)
    return pl.pallas_call(
        functools.partial(attend_back_kernel, block=BLOCK),
        out_shape=jax.ShapeDtypeStruct((width, length), bf16),
        in_specs=[SMEM] * 2 + [VMEM] * 6,
        out_specs=VMEM,
        scratch_shapes=[
            pltpu.VMEM((heads, length, HD), bf16),
            pltpu.VMEM((heads, length, HD), bf16),
            pltpu.VMEM((length, BLOCK), f32),
            pltpu.VMEM((heads * HD, length), f32),
            pltpu.VMEM((heads * HD, length), f32),
            pltpu.VMEM((heads * HD, length), bf16),
            pltpu.VMEM((one.shape[0], heads * HD), bf16),
        ],
        compiler_params=pltpu.CompilerParams(vmem_limit_bytes=ATTEND_ROOM),
        cost_estimate=pl.CostEstimate(
            flops=10 * heads * length * length * HD,
            bytes_accessed=6 * width * length,
            transcendentals=heads * length * length,
        ),
        name="attend_back",
    )(window, jnp.full((1,), half, jnp.int32), qkv, span, out, logs, weight, one)


def grad_weight_kernel(tokens_ref, grad_ref, one_ref, mixture_ref, *refs, starts):
    more, out_ref = refs[2:-1], refs[-1]
    up_ref, vectors_ref = refs[0], refs[1]
    dp, full, columns = out_ref.shape
    rows = full - TAIL
    wide = grad_ref.shape[0]
    group = wide // 3
    made = contract(tokens_ref[...], grad_ref[...], ((1,), (1,)))
    out_low = contract(one_ref[...], mixture_ref[...], ((1,), (1,)))
    ones = jnp.ones((TAIL, grad_ref.shape[1]), bf16)
    lane = contract(ones, grad_ref[...], ((1,), (1,)))
    line = lax.broadcasted_iota(jnp.int32, (TAIL, columns), 0)
    bias_row = jnp.concatenate([lane, jnp.zeros((TAIL, columns - wide), f32)], axis=1)
    side = jnp.where(line == 0, bias_row, 0.0) + jnp.where(line == 1, up_ref[0:1, :], 0.0)
    lower = jnp.concatenate([jnp.zeros((2, columns), f32), vectors_ref[0:6, :]], axis=0)
    side = side + lower
    for index in range(dp):
        own = slice(index * rows, (index + 1) * rows)
        left, right, low = made[own], out_low[own], side
        for held, start in zip(more, starts):
            at = index - start
            if not 0 <= at < held.shape[0]:
                continue
            left = left + held[at, 0:rows, 0:wide].astype(f32)
            right = right + held[at, 0:rows, wide:].astype(f32)
            low = low + held[at, rows:, :].astype(f32)
        out_ref[index, 0:rows, 0:wide] = left.astype(bf16)
        out_ref[index, 0:rows, wide:] = right.astype(bf16)
        out_ref[index, rows:, :] = low.astype(bf16)


def grad_weight(dp, tokens, grad, one, mixture, up_row, vectors, more, starts):
    model, length = tokens.shape
    wide, group = grad.shape[0], mixture.shape[0]
    return pl.pallas_call(
        functools.partial(grad_weight_kernel, starts=starts),
        out_shape=jax.ShapeDtypeStruct((dp, model // dp + TAIL, wide + group), bf16),
        in_specs=[VMEM] * (6 + len(more)),
        out_specs=VMEM,
        compiler_params=pltpu.CompilerParams(vmem_limit_bytes=ATTEND_ROOM),
        cost_estimate=pl.CostEstimate(
            flops=2 * length * model * (wide + group),
            bytes_accessed=2 * (length + model) * (wide + group + model),
            transcendentals=0,
        ),
        name="grad_weight",
    )(tokens, grad, one, mixture, up_row, vectors, *more)


def normalize(values):
    average = jnp.mean(values, axis=-1, keepdims=True)
    centred = values - average
    variance = jnp.mean(centred * centred, axis=-1, keepdims=True)
    inv_scale = lax.rsqrt(variance + epsilon)
    return centred * inv_scale, inv_scale


def normalize_back(grad_out, unit_rows, inv_scale, norm_gain):
    grad_unit = grad_out * norm_gain
    middle = grad_unit - jnp.mean(grad_unit, axis=-1, keepdims=True)
    middle = middle - unit_rows * jnp.mean(grad_unit * unit_rows, axis=-1, keepdims=True)
    return inv_scale * middle


def gelu_parts(up_pre):
    normal_cdf = 0.5 * (1.0 + lax.erf(up_pre * root_half))
    return (
        up_pre * normal_cdf,
        normal_cdf + up_pre * inv_root_tau * jnp.exp(-0.5 * up_pre * up_pre),
    )


def tile_kernel(*refs, kernel, steps, tiles):
    def step(index, _):
        views = []
        for ref, tile in zip(refs, tiles):
            if tile is None or steps == 1:
                views.append(ref)
                continue
            size = ref.shape[tile] // steps
            own = pl.ds(pl.multiple_of(index * size, size), size)
            views.append(ref.at[own, :] if tile == 0 else ref.at[:, own])
        kernel(index, *views)
        return 0

    lax.fori_loop(0, steps, step, 0)


def tiled(kernel, name, steps, operands, tiles, shapes, flops):
    shapes, out_tiles = [x for x, _ in shapes], [x for _, x in shapes]
    moved = sum(x.size * x.dtype.itemsize for x in list(operands) + shapes)
    return pl.pallas_call(
        functools.partial(
            tile_kernel, kernel=kernel, steps=steps, tiles=tuple(tiles) + tuple(out_tiles)
        ),
        out_shape=shapes,
        in_specs=[VMEM] * len(operands),
        out_specs=[VMEM] * len(shapes),
        compiler_params=pltpu.CompilerParams(vmem_limit_bytes=TILE_ROOM),
        cost_estimate=pl.CostEstimate(flops=flops, bytes_accessed=moved, transcendentals=0),
        name=name,
    )(*operands)


def shape(*size, dtype=f32):
    return jax.ShapeDtypeStruct(size, dtype)


def vectors_kernel(step, lane_ref, near_ref, far_ref, out_ref):
    model = out_ref.shape[1]
    wide = near_ref.shape[1]
    size = wide // 2
    total = jnp.zeros((SIDE, model), f32)
    lanes = lax.broadcasted_iota(jnp.int32, (size, model), 1)
    for j in range(4):
        held = near_ref if j % 2 == 0 else far_ref
        first = (j // 2) * 3 * size
        place = jnp.where(lanes == lane_ref[:, j : j + 1], 1.0, 0.0).astype(bf16)
        for part in range(3):
            at = first + part * size
            line = model + at // wide * SIDE
            part = held[line : line + SIDE, at % wide : at % wide + size]
            total = total + contract(part, place, ((1,), (0,)))
    out_ref[...] = total


def out_kernel(step, m0, m1, m2, m3, near, far, vectors, tokens, low_ref, turned_ref, unit_ref, scale_ref):
    total = vectors[0:1, :] + tokens[...].astype(f32)
    model, group = total.shape[1], m0.shape[0]
    for index, mixture in enumerate((m0, m1, m2, m3)):
        held = near if index % 2 == 0 else far
        weight = held[0:model, index // 2 * group : (index // 2 + 1) * group]
        total = total + contract(mixture[...], weight, ((0,), (1,)))
    unit, scale = normalize(total)
    unit_ref[...] = unit
    scale_ref[...] = scale
    low = (unit * vectors[2:3, :] + vectors[3:4, :]).astype(bf16)
    low_ref[...] = low
    turned_ref[...] = low.T


def up_kernel(step, low, weight, act_ref, slope_ref):
    model = low.shape[1]
    up_pre = contract(low[...], weight[0:model, :], ((1,), (0,)))
    act, slope = gelu_parts(up_pre + weight[model : model + 1, :].astype(f32))
    act_ref[...] = act.astype(bf16)
    slope_ref[...] = slope.astype(bf16)


def column_sums(step, ref, rows, start=0.0):
    line = lax.broadcasted_iota(jnp.int32, ref.shape, 0)
    made = jnp.zeros(ref.shape, f32)
    for at, values in rows:
        made = made + jnp.where(line == at, jnp.sum(values, axis=0, keepdims=True), 0.0)

    @pl.when(step == 0)
    def _():
        ref[...] = made + start

    @pl.when(step > 0)
    def _():
        ref[...] += made


def down_kernel(
    step, a0, a1, a2, a3, w0, w1, w2, w3, vectors, unit_ref, cotangent, result_ref, grad_ref, low_ref, turned_ref, sums_ref
):
    total = vectors[1:2, :] + unit_ref[...] * vectors[2:3, :] + vectors[3:4, :]
    for act, weight in ((a0, w0), (a1, w1), (a2, w2), (a3, w3)):
        total = total + contract(act[...], weight[...], ((1,), (1,)))
    unit, scale = normalize(total)
    result_ref[...] = (unit * vectors[4:5, :] + vectors[5:6, :]).astype(bf16)
    grad_out = cotangent[...].astype(f32)
    grad = normalize_back(grad_out, unit, scale, vectors[4:5, :])
    grad_ref[...] = grad
    low_ref[...] = grad.astype(bf16)
    turned_ref[...] = grad.astype(bf16).T
    column_sums(step, sums_ref, ((1, grad), (4, grad_out * unit), (5, grad_out)))


def turn_kernel(step, rows, turned_ref):
    turned_ref[...] = rows[...].T


def outer_kernel(turned_ref, right_ref, *refs, added):
    outs = refs[added:]
    at = 0
    for out in outs:
        rows = slice(at, at + out.shape[0])
        made = contract(turned_ref[rows, :], right_ref[...], ((1,), (0,)))
        if added:
            made = made + refs[0][rows, :].astype(f32)
        out[...] = made.astype(bf16)
        at = at + out.shape[0]


def outer(turned, right, cuts=None, arrived=()):
    rows, columns = turned.shape[0], right.shape[1]
    cuts = cuts or [0, rows]
    shapes = [shape(high - low, columns, dtype=bf16) for low, high in zip(cuts, cuts[1:])]
    return pl.pallas_call(
        functools.partial(outer_kernel, added=len(arrived)),
        out_shape=shapes,
        in_specs=[VMEM] * (2 + len(arrived)),
        out_specs=[VMEM] * len(shapes),
        compiler_params=pltpu.CompilerParams(vmem_limit_bytes=TILE_ROOM),
        cost_estimate=pl.CostEstimate(
            flops=2 * turned.size * columns, bytes_accessed=6 * rows * columns, transcendentals=0
        ),
        name="outer",
    )(turned, right, *arrived)


def input_kernel(step, grad, weight, total, out_ref):
    model = total.shape[1]
    made = contract(grad[...], weight[0:model, :], ((0,), (1,)))
    out_ref[...] = (total[...] + made).astype(out_ref.dtype)


def down_end_kernel(own, far, out_ref):
    out_ref[...] = own[...] + far[...].astype(f32)


def slope_kernel(step, low, weight, slope, grad_ref, sums_ref):
    made = contract(low[...], weight[...], ((1,), (0,))) * slope[...].astype(f32)
    made = made.astype(bf16)
    grad_ref[...] = made
    column_sums(step, sums_ref, ((0, made.astype(f32)),))


def first_kernel(
    step, g0, g1, g2, g3, w0, w1, w2, w3, vectors, two, unit_ref, scale, sums_two, grad_ref, turned_ref, sums_ref
):
    total = two[...]
    model = total.shape[1]
    for grad, weight in ((g0, w0), (g1, w1), (g2, w2), (g3, w3)):
        total = total + contract(grad[...], weight[0:model, :], ((1,), (1,)))
    unit = unit_ref[...]
    grad = normalize_back(total, unit, scale[...], vectors[2:3, :])
    grad_ref[...] = grad
    turned_ref[...] = grad.astype(bf16).T
    column_sums(step, sums_ref, ((0, grad), (2, total * unit), (3, total)), sums_two[...])


def per_device(
    tokens,
    doc_lengths,
    w_query,
    w_key,
    w_value,
    w_out,
    w_up,
    w_down,
    b_query,
    b_value,
    b_up,
    b_out,
    b_down,
    gain_one,
    shift_one,
    gain_two,
    shift_two,
    cotangent,
):
    dp, tensor = lax.axis_size("dp"), lax.axis_size("tensor")
    length, model = tokens.shape
    rows = model // dp
    group = w_query.shape[1]
    links = Links(dp, tensor)
    swap = links.swap

    share = b_out.shape[0]
    me = links.me
    mine = lax.axis_index("tensor")
    hidden = w_up.shape[1]
    (packed,) = small_call(
        pack_kernel,
        "pack",
        links,
        [shape(rows + SIDE, 3 * group, dtype=bf16)],
        w_query,
        w_key,
        w_value,
        b_query,
        b_value,
        copied=True,
    )
    ring_attn = GatherRing(links, packed)
    zero = jnp.zeros((share,), f32)
    vectors = jnp.stack([b_out, b_down, gain_one, shift_one, gain_two, shift_two, zero, zero])

    ring_attn.step()
    late_out, late_down = small_call(
        pack_late_kernel,
        "pack_late",
        links,
        [shape(rows, group, dtype=bf16), shape(rows + SIDE, hidden, dtype=bf16)],
        w_out,
        w_down.T,
        vectors,
    )
    late = Box(late_out, late_down, doc_lengths)
    tie(ring_attn, late)
    late_out, late_down, early_lengths = late.live
    ring_attn.step()
    far_late = Box(swap(late_out, 2), swap(late_down, 2))
    span, window = documents(mine, early_lengths, length, BLOCK)
    done = Box(span)
    tie(ring_attn, done)
    span = done.live[0]
    ring_attn.step()
    tie(ring_attn)
    up_chunk, down_chunk = small_call(
        pack_up_kernel,
        "pack_up",
        links,
        [
            shape(rows + SIDE, 2 * group + hidden, dtype=bf16),
            shape(rows, 2 * hidden, dtype=bf16),
        ],
        late_out,
        far_late.live[0],
        w_up,
        late_down,
        far_late.live[1],
        b_up,
    )
    ring_up = GatherRing(links, up_chunk)
    ring_down = GatherRing(links, down_chunk)
    for _ in range(links.ahead - 3):
        ring_attn.step()
    (attn_own,) = ring_attn.full([(0, 3 * group, 0)], rows)

    attn_w = [attn_own, None, None, None]
    qkv, mixture, logs = [None] * 4, [None] * 4, [None] * 4

    def attend_group(j):
        mixture[j], logs[j], qkv[j] = attend(work.live[0], attn_w[j], window, span)
        return Box(mixture[j])

    work = Box(tokens, attn_own)
    tie(ring_attn, ring_up, work)
    attn_w[0] = work.live[1]
    work = Box(work.live[0])
    far = Box(swap(attn_w[0], 2))
    attn_w[1] = swap(attn_w[0], 1)
    ring_up.step()
    done = attend_group(0)
    tie(ring_up, work, done)
    ring_up.step()
    done = attend_group(1)
    tie(ring_up, work, done)
    ring_up.step()
    (tokens_turned,) = tiled(
        turn_kernel, "turn", 4, (work.live[0],), (0,), [(shape(model, length, dtype=bf16), 1)], 0
    )
    turned = Box(tokens_turned)
    tie(ring_up, work, far, turned)
    tokens_turned = turned.live[0]
    attn_w[2] = far.live[0]
    attn_w[3] = swap(attn_w[2], 1)
    for _ in range(links.ahead - 3):
        ring_up.step()
    done = attend_group(2)
    tie(ring_up, work, done, ring_down)
    ring_down.step()
    out_near, up_own = ring_up.full([(0, 2 * group, "all"), (2 * group, hidden, 6)], rows)
    out_far = swap(out_near, 1)
    cuts = [0, model // 3, 2 * model // 3, up_own.shape[0]]
    held, across_up = Box(up_own), []

    def up_across():
        low, high = cuts[len(across_up) : len(across_up) + 2]
        across_up.append(Box(swap(held.live[0][low:high], 2)))
        return across_up[-1]

    moved = up_across()
    done = attend_group(3)
    tie(ring_down, work, done, held, moved)

    ring_down.step()
    moved = up_across()
    count = np.arange(dp * share)
    base = jnp.asarray((count // share * tensor * share + count % share)[:, None], jnp.int32)
    lanes = base + (mine ^ jnp.arange(4, dtype=jnp.int32))[None, :] * share
    (vectors,) = tiled(
        vectors_kernel,
        "vectors",
        1,
        (lanes, out_near, out_far),
        (None,) * 3,
        [(shape(SIDE, model), None)],
        0,
    )
    up_w = [up_own, None, None, None]
    first_low, first_turned, unit_one, scale_one = tiled(
        out_kernel,
        "attention_out",
        4,
        (*mixture, out_near, out_far, vectors, work.live[0]),
        (1,) * 4 + (None,) * 3 + (0,),
        [
            (shape(length, model, dtype=bf16), 0),
            (shape(model, length, dtype=bf16), 1),
            (shape(length, model), 0),
            (shape(length, 1), 0),
        ],
        2 * length * model * model,
    )
    activated, slopes = [None] * 4, [None] * 4

    def up_group(j):
        activated[j], slopes[j] = tiled(
            up_kernel,
            "up",
            4,
            (work.live[0], up_w[j]),
            (0, None),
            [(shape(length, hidden, dtype=bf16), 0)] * 2,
            2 * length * model * hidden,
        )
        return Box(activated[j])

    work = Box(first_low)
    tie(ring_down, work, held, moved)
    up_w[0] = held.live[0]
    moved = up_across()
    up_w[1] = swap(up_w[0], 1)
    ring_down.step()
    done = up_group(0)
    tie(ring_down, work, done, moved)
    for _ in range(links.ahead - 3):
        ring_down.step()
    up_w[2] = jnp.concatenate([box.live[0] for box in across_up])
    up_w[3] = swap(up_w[2], 1)
    done = up_group(1)
    tie(ring_down, work, done)
    down_own, down_across = ring_down.full([(0, hidden, None), (hidden, hidden, None)], rows)
    down_w = [down_own, swap(down_own, 1), down_across, swap(down_across, 1)]
    done = [up_group(2), up_group(3)]
    result, grad_two, grad_two_low, grad_two_turned, sums_two = tiled(
        down_kernel,
        "down",
        4,
        (*activated, *down_w, vectors, unit_one, cotangent),
        (0,) * 4 + (None,) * 5 + (0,) * 2,
        [
            (shape(length, model, dtype=bf16), 0),
            (shape(length, model), 0),
            (shape(length, model, dtype=bf16), 0),
            (shape(model, length, dtype=bf16), 1),
            (shape(SIDE, model), None),
        ],
        8 * length * model * hidden,
    )
    work = Box(grad_two_low)

    def blocks(value):
        return value.reshape(-1, rows, value.shape[-1])

    def grad_down(j):
        return outer(grad_two_turned, activated[j])[0]

    def grad_w_up(j, cuts=None, arrived=()):
        return outer(first_turned, grad_up[j], cuts, arrived)

    grad_up, grad_bias_up = [None] * 4, [None] * 4

    def back_up(j):
        grad_up[j], grad_bias_up[j] = tiled(
            slope_kernel,
            "back_up",
            4,
            (work.live[0], down_w[j], slopes[j]),
            (0, None, 0),
            [(shape(length, hidden, dtype=bf16), 0), (shape(SIDE, hidden), None)],
            2 * length * model * hidden,
        )

    def cuts(total):
        return [0, total * 3 // 8, total * 5 // 8, total]

    sent = Box(grad_down(3), grad_down(1))
    tie(work, sent)
    three, one = (swap(v, 1) for v in sent.live)
    two, zero = grad_down(2), grad_down(0)
    back_up(3)
    three_up = Box(*grad_w_up(3))
    pair = Box(two, zero, three, one)
    tie(work, pair, three_up)
    two, zero, three, one = (blocks(v) for v in pair.live)
    sums_down = ScatterRing(links, [[zero, one], [two, three]])
    sums_down.step()
    three_up = Box(swap(three_up.live[0], 1))
    back_up(2)
    back_up(1)
    back_up(0)
    across = grad_w_up(2, cuts(model), (three_up.live[0],))
    across = Box(*across)
    tie(work, sums_down, across)
    across = across.live
    far_up = [Box(swap(across[0], 2))]
    kept = Box(*grad_w_up(1), *grad_w_up(0), grad_up[0])
    sums_down.step()
    grad_one, grad_one_turned, sums = tiled(
        first_kernel,
        "back_first",
        4,
        (*grad_up, *up_w, vectors, grad_two, unit_one, scale_one, sums_two),
        (0,) * 4 + (None,) * 5 + (0,) * 3 + (None,),
        [
            (shape(length, model), 0),
            (shape(model, length, dtype=bf16), 1),
            (shape(SIDE, model), None),
        ],
        8 * length * model * hidden,
    )
    work = Box(grad_one_turned)
    tie(work, kept, sums_down, far_up[0])
    one_up, zero_up, _ = kept.live
    one_up = Box(swap(one_up, 1))
    far_up.append(Box(swap(across[1], 2)))
    grad_qkv = [None] * 4

    def back_attention(j):
        grad_qkv[j] = attend_back(
            qkv[j],
            mixture[j],
            logs[j],
            out_near if j % 2 == 0 else out_far,
            j // 2,
            work.live[0],
            window,
            span,
        )
        return Box(grad_qkv[j])

    grad_input = Box(grad_one)

    def back_input(j):
        grad_input.live = tiled(
            input_kernel,
            "back_input",
            4,
            (grad_qkv[j], attn_w[j], grad_input.live[0]),
            (1, None, 0),
            [(shape(length, model, dtype=f32 if j else bf16), 0)],
            6 * length * model * group,
        )

    def back_group(j, arrived=(), starts=()):
        return grad_weight(
            dp,
            tokens_turned,
            grad_qkv[j],
            work.live[0],
            mixture[j],
            grad_bias_up[j],
            sums,
            arrived,
            starts,
        )

    sums_down.step()
    back_attention(3)
    three = Box(back_group(3))
    tie(work, three, one_up, far_up[1], sums_down)
    recv = Box(swap(three.live[0], 1))
    far_up.append(Box(swap(across[2], 2)))
    for _ in range(links.ahead - 3):
        sums_down.step()
    done = back_attention(2)
    tie(work, done, recv, far_up[2], sums_down)
    grad_qkv[2] = done.live[0]
    far = blocks(jnp.concatenate([box.live[0] for box in far_up]))
    sums_up = ScatterRing(links, [[blocks(zero_up), blocks(one_up.live[0]), far]])
    sums_up.step()
    down_total, down_far = sums_down.total()
    end_down = Box(swap(down_far, 2))
    two = Box(back_group(2, (recv.live[0],), (0,)))
    back_input(3)
    tie(work, two, sums_up, end_down, grad_input)
    split = cuts(dp)
    far_attn = [Box(swap(two.live[0][split[0] : split[1]], 2))]
    sums_up.step()
    done = back_attention(1)
    tie(work, done, sums_up, far_attn[0])
    grad_qkv[1] = done.live[0]
    far_attn.append(Box(swap(two.live[0][split[1] : split[2]], 2)))
    sums_up.step()
    one = Box(back_group(1))
    back_input(2)
    tie(work, one, far_attn[1], sums_up, grad_input)
    recv = Box(swap(one.live[0], 1))
    far_attn.append(Box(swap(two.live[0][split[2] :], 2)))
    for _ in range(links.ahead - 3):
        sums_up.step()
    done = back_attention(0)
    tie(work, done, recv, far_attn[2], sums_up)
    grad_qkv[0] = done.live[0]
    arrived = [recv.live[0]] + [box.live[0] for box in far_attn]
    (grad_down_own,) = pl.pallas_call(
        down_end_kernel,
        out_shape=[shape(rows, hidden)],
        in_specs=[VMEM] * 2,
        out_specs=[VMEM],
        compiler_params=pltpu.CompilerParams(vmem_limit_bytes=RING_ROOM),
        name="down_end",
    )(down_total, end_down.live[0])
    ends = Box(grad_down_own, *sums_up.total())
    zero = Box(back_group(0, arrived, (0, *split[:3])), grad_qkv[:2])
    tie(work, zero, ends)
    sums_attn = ScatterRing(links, [[zero.live[0]]])
    grad_qkv[:2] = zero.live[1]
    for j in (1, 0):
        sums_attn.step()
        back_input(j)
        tie(grad_input, sums_attn)
    while sums_attn.count < links.ahead:
        sums_attn.step()
    full = dp * b_query.shape[1]
    full_up = dp * b_up.shape[1]
    *made, held = finish(
        links,
        sums_attn,
        jnp.stack([me, me * tensor + mine]),
        [shape(rows, group)] * 3
        + [shape(group, rows)]
        + [shape(*table.shape) for table in (b_query, b_value, b_up)]
        + [shape(SIDE, share)],
        (
            (0, 0, b_query.shape[1], full),
            (0, 2 * group, b_value.shape[1], full),
            (1, 0, b_up.shape[1], full_up),
        ),
    )
    return (
        result,
        grad_input.live[0],
        *made[:4],
        ends.live[1],
        ends.live[0].T,
        *made[4:],
        *[held[i + 2] for i in range(6)],
    )


def solution(mesh):
    both = P(("dp", "tensor"))
    rows = P(("dp", "tensor"), None)
    down = P("tensor", "dp")
    wide = P("dp", "tensor")
    weights = (wide, wide, wide, down, wide, down, down, down, down)
    return jax.shard_map(
        per_device,
        mesh=mesh,
        in_specs=(rows, P("dp", None)) + weights + (both,) * 6 + (rows,),
        out_specs=(rows, rows) + weights + (both,) * 6,
        check_vma=False,
    )
```

```python
import functools

import jax
import jax.numpy as jnp
import numpy as np
from jax import lax
from jax.experimental import pallas as pl
from jax.experimental.pallas import tpu as pltpu
from jax.sharding import PartitionSpec as P

HD = 64
BLOCK = 256
EXTRA = 16
STEP = 128
SIDE = 8
RING_ROOM = 2 << 20
ATTEND_ROOM = 12 << 20
TILE_ROOM = 8 << 20
TAIL = 8

epsilon = 1e-06
root_half = 0.7071067811865476
inv_root_tau = 0.3989422804014327
masked_value = -1e30
bf16 = jnp.bfloat16
f32 = jnp.float32


def contract(a, b, dims, out=f32):
    return lax.dot_general(a, b, (dims, ((), ())), preferred_element_type=f32).astype(out)


def ring_order(size):
    return list(range(0, size, 2)) + list(range(size - 1, 0, -2)) if size > 1 else [0]


class Links:
    def __init__(self, dp, tensor):
        self.dp, self.tensor = dp, tensor
        order = ring_order(dp)
        self.forward = [(order[i], order[(i + 1) % dp]) for i in range(dp)]
        self.backward = [(b, a) for a, b in self.forward]
        self.me = lax.axis_index("dp")
        self.ahead = dp // 2
        self.behind = dp - 1 - self.ahead
        offsets = jnp.arange(-self.ahead, self.behind + 1, dtype=jnp.int32)
        half = lax.shift_right_logical(self.me, 1)
        position = jnp.where((self.me & 1) == 0, half, dp - 1 - half)
        place = position + offsets
        place = jnp.where(place < 0, place + dp, jnp.where(place < dp, place, place - dp))
        self.members = jnp.where(place < (dp + 1) // 2, 2 * place, 2 * (dp - 1 - place) + 1)

    def swap(self, value, mask):
        return lax.ppermute(value, "tensor", [(i, i ^ mask) for i in range(self.tensor)])


def tie(*holders):
    flat, tree = jax.tree.flatten([holder.live for holder in holders])
    flat = lax.optimization_barrier(tuple(flat))
    for holder, live in zip(holders, jax.tree.unflatten(tree, flat)):
        holder.live = live


class Box:
    def __init__(self, *live):
        self.live = list(live)


class GatherRing:
    def __init__(self, links, value):
        self.links = links
        self.live = [value, value]
        self.pieces = {0: value}
        self.count = 0

    def step(self):
        links = self.links
        self.count += 1
        up, down = self.live
        half = up.shape[0] // 32 * 16
        if self.count == links.ahead and half:
            up, down = up[:half], down[half:]
            up = lax.ppermute(up, "dp", links.forward)
            self.live = [up, lax.ppermute(down, "dp", links.backward)]
            return
        up = lax.ppermute(up, "dp", links.forward)
        self.pieces[-self.count] = up
        if self.count <= links.behind:
            down = lax.ppermute(down, "dp", links.backward)
            self.pieces[self.count] = down
        self.live = [up, down]

    def full(self, plan, rows):
        links = self.links
        pieces = [self.pieces[offset] for offset in range(1 - links.ahead, links.behind + 1)]
        halves = self.live if self.live[0].shape[0] < self.pieces[0].shape[0] else self.live[:1]
        return assemble(links.members, halves + pieces, plan, rows)


class ScatterRing:
    def __init__(self, links, groups):
        self.links = links
        self.groups = groups
        self.count = 0
        self.live = ring_call(links, groups, (links.ahead, -links.ahead), (), bf16, first=True)

    def step(self):
        links = self.links
        self.count += 1
        up, down = self.live
        up = lax.ppermute(up, "dp", links.forward)
        down = lax.ppermute(down, "dp", links.backward)
        left = links.ahead - self.count
        if left:
            up, down = ring_call(links, self.groups, (left, -left), (up, down), bf16)
        self.live = [up, down]

    def total(self):
        sources, counts, rows, _ = flatten(self.groups)
        widths = [group[0].shape[2] for group in self.groups]
        return pl.pallas_call(
            functools.partial(total_kernel, counts=counts, place=self.links.ahead),
            out_shape=[
                jax.ShapeDtypeStruct((rows, width), f32 if index == 0 else bf16)
                for index, width in enumerate(widths)
            ],
            in_specs=[SMEM] + [VMEM] * (len(sources) + 2),
            out_specs=[VMEM] * len(widths),
            compiler_params=pltpu.CompilerParams(vmem_limit_bytes=RING_ROOM),
            name="ring_total",
        )(self.links.members, *sources, *self.live)


VMEM = pl.BlockSpec(memory_space=pltpu.VMEM)
SMEM = pl.BlockSpec(memory_space=pltpu.SMEM)


def block_of(sources, member):
    if len(sources) == 1:
        return sources[0][member].astype(f32)
    low, high = sources
    half = low.shape[0]
    lower = low[jnp.minimum(member, half - 1)].astype(f32)
    return jnp.where(member < half, lower, high[jnp.maximum(member - half, 0)].astype(f32))


def ring_sums(members_ref, refs, counts, place):
    member = members_ref[place]
    at = 0
    for count in counts:
        total = None
        for pieces in count:
            made = block_of(refs[at : at + pieces], member)
            total = made if total is None else total + made
            at += pieces
        yield total


def ring_kernel(members_ref, *refs, counts, places, dtype, first):
    size, sends = sum(map(sum, counts)), len(places)
    sources, arrived, outs = refs[:size], refs[size:-sends], refs[-sends:]
    for index, place in enumerate(places):
        column = 0
        out = outs[index]
        mine = arrived if sends == 1 else arrived[index : index + 1]
        for made in ring_sums(members_ref, sources, counts, place):
            rows, width = made.shape
            own = slice(column, column + width)
            column += width
            if first:
                half = out.shape[0]
                out[:, own] = (made[:half] if index == 0 else made[rows - half :]).astype(dtype)
                continue
            whole = [one for one in mine if one.shape[0] == rows]
            for one in whole:
                made = made + one[:, own].astype(f32)
            out[:, own] = made.astype(dtype)
            for one in mine:
                if one.shape[0] < rows:
                    half = one.shape[0]
                    part = slice(0, half) if index == 0 else slice(rows - half, rows)
                    out[part, own] = (made[part] + one[:, own].astype(f32)).astype(dtype)


def total_kernel(members_ref, *refs, counts, place):
    size = sum(map(sum, counts))
    sources, arrived, outs = refs[:size], refs[size : size + 2], refs[size + 2 :]
    column = 0
    for out, made in zip(outs, ring_sums(members_ref, sources, counts, place)):
        own = slice(column, column + out.shape[1])
        for one in arrived:
            made = made + one[:, own].astype(f32)
        out[...] = made.astype(out.dtype)
        column += out.shape[1]


def flatten(groups):
    sources, counts = [], []
    for group in groups:
        pieces = [one if isinstance(one, (list, tuple)) else [one] for one in group]
        counts.append([len(one) for one in pieces])
        sources += [part for one in pieces for part in one]
    widths = [(group[0][0] if isinstance(group[0], (list, tuple)) else group[0]).shape for group in groups]
    return sources, counts, widths[0][1], sum(width[2] for width in widths)


def ring_call(links, groups, offsets, arrived, dtype, first=False):
    sources, counts, rows, columns = flatten(groups)
    size = rows * columns
    return list(
        pl.pallas_call(
            functools.partial(
                ring_kernel,
                counts=counts,
                places=[(offset + links.ahead) % links.dp for offset in offsets],
                dtype=dtype,
                first=first,
            ),
            out_shape=[
                jax.ShapeDtypeStruct((rows // 2 if first else rows, columns), dtype) for _ in offsets
            ],
            in_specs=[SMEM] + [VMEM] * (len(sources) + len(arrived)),
            out_specs=[VMEM] * len(offsets),
            compiler_params=pltpu.CompilerParams(vmem_limit_bytes=RING_ROOM),
            cost_estimate=pl.CostEstimate(
                flops=size * 2, bytes_accessed=6 * size * len(offsets), transcendentals=0
            ),
            name="ring_sum",
        )(links.members, *sources, *arrived)
    )


def finish_kernel(
    members_ref, me_ref, *refs, counts, place, tables
):
    size = sum(map(sum, counts))
    sources, arrived, outs = refs[:size], refs[size : size + 2], refs[size + 2 :]
    (total,) = ring_sums(members_ref, sources, counts, place)
    for one in arrived:
        total = total + one[...].astype(f32)
    rows, group = outs[0].shape
    for index in range(3):
        outs[index][...] = total[:rows, index * group : (index + 1) * group]
    outs[3][...] = total[:rows, 3 * group :].T
    side = total[rows:]
    wide = side.shape[1]
    for out, (line, at, per, full) in zip(outs[4:7], tables):
        turned = pltpu.roll(side, wide - me_ref[0] * per, axis=1)
        for row in range(out.shape[0]):
            start = at + row * full
            out[row : row + 1, :] = turned[line : line + 1, start : start + per]
    share = outs[7].shape[1]
    turned = pltpu.roll(side, wide - me_ref[1] * share, axis=1)
    outs[7][...] = turned[:, 0:share]


def finish(links, ring, places, shapes, tables):
    sources, counts, _, _ = flatten(ring.groups)
    return pl.pallas_call(
        functools.partial(finish_kernel, counts=counts, place=links.ahead, tables=tables),
        out_shape=shapes,
        in_specs=[SMEM] * 2 + [VMEM] * (len(sources) + 2),
        out_specs=[VMEM] * len(shapes),
        compiler_params=pltpu.CompilerParams(vmem_limit_bytes=RING_ROOM),
        name="finish",
    )(links.members, places, *sources, *ring.live)


def assemble_kernel(members_ref, *refs, count, total_rows, plan, rows):
    pieces, outs = refs[:count], refs[count:]
    total, index, done = None, 0, 0
    blocks = 0
    for piece in pieces:
        first = members_ref[index] * rows + done
        own = min(piece.shape[0], rows - done)
        for out, (at, width, _) in zip(outs, plan):
            out[pl.ds(pl.multiple_of(first, 16), own), :] = piece[0:own, at : at + width]
        done += piece.shape[0]
        if done == total_rows:
            if total_rows > rows:
                side = piece[own:, :].astype(f32)
                total = side if total is None else total + side
            index, done, blocks = index + 1, 0, blocks + 1
    for out, (at, width, kept) in zip(outs, plan):
        if kept == "all":
            for index in range(3):
                first = blocks * rows + index * SIDE
                out[first : first + SIDE, :] = total[:, index * width : (index + 1) * width].astype(bf16)
        elif kept is not None:
            out[blocks * rows :, :] = jnp.broadcast_to(
                total[kept : kept + 1, at : at + width], (SIDE, width)
            ).astype(bf16)


def assemble(members, pieces, plan, rows):
    count = members.shape[0]
    full, wide = pieces[-1].shape
    if rows % 16:
        if len(pieces) > count:
            pieces = [jnp.concatenate(pieces[:2])] + pieces[2:]
        stacked = jnp.stack(pieces)
        back = jnp.zeros((count,), jnp.int32).at[members].set(jnp.arange(count, dtype=jnp.int32))
        stacked = jnp.take(stacked, back, axis=0)
        weights = stacked[:, :rows].reshape(count * rows, -1)
        total = jnp.sum(stacked[:, rows:].astype(f32), axis=0)
        outs = []
        for at, width, kept in plan:
            out = weights[:, at : at + width]
            if kept == "all":
                parts = [total[:, i * width : (i + 1) * width].astype(bf16) for i in range(3)]
                out = jnp.concatenate([out] + parts)
            elif kept is not None:
                row = jnp.broadcast_to(total[kept : kept + 1, at : at + width], (SIDE, width))
                out = jnp.concatenate([out, row.astype(bf16)])
            outs.append(out)
        return outs
    shapes = [
        jax.ShapeDtypeStruct(
            (count * rows + SIDE * {None: 0, "all": 3}.get(kept, 1), width), bf16
        )
        for _, width, kept in plan
    ]
    return pl.pallas_call(
        functools.partial(
            assemble_kernel, count=len(pieces), total_rows=full, plan=plan, rows=rows
        ),
        out_shape=shapes,
        in_specs=[SMEM] + [VMEM] * len(pieces),
        out_specs=[VMEM] * len(shapes),
        compiler_params=pltpu.CompilerParams(vmem_limit_bytes=RING_ROOM),
        cost_estimate=pl.CostEstimate(
            flops=0, bytes_accessed=4 * count * full * wide, transcendentals=0
        ),
        name="assemble",
    )(members, *pieces)


def one_hot(first, rows, size):
    hit = lax.broadcasted_iota(jnp.int32, (rows, size), 1) == (
        lax.broadcasted_iota(jnp.int32, (rows, size), 0) + first
    )
    return jnp.where(hit, 1.0, 0.0).astype(bf16)


def placed(table, me, dp):
    count, per = table.shape
    spread = contract(table, one_hot(me * per, per, per * dp), ((1,), (0,)))
    return [spread[row : row + 1] for row in range(count)]


def only_row(row, at):
    line = lax.broadcasted_iota(jnp.int32, (SIDE, row.shape[1]), 0)
    return jnp.where(line == at, row, 0.0)


def pack_kernel(me_ref, *refs, dp):
    sources, out_ref, held, sems = refs[:5], refs[5], refs[6:11], refs[11]
    copies = [
        pltpu.make_async_copy(source, target, sems.at[index])
        for index, (source, target) in enumerate(zip(sources, held))
    ]
    for copy in copies:
        copy.start()
    for copy in copies:
        copy.wait()
    query_ref, key_ref, value_ref, b_query_ref, b_value_ref = held
    rows, group = query_ref.shape
    out_ref[0:rows, 0:group] = query_ref[...]
    out_ref[0:rows, group : 2 * group] = key_ref[...]
    out_ref[0:rows, 2 * group :] = value_ref[...]
    me = me_ref[0]
    row = jnp.concatenate(
        placed(b_query_ref[...], me, dp)
        + [jnp.zeros((1, group), f32)]
        + placed(b_value_ref[...], me, dp),
        axis=1,
    )
    out_ref[rows:, :] = only_row(row, 0).astype(bf16)


def pack_late_kernel(me_ref, w_out_ref, w_down_ref, vectors_ref, out_ref, down_ref, *, dp):
    rows, hidden = w_down_ref.shape
    out_ref[...] = w_out_ref[...].T
    down_ref[0:rows, :] = w_down_ref[...]
    left = vectors_ref[...]
    share = left.shape[1]
    place = one_hot(me_ref[0] * share, share, share * dp)
    spread = []
    for _ in range(3):
        part = left.astype(bf16)
        left = left - part.astype(f32)
        spread.append(contract(part, place, ((1,), (0,))))
    row = jnp.concatenate(spread, axis=1)
    blank = jnp.zeros((SIDE, hidden - row.shape[1]), f32)
    down_ref[rows:, :] = jnp.concatenate([row, blank], axis=1).astype(bf16)


def pack_up_kernel(
    me_ref, out_ref, far_out_ref, w_up_ref, down_ref, far_down_ref, b_up_ref, up_ref, pair_ref, *, dp
):
    rows, hidden = w_up_ref.shape
    group = out_ref.shape[1]
    up_ref[0:rows, 0:group] = out_ref[...]
    up_ref[0:rows, group : 2 * group] = far_out_ref[...]
    up_ref[0:rows, 2 * group :] = w_up_ref[...]
    pair_ref[:, 0:hidden] = down_ref[0:rows, :]
    pair_ref[:, hidden:] = far_down_ref[0:rows, :]
    near = down_ref[rows:, 0 : 3 * group].astype(f32)
    far = far_down_ref[rows:, 0 : 3 * group].astype(f32)
    bias = jnp.concatenate(
        [jnp.zeros((1, 2 * group), f32)] + placed(b_up_ref[...], me_ref[0], dp), axis=1
    )
    side = jnp.concatenate([near, far], axis=1) + only_row(bias, 6)
    up_ref[rows:, :] = side.astype(bf16)


def small_call(kernel, name, links, shapes, *operands, copied=False):
    place = pl.BlockSpec(memory_space=pltpu.HBM) if copied else VMEM
    scratch = []
    if copied:
        operands = [pltpu.with_memory_space_constraint(x, pltpu.HBM) for x in operands]
        scratch = [pltpu.VMEM(x.shape, x.dtype) for x in operands]
        scratch.append(pltpu.SemaphoreType.DMA((len(operands),)))
    return pl.pallas_call(
        functools.partial(kernel, dp=links.dp),
        out_shape=shapes,
        in_specs=[SMEM] + [place] * len(operands),
        out_specs=[VMEM] * len(shapes),
        scratch_shapes=scratch,
        compiler_params=pltpu.CompilerParams(vmem_limit_bytes=RING_ROOM),
        name=name,
    )(links.me.reshape(1), *operands)


def documents_kernel(mine_ref, lengths_ref, span_ref, window_ref, *, block):
    length = span_ref.shape[1]
    count = length // block
    place = lax.broadcasted_iota(jnp.int32, (1, length), 1)
    low = high = jnp.zeros((1, length), jnp.int32)
    begins, ends = [jnp.int32(0)] * count, [jnp.int32(0)] * count
    start = jnp.int32(0)
    for document in range(lengths_ref.shape[1]):
        end = start + lengths_ref[mine_ref[0], document]
        inside = (place >= start) & (place < end)
        low, high = jnp.where(inside, start, low), jnp.where(inside, end, high)
        for index in range(count):
            first, last = index * block, (index + 1) * block - 1
            begins[index] = jnp.where((start <= first) & (first < end), start, begins[index])
            ends[index] = jnp.where((start <= last) & (last < end), end, ends[index])
        start = end
    span_ref[0:1, :] = low
    span_ref[1:2, :] = high
    for index in range(count):
        begin = lax.div(begins[index], jnp.int32(STEP)) * STEP
        window_ref[0, index] = begin
        window_ref[1, index] = lax.div(ends[index] - begin + (STEP - 1), jnp.int32(STEP))


def documents(mine, lengths, length, block):
    return pl.pallas_call(
        functools.partial(documents_kernel, block=block),
        out_shape=[
            jax.ShapeDtypeStruct((2, length), jnp.int32),
            jax.ShapeDtypeStruct((2, length // block), jnp.int32),
        ],
        in_specs=[SMEM, SMEM],
        out_specs=[VMEM, SMEM],
        compiler_params=pltpu.CompilerParams(vmem_limit_bytes=RING_ROOM),
        name="documents",
    )(mine.reshape(1), lengths)


def fill_bias(bias, begin, low, high, size):
    keys = lax.broadcasted_iota(jnp.int32, (size, low.shape[1]), 0) + begin
    bias[0:size, :] = jnp.where((keys >= low) & (keys < high), 0.0, masked_value)


def attend_kernel(
    window_ref, tokens_ref, weight_ref, span_ref, out_ref, log_ref, qkv_ref, keys, values, bias, hold, *, block
):
    length = qkv_ref.shape[1]
    heads = qkv_ref.shape[0] // (3 * HD)
    width = heads * HD
    model = tokens_ref.shape[1]
    made = contract(tokens_ref[...], weight_ref[0:model, :], ((1,), (0,)))
    made = made + weight_ref[model : model + 1, :].astype(f32)
    qkv_ref[...] = made.astype(bf16).T
    tail = jnp.where(lax.broadcasted_iota(jnp.int32, (EXTRA, length), 0) == 0, 1.0, 0.0).astype(bf16)
    for head in range(heads):
        keys[head] = qkv_ref[width + head * HD : width + (head + 1) * HD, :].T
        values[head, 0:HD, :] = qkv_ref[2 * width + head * HD : 2 * width + (head + 1) * HD, :]
        values[head, HD : HD + EXTRA, :] = tail

    def one_block(index, _):
        lanes = pl.ds(pl.multiple_of(index * block, block), block)
        begin = pl.multiple_of(window_ref[0, index], STEP)

        def with_count(count):
            fill_bias(bias, begin, span_ref[0:1, lanes], span_ref[1:2, lanes], count * STEP)
            parts = [(at, min(block, count * STEP - at)) for at in range(0, count * STEP, block)]
            tops = []
            for head in range(heads):
                queries = qkv_ref[head * HD : (head + 1) * HD, lanes] * 0.125
                top = None
                for at, size in parts:
                    own = pl.ds(begin + at, size)
                    scores = contract(keys[head, own, :], queries, ((1,), (0,))) + bias[at : at + size, :]
                    hold[head, at : at + size, :] = scores
                    most = jnp.max(scores.reshape(size // 8, 8, block), axis=0)
                    top = most if top is None else jnp.maximum(top, most)
                tops.append(jnp.max(top, axis=0, keepdims=True))
            for head in range(heads):
                total = None
                for at, size in parts:
                    own = pl.ds(begin + at, size)
                    weights = jnp.exp(hold[head, at : at + size, :] - tops[head]).astype(bf16)
                    made = contract(values[head, :, own], weights, ((1,), (0,)))
                    total = made if total is None else total + made
                mass = total[HD : HD + 1, :]
                out_ref[head * HD : (head + 1) * HD, lanes] = (total[:HD] / mass).astype(bf16)
                log_ref[head : head + 1, lanes] = tops[head] + jnp.log(mass)

        for count in range(1, length // STEP + 1):
            pl.when(window_ref[1, index] == count)(functools.partial(with_count, count))
        return 0

    lax.fori_loop(0, length // block, one_block, 0)


def attend_back_kernel(
    window_ref, half_ref, qkv_ref, span_ref, out_ref, log_ref, weight_ref, one_ref, result_ref, keys, values, bias, grad_key, grad_value, grad_ref, weight, *, block
):
    length = qkv_ref.shape[1]
    model = one_ref.shape[0]
    group = grad_ref.shape[0]
    for half in range(2):

        @pl.when(half_ref[0] == half)
        def _():
            weight[...] = weight_ref[0:model, half * group : (half + 1) * group]

    grad_ref[...] = contract(weight[...], one_ref[...], ((0,), (0,)), bf16)
    heads = qkv_ref.shape[0] // (3 * HD)
    width = heads * HD
    for head in range(heads):
        keys[head] = qkv_ref[width + head * HD : width + (head + 1) * HD, :].T
        values[head] = qkv_ref[2 * width + head * HD : 2 * width + (head + 1) * HD, :].T
    grad_key[...] = jnp.zeros_like(grad_key)
    grad_value[...] = jnp.zeros_like(grad_value)

    def one_block(index, _):
        lanes = pl.ds(pl.multiple_of(index * block, block), block)
        begin = pl.multiple_of(window_ref[0, index], STEP)

        def with_count(count):
            size = count * STEP
            window = pl.ds(begin, size)
            fill_bias(bias, begin, span_ref[0:1, lanes], span_ref[1:2, lanes], size)
            owns = [slice(head * HD, (head + 1) * HD) for head in range(heads)]
            queries = [qkv_ref[own, lanes] * 0.125 for own in owns]
            grads = [grad_ref[own, lanes] for own in owns]
            deltas = [
                jnp.sum(out_ref[own, lanes].astype(f32) * grad.astype(f32), axis=0, keepdims=True)
                for own, grad in zip(owns, grads)
            ]
            made = [None] * heads
            for at in range(0, size, block):
                step = min(block, size - at)
                part = pl.ds(begin + at, step)
                raw = []
                for head in range(heads):
                    scores = contract(keys[head, part, :], queries[head], ((1,), (0,)))
                    grad_prob = contract(values[head, part, :], grads[head], ((1,), (0,)))
                    raw.append((scores + bias[at : at + step, :], grad_prob))
                both = []
                for head, (scores, grad_prob) in enumerate(raw):
                    weights = jnp.exp(scores - log_ref[head : head + 1, lanes])
                    both.append((weights.astype(bf16), (weights * (grad_prob - deltas[head])).astype(bf16)))
                for head, (weights, grad_scores) in enumerate(both):
                    own = owns[head]
                    grad_value[own, part] += contract(grads[head], weights, ((1,), (1,)))
                    grad_key[own, part] += contract(queries[head], grad_scores, ((1,), (1,)))
                    key_cols = qkv_ref[width + head * HD : width + (head + 1) * HD, part]
                    more = contract(key_cols, grad_scores, ((1,), (0,)))
                    made[head] = more if made[head] is None else made[head] + more
            for head, own in enumerate(owns):
                result_ref[own, lanes] = (made[head] * 0.125).astype(bf16)

        for count in range(1, length // STEP + 1):
            pl.when(window_ref[1, index] == count)(functools.partial(with_count, count))
        return 0

    lax.fori_loop(0, length // block, one_block, 0)
    result_ref[width : 2 * width, :] = grad_key[...].astype(bf16)
    result_ref[2 * width :, :] = grad_value[...].astype(bf16)


def attend(tokens, weight, window, span):
    length, model = tokens.shape
    width = weight.shape[1]
    heads = width // (3 * HD)
    return pl.pallas_call(
        functools.partial(attend_kernel, block=BLOCK),
        out_shape=(
            jax.ShapeDtypeStruct((heads * HD, length), bf16),
            jax.ShapeDtypeStruct((8, length), f32),
            jax.ShapeDtypeStruct((width, length), bf16),
        ),
        in_specs=[SMEM] + [VMEM] * 3,
        out_specs=(VMEM,) * 3,
        scratch_shapes=[
            pltpu.VMEM((heads, length, HD), bf16),
            pltpu.VMEM((heads, HD + EXTRA, length), bf16),
            pltpu.VMEM((length, BLOCK), f32),
            pltpu.VMEM((heads, length, BLOCK), f32),
        ],
        compiler_params=pltpu.CompilerParams(vmem_limit_bytes=ATTEND_ROOM),
        cost_estimate=pl.CostEstimate(
            flops=4 * heads * length * length * HD + 2 * length * model * width,
            bytes_accessed=4 * width * length,
            transcendentals=heads * length * length,
        ),
        name="attend",
    )(window, tokens, weight, span)


def attend_back(qkv, out, logs, weight, half, one, window, span):
    width, length = qkv.shape
    heads = width // (3 * HD)
    return pl.pallas_call(
        functools.partial(attend_back_kernel, block=BLOCK),
        out_shape=jax.ShapeDtypeStruct((width, length), bf16),
        in_specs=[SMEM] * 2 + [VMEM] * 6,
        out_specs=VMEM,
        scratch_shapes=[
            pltpu.VMEM((heads, length, HD), bf16),
            pltpu.VMEM((heads, length, HD), bf16),
            pltpu.VMEM((length, BLOCK), f32),
            pltpu.VMEM((heads * HD, length), f32),
            pltpu.VMEM((heads * HD, length), f32),
            pltpu.VMEM((heads * HD, length), bf16),
            pltpu.VMEM((one.shape[0], heads * HD), bf16),
        ],
        compiler_params=pltpu.CompilerParams(vmem_limit_bytes=ATTEND_ROOM),
        cost_estimate=pl.CostEstimate(
            flops=10 * heads * length * length * HD,
            bytes_accessed=6 * width * length,
            transcendentals=heads * length * length,
        ),
        name="attend_back",
    )(window, jnp.full((1,), half, jnp.int32), qkv, span, out, logs, weight, one)


def grad_weight_kernel(tokens_ref, grad_ref, one_ref, mixture_ref, *refs, starts):
    more, out_ref = refs[2:-1], refs[-1]
    up_ref, vectors_ref = refs[0], refs[1]
    dp, full, columns = out_ref.shape
    rows = full - TAIL
    wide = grad_ref.shape[0]
    group = wide // 3
    made = contract(tokens_ref[...], grad_ref[...], ((1,), (1,)))
    out_low = contract(one_ref[...], mixture_ref[...], ((1,), (1,)))
    ones = jnp.ones((TAIL, grad_ref.shape[1]), bf16)
    lane = contract(ones, grad_ref[...], ((1,), (1,)))
    line = lax.broadcasted_iota(jnp.int32, (TAIL, columns), 0)
    bias_row = jnp.concatenate([lane, jnp.zeros((TAIL, columns - wide), f32)], axis=1)
    side = jnp.where(line == 0, bias_row, 0.0) + jnp.where(line == 1, up_ref[0:1, :], 0.0)
    lower = jnp.concatenate([jnp.zeros((2, columns), f32), vectors_ref[0:6, :]], axis=0)
    side = side + lower
    for index in range(dp):
        own = slice(index * rows, (index + 1) * rows)
        left, right, low = made[own], out_low[own], side
        for held, start in zip(more, starts):
            at = index - start
            if not 0 <= at < held.shape[0]:
                continue
            left = left + held[at, 0:rows, 0:wide].astype(f32)
            right = right + held[at, 0:rows, wide:].astype(f32)
            low = low + held[at, rows:, :].astype(f32)
        out_ref[index, 0:rows, 0:wide] = left.astype(bf16)
        out_ref[index, 0:rows, wide:] = right.astype(bf16)
        out_ref[index, rows:, :] = low.astype(bf16)


def grad_weight(dp, tokens, grad, one, mixture, up_row, vectors, more, starts):
    model, length = tokens.shape
    wide, group = grad.shape[0], mixture.shape[0]
    return pl.pallas_call(
        functools.partial(grad_weight_kernel, starts=starts),
        out_shape=jax.ShapeDtypeStruct((dp, model // dp + TAIL, wide + group), bf16),
        in_specs=[VMEM] * (6 + len(more)),
        out_specs=VMEM,
        compiler_params=pltpu.CompilerParams(vmem_limit_bytes=ATTEND_ROOM),
        cost_estimate=pl.CostEstimate(
            flops=2 * length * model * (wide + group),
            bytes_accessed=2 * (length + model) * (wide + group + model),
            transcendentals=0,
        ),
        name="grad_weight",
    )(tokens, grad, one, mixture, up_row, vectors, *more)


def normalize(values):
    average = jnp.mean(values, axis=-1, keepdims=True)
    centred = values - average
    variance = jnp.mean(centred * centred, axis=-1, keepdims=True)
    inv_scale = lax.rsqrt(variance + epsilon)
    return centred * inv_scale, inv_scale


def normalize_back(grad_out, unit_rows, inv_scale, norm_gain):
    grad_unit = grad_out * norm_gain
    middle = grad_unit - jnp.mean(grad_unit, axis=-1, keepdims=True)
    middle = middle - unit_rows * jnp.mean(grad_unit * unit_rows, axis=-1, keepdims=True)
    return inv_scale * middle


def gelu_parts(up_pre):
    normal_cdf = 0.5 * (1.0 + lax.erf(up_pre * root_half))
    return (
        up_pre * normal_cdf,
        normal_cdf + up_pre * inv_root_tau * jnp.exp(-0.5 * up_pre * up_pre),
    )


def tile_kernel(*refs, kernel, steps, tiles):
    def step(index, _):
        views = []
        for ref, tile in zip(refs, tiles):
            if tile is None or steps == 1:
                views.append(ref)
                continue
            size = ref.shape[tile] // steps
            own = pl.ds(pl.multiple_of(index * size, size), size)
            views.append(ref.at[own, :] if tile == 0 else ref.at[:, own])
        kernel(index, *views)
        return 0

    lax.fori_loop(0, steps, step, 0)


def tiled(kernel, name, steps, operands, tiles, shapes, flops):
    shapes, out_tiles = [x for x, _ in shapes], [x for _, x in shapes]
    moved = sum(x.size * x.dtype.itemsize for x in list(operands) + shapes)
    return pl.pallas_call(
        functools.partial(
            tile_kernel, kernel=kernel, steps=steps, tiles=tuple(tiles) + tuple(out_tiles)
        ),
        out_shape=shapes,
        in_specs=[VMEM] * len(operands),
        out_specs=[VMEM] * len(shapes),
        compiler_params=pltpu.CompilerParams(vmem_limit_bytes=TILE_ROOM),
        cost_estimate=pl.CostEstimate(flops=flops, bytes_accessed=moved, transcendentals=0),
        name=name,
    )(*operands)


def shape(*size, dtype=f32):
    return jax.ShapeDtypeStruct(size, dtype)


def vectors_kernel(step, lane_ref, near_ref, far_ref, out_ref):
    model = out_ref.shape[1]
    wide = near_ref.shape[1]
    size = wide // 2
    total = jnp.zeros((SIDE, model), f32)
    lanes = lax.broadcasted_iota(jnp.int32, (size, model), 1)
    for j in range(4):
        held = near_ref if j % 2 == 0 else far_ref
        first = (j // 2) * 3 * size
        place = jnp.where(lanes == lane_ref[:, j : j + 1], 1.0, 0.0).astype(bf16)
        for part in range(3):
            at = first + part * size
            line = model + at // wide * SIDE
            part = held[line : line + SIDE, at % wide : at % wide + size]
            total = total + contract(part, place, ((1,), (0,)))
    out_ref[...] = total


def out_kernel(step, m0, m1, m2, m3, near, far, vectors, tokens, low_ref, turned_ref, unit_ref, scale_ref):
    total = vectors[0:1, :] + tokens[...].astype(f32)
    model, group = total.shape[1], m0.shape[0]
    for index, mixture in enumerate((m0, m1, m2, m3)):
        held = near if index % 2 == 0 else far
        weight = held[0:model, index // 2 * group : (index // 2 + 1) * group]
        total = total + contract(mixture[...], weight, ((0,), (1,)))
    unit, scale = normalize(total)
    unit_ref[...] = unit
    scale_ref[...] = scale
    low = (unit * vectors[2:3, :] + vectors[3:4, :]).astype(bf16)
    low_ref[...] = low
    turned_ref[...] = low.T


def up_kernel(step, low, weight, act_ref, slope_ref):
    model = low.shape[1]
    up_pre = contract(low[...], weight[0:model, :], ((1,), (0,)))
    act, slope = gelu_parts(up_pre + weight[model : model + 1, :].astype(f32))
    act_ref[...] = act.astype(bf16)
    slope_ref[...] = slope.astype(bf16)


def column_sums(step, ref, rows, start=0.0):
    line = lax.broadcasted_iota(jnp.int32, ref.shape, 0)
    made = jnp.zeros(ref.shape, f32)
    for at, values in rows:
        made = made + jnp.where(line == at, jnp.sum(values, axis=0, keepdims=True), 0.0)

    @pl.when(step == 0)
    def _():
        ref[...] = made + start

    @pl.when(step > 0)
    def _():
        ref[...] += made


def down_kernel(
    step, a0, a1, a2, a3, w0, w1, w2, w3, vectors, unit_ref, cotangent, result_ref, grad_ref, low_ref, turned_ref, sums_ref
):
    total = vectors[1:2, :] + unit_ref[...] * vectors[2:3, :] + vectors[3:4, :]
    for act, weight in ((a0, w0), (a1, w1), (a2, w2), (a3, w3)):
        total = total + contract(act[...], weight[...], ((1,), (1,)))
    unit, scale = normalize(total)
    result_ref[...] = (unit * vectors[4:5, :] + vectors[5:6, :]).astype(bf16)
    grad_out = cotangent[...].astype(f32)
    grad = normalize_back(grad_out, unit, scale, vectors[4:5, :])
    grad_ref[...] = grad
    low_ref[...] = grad.astype(bf16)
    turned_ref[...] = grad.astype(bf16).T
    column_sums(step, sums_ref, ((1, grad), (4, grad_out * unit), (5, grad_out)))


def turn_kernel(step, rows, turned_ref):
    turned_ref[...] = rows[...].T


def outer_kernel(turned_ref, right_ref, *refs, added):
    outs = refs[added:]
    at = 0
    for out in outs:
        rows = slice(at, at + out.shape[0])
        made = contract(turned_ref[rows, :], right_ref[...], ((1,), (0,)))
        if added:
            made = made + refs[0][rows, :].astype(f32)
        out[...] = made.astype(bf16)
        at = at + out.shape[0]


def outer(turned, right, cuts=None, arrived=()):
    rows, columns = turned.shape[0], right.shape[1]
    cuts = cuts or [0, rows]
    shapes = [shape(high - low, columns, dtype=bf16) for low, high in zip(cuts, cuts[1:])]
    return pl.pallas_call(
        functools.partial(outer_kernel, added=len(arrived)),
        out_shape=shapes,
        in_specs=[VMEM] * (2 + len(arrived)),
        out_specs=[VMEM] * len(shapes),
        compiler_params=pltpu.CompilerParams(vmem_limit_bytes=TILE_ROOM),
        cost_estimate=pl.CostEstimate(
            flops=2 * turned.size * columns, bytes_accessed=6 * rows * columns, transcendentals=0
        ),
        name="outer",
    )(turned, right, *arrived)


def input_kernel(step, grad, weight, total, out_ref):
    model = total.shape[1]
    made = contract(grad[...], weight[0:model, :], ((0,), (1,)))
    out_ref[...] = (total[...] + made).astype(out_ref.dtype)


def down_end_kernel(own, far, out_ref):
    out_ref[...] = own[...] + far[...].astype(f32)


def slope_kernel(step, low, weight, slope, grad_ref, sums_ref):
    made = contract(low[...], weight[...], ((1,), (0,))) * slope[...].astype(f32)
    made = made.astype(bf16)
    grad_ref[...] = made
    column_sums(step, sums_ref, ((0, made.astype(f32)),))


def first_kernel(
    step, g0, g1, g2, g3, w0, w1, w2, w3, vectors, two, unit_ref, scale, sums_two, grad_ref, turned_ref, sums_ref
):
    total = two[...]
    model = total.shape[1]
    for grad, weight in ((g0, w0), (g1, w1), (g2, w2), (g3, w3)):
        total = total + contract(grad[...], weight[0:model, :], ((1,), (1,)))
    unit = unit_ref[...]
    grad = normalize_back(total, unit, scale[...], vectors[2:3, :])
    grad_ref[...] = grad
    turned_ref[...] = grad.astype(bf16).T
    column_sums(step, sums_ref, ((0, grad), (2, total * unit), (3, total)), sums_two[...])


def per_device(
    tokens,
    doc_lengths,
    w_query,
    w_key,
    w_value,
    w_out,
    w_up,
    w_down,
    b_query,
    b_value,
    b_up,
    b_out,
    b_down,
    gain_one,
    shift_one,
    gain_two,
    shift_two,
    cotangent,
):
    dp, tensor = lax.axis_size("dp"), lax.axis_size("tensor")
    length, model = tokens.shape
    rows = model // dp
    group = w_query.shape[1]
    links = Links(dp, tensor)
    swap = links.swap

    share = b_out.shape[0]
    me = links.me
    mine = lax.axis_index("tensor")
    hidden = w_up.shape[1]
    (packed,) = small_call(
        pack_kernel,
        "pack",
        links,
        [shape(rows + SIDE, 3 * group, dtype=bf16)],
        w_query,
        w_key,
        w_value,
        b_query,
        b_value,
        copied=True,
    )
    ring_attn = GatherRing(links, packed)
    zero = jnp.zeros((share,), f32)
    vectors = jnp.stack([b_out, b_down, gain_one, shift_one, gain_two, shift_two, zero, zero])

    ring_attn.step()
    late_out, late_down = small_call(
        pack_late_kernel,
        "pack_late",
        links,
        [shape(rows, group, dtype=bf16), shape(rows + SIDE, hidden, dtype=bf16)],
        w_out,
        w_down.T,
        vectors,
    )
    late = Box(late_out, late_down, doc_lengths)
    tie(ring_attn, late)
    late_out, late_down, early_lengths = late.live
    ring_attn.step()
    far_late = Box(swap(late_out, 2), swap(late_down, 2))
    span, window = documents(mine, early_lengths, length, BLOCK)
    done = Box(span)
    tie(ring_attn, done)
    span = done.live[0]
    ring_attn.step()
    tie(ring_attn)
    up_chunk, down_chunk = small_call(
        pack_up_kernel,
        "pack_up",
        links,
        [
            shape(rows + SIDE, 2 * group + hidden, dtype=bf16),
            shape(rows, 2 * hidden, dtype=bf16),
        ],
        late_out,
        far_late.live[0],
        w_up,
        late_down,
        far_late.live[1],
        b_up,
    )
    ring_up = GatherRing(links, up_chunk)
    ring_down = GatherRing(links, down_chunk)
    for _ in range(links.ahead - 3):
        ring_attn.step()
    (attn_own,) = ring_attn.full([(0, 3 * group, 0)], rows)

    attn_w = [attn_own, None, None, None]
    qkv, mixture, logs = [None] * 4, [None] * 4, [None] * 4

    def attend_group(j):
        mixture[j], logs[j], qkv[j] = attend(work.live[0], attn_w[j], window, span)
        return Box(mixture[j])

    work = Box(tokens, attn_own)
    tie(ring_attn, ring_up, work)
    attn_w[0] = work.live[1]
    work = Box(work.live[0])
    far = Box(swap(attn_w[0], 2))
    attn_w[1] = swap(attn_w[0], 1)
    ring_up.step()
    done = attend_group(0)
    tie(ring_up, work, done)
    ring_up.step()
    done = attend_group(1)
    tie(ring_up, work, done)
    ring_up.step()
    (tokens_turned,) = tiled(
        turn_kernel, "turn", 4, (work.live[0],), (0,), [(shape(model, length, dtype=bf16), 1)], 0
    )
    turned = Box(tokens_turned)
    tie(ring_up, work, far, turned)
    tokens_turned = turned.live[0]
    attn_w[2] = far.live[0]
    attn_w[3] = swap(attn_w[2], 1)
    for _ in range(links.ahead - 3):
        ring_up.step()
    done = attend_group(2)
    tie(ring_up, work, done, ring_down)
    ring_down.step()
    out_near, up_own = ring_up.full([(0, 2 * group, "all"), (2 * group, hidden, 6)], rows)
    out_far = swap(out_near, 1)
    cuts = [0, model // 3, 2 * model // 3, up_own.shape[0]]
    held, across_up = Box(up_own), []

    def up_across():
        low, high = cuts[len(across_up) : len(across_up) + 2]
        across_up.append(Box(swap(held.live[0][low:high], 2)))
        return across_up[-1]

    moved = up_across()
    done = attend_group(3)
    tie(ring_down, work, done, held, moved)

    ring_down.step()
    moved = up_across()
    count = np.arange(dp * share)
    base = jnp.asarray((count // share * tensor * share + count % share)[:, None], jnp.int32)
    lanes = base + (mine ^ jnp.arange(4, dtype=jnp.int32))[None, :] * share
    (vectors,) = tiled(
        vectors_kernel,
        "vectors",
        1,
        (lanes, out_near, out_far),
        (None,) * 3,
        [(shape(SIDE, model), None)],
        0,
    )
    up_w = [up_own, None, None, None]
    first_low, first_turned, unit_one, scale_one = tiled(
        out_kernel,
        "attention_out",
        2,
        (*mixture, out_near, out_far, vectors, work.live[0]),
        (1,) * 4 + (None,) * 3 + (0,),
        [
            (shape(length, model, dtype=bf16), 0),
            (shape(model, length, dtype=bf16), 1),
            (shape(length, model), 0),
            (shape(length, 1), 0),
        ],
        2 * length * model * model,
    )
    activated, slopes = [None] * 4, [None] * 4

    def up_group(j):
        activated[j], slopes[j] = tiled(
            up_kernel,
            "up",
            2,
            (work.live[0], up_w[j]),
            (0, None),
            [(shape(length, hidden, dtype=bf16), 0)] * 2,
            2 * length * model * hidden,
        )
        return Box(activated[j])

    work = Box(first_low)
    tie(ring_down, work, held, moved)
    up_w[0] = held.live[0]
    moved = up_across()
    up_w[1] = swap(up_w[0], 1)
    ring_down.step()
    done = up_group(0)
    tie(ring_down, work, done, moved)
    for _ in range(links.ahead - 3):
        ring_down.step()
    up_w[2] = jnp.concatenate([box.live[0] for box in across_up])
    up_w[3] = swap(up_w[2], 1)
    done = up_group(1)
    tie(ring_down, work, done)
    down_own, down_across = ring_down.full([(0, hidden, None), (hidden, hidden, None)], rows)
    down_w = [down_own, swap(down_own, 1), down_across, swap(down_across, 1)]
    done = [up_group(2), up_group(3)]
    result, grad_two, grad_two_low, grad_two_turned, sums_two = tiled(
        down_kernel,
        "down",
        2,
        (*activated, *down_w, vectors, unit_one, cotangent),
        (0,) * 4 + (None,) * 5 + (0,) * 2,
        [
            (shape(length, model, dtype=bf16), 0),
            (shape(length, model), 0),
            (shape(length, model, dtype=bf16), 0),
            (shape(model, length, dtype=bf16), 1),
            (shape(SIDE, model), None),
        ],
        8 * length * model * hidden,
    )
    work = Box(grad_two_low)

    def blocks(value):
        return value.reshape(-1, rows, value.shape[-1])

    def grad_down(j):
        return outer(grad_two_turned, activated[j])[0]

    def grad_w_up(j, cuts=None, arrived=()):
        return outer(first_turned, grad_up[j], cuts, arrived)

    grad_up, grad_bias_up = [None] * 4, [None] * 4

    def back_up(j):
        grad_up[j], grad_bias_up[j] = tiled(
            slope_kernel,
            "back_up",
            2,
            (work.live[0], down_w[j], slopes[j]),
            (0, None, 0),
            [(shape(length, hidden, dtype=bf16), 0), (shape(SIDE, hidden), None)],
            2 * length * model * hidden,
        )

    def cuts(total):
        return [0, total * 3 // 8, total * 5 // 8, total]

    sent = Box(grad_down(3), grad_down(1))
    tie(work, sent)
    three, one = (swap(v, 1) for v in sent.live)
    two, zero = grad_down(2), grad_down(0)
    back_up(3)
    three_up = Box(*grad_w_up(3))
    pair = Box(two, zero, three, one)
    tie(work, pair, three_up)
    two, zero, three, one = (blocks(v) for v in pair.live)
    sums_down = ScatterRing(links, [[zero, one], [two, three]])
    sums_down.step()
    three_up = Box(swap(three_up.live[0], 1))
    back_up(2)
    back_up(1)
    back_up(0)
    across = grad_w_up(2, cuts(model), (three_up.live[0],))
    across = Box(*across)
    tie(work, sums_down, across)
    across = across.live
    far_up = [Box(swap(across[0], 2))]
    kept = Box(*grad_w_up(1), *grad_w_up(0), grad_up[0])
    sums_down.step()
    grad_one, grad_one_turned, sums = tiled(
        first_kernel,
        "back_first",
        2,
        (*grad_up, *up_w, vectors, grad_two, unit_one, scale_one, sums_two),
        (0,) * 4 + (None,) * 5 + (0,) * 3 + (None,),
        [
            (shape(length, model), 0),
            (shape(model, length, dtype=bf16), 1),
            (shape(SIDE, model), None),
        ],
        8 * length * model * hidden,
    )
    work = Box(grad_one_turned)
    tie(work, kept, sums_down, far_up[0])
    one_up, zero_up, _ = kept.live
    one_up = Box(swap(one_up, 1))
    far_up.append(Box(swap(across[1], 2)))
    grad_qkv = [None] * 4

    def back_attention(j):
        grad_qkv[j] = attend_back(
            qkv[j],
            mixture[j],
            logs[j],
            out_near if j % 2 == 0 else out_far,
            j // 2,
            work.live[0],
            window,
            span,
        )
        return Box(grad_qkv[j])

    grad_input = Box(grad_one)

    def back_input(j):
        grad_input.live = tiled(
            input_kernel,
            "back_input",
            2,
            (grad_qkv[j], attn_w[j], grad_input.live[0]),
            (1, None, 0),
            [(shape(length, model, dtype=f32 if j else bf16), 0)],
            6 * length * model * group,
        )

    def back_group(j, arrived=(), starts=()):
        return grad_weight(
            dp,
            tokens_turned,
            grad_qkv[j],
            work.live[0],
            mixture[j],
            grad_bias_up[j],
            sums,
            arrived,
            starts,
        )

    sums_down.step()
    back_attention(3)
    three = Box(back_group(3))
    tie(work, three, one_up, far_up[1], sums_down)
    recv = Box(swap(three.live[0], 1))
    far_up.append(Box(swap(across[2], 2)))
    for _ in range(links.ahead - 3):
        sums_down.step()
    done = back_attention(2)
    tie(work, done, recv, far_up[2], sums_down)
    grad_qkv[2] = done.live[0]
    far = blocks(jnp.concatenate([box.live[0] for box in far_up]))
    sums_up = ScatterRing(links, [[blocks(zero_up), blocks(one_up.live[0]), far]])
    sums_up.step()
    down_total, down_far = sums_down.total()
    end_down = Box(swap(down_far, 2))
    two = Box(back_group(2, (recv.live[0],), (0,)))
    back_input(3)
    tie(work, two, sums_up, end_down, grad_input)
    split = cuts(dp)
    far_attn = [Box(swap(two.live[0][split[0] : split[1]], 2))]
    sums_up.step()
    done = back_attention(1)
    tie(work, done, sums_up, far_attn[0])
    grad_qkv[1] = done.live[0]
    far_attn.append(Box(swap(two.live[0][split[1] : split[2]], 2)))
    sums_up.step()
    one = Box(back_group(1))
    back_input(2)
    tie(work, one, far_attn[1], sums_up, grad_input)
    recv = Box(swap(one.live[0], 1))
    far_attn.append(Box(swap(two.live[0][split[2] :], 2)))
    for _ in range(links.ahead - 3):
        sums_up.step()
    done = back_attention(0)
    up_total = Box(*sums_up.total())
    tie(work, done, recv, far_attn[2], up_total)
    grad_qkv[0] = done.live[0]
    arrived = [recv.live[0]] + [box.live[0] for box in far_attn]
    (grad_down_own,) = pl.pallas_call(
        down_end_kernel,
        out_shape=[shape(rows, hidden)],
        in_specs=[VMEM] * 2,
        out_specs=[VMEM],
        compiler_params=pltpu.CompilerParams(vmem_limit_bytes=RING_ROOM),
        name="down_end",
    )(down_total, end_down.live[0])
    ends = Box(grad_down_own, up_total.live[0])
    zero = Box(back_group(0, arrived, (0, *split[:3])), grad_qkv[:2])
    tie(work, zero, ends)
    sums_attn = ScatterRing(links, [[zero.live[0]]])
    grad_qkv[:2] = zero.live[1]
    for j in (1, 0):
        sums_attn.step()
        back_input(j)
        tie(grad_input, sums_attn)
    while sums_attn.count < links.ahead:
        sums_attn.step()
    full = dp * b_query.shape[1]
    full_up = dp * b_up.shape[1]
    *made, held = finish(
        links,
        sums_attn,
        jnp.stack([me, me * tensor + mine]),
        [shape(rows, group)] * 3
        + [shape(group, rows)]
        + [shape(*table.shape) for table in (b_query, b_value, b_up)]
        + [shape(SIDE, share)],
        (
            (0, 0, b_query.shape[1], full),
            (0, 2 * group, b_value.shape[1], full),
            (1, 0, b_up.shape[1], full_up),
        ),
    )
    return (
        result,
        grad_input.live[0],
        *made[:4],
        ends.live[1],
        ends.live[0].T,
        *made[4:],
        *[held[i + 2] for i in range(6)],
    )


def solution(mesh):
    both = P(("dp", "tensor"))
    rows = P(("dp", "tensor"), None)
    down = P("tensor", "dp")
    wide = P("dp", "tensor")
    weights = (wide, wide, wide, down, wide, down, down, down, down)
    return jax.shard_map(
        per_device,
        mesh=mesh,
        in_specs=(rows, P("dp", None)) + weights + (both,) * 6 + (rows,),
        out_specs=(rows, rows) + weights + (both,) * 6,
        check_vma=False,
    )
```

```python
import functools

import jax
import jax.numpy as jnp
import numpy as np
from jax import lax
from jax.experimental import pallas as pl
from jax.experimental.pallas import tpu as pltpu
from jax.sharding import PartitionSpec as P

HD = 64
BLOCK = 256
EXTRA = 16
STEP = 128
SIDE = 8
RING_ROOM = 2 << 20
ATTEND_ROOM = 12 << 20
TILE_ROOM = 8 << 20
TAIL = 8

epsilon = 1e-06
root_half = 0.7071067811865476
inv_root_tau = 0.3989422804014327
masked_value = -1e30
bf16 = jnp.bfloat16
f32 = jnp.float32


def contract(a, b, dims, out=f32):
    return lax.dot_general(a, b, (dims, ((), ())), preferred_element_type=f32).astype(out)


def ring_order(size):
    return list(range(0, size, 2)) + list(range(size - 1, 0, -2)) if size > 1 else [0]


class Links:
    def __init__(self, dp, tensor):
        self.dp, self.tensor = dp, tensor
        order = ring_order(dp)
        self.forward = [(order[i], order[(i + 1) % dp]) for i in range(dp)]
        self.backward = [(b, a) for a, b in self.forward]
        self.me = lax.axis_index("dp")
        self.ahead = dp // 2
        self.behind = dp - 1 - self.ahead
        offsets = jnp.arange(-self.ahead, self.behind + 1, dtype=jnp.int32)
        half = lax.shift_right_logical(self.me, 1)
        position = jnp.where((self.me & 1) == 0, half, dp - 1 - half)
        place = position + offsets
        place = jnp.where(place < 0, place + dp, jnp.where(place < dp, place, place - dp))
        self.members = jnp.where(place < (dp + 1) // 2, 2 * place, 2 * (dp - 1 - place) + 1)

    def swap(self, value, mask):
        return lax.ppermute(value, "tensor", [(i, i ^ mask) for i in range(self.tensor)])


def tie(*holders):
    flat, tree = jax.tree.flatten([holder.live for holder in holders])
    flat = lax.optimization_barrier(tuple(flat))
    for holder, live in zip(holders, jax.tree.unflatten(tree, flat)):
        holder.live = live


class Box:
    def __init__(self, *live):
        self.live = list(live)


class GatherRing:
    def __init__(self, links, value):
        self.links = links
        self.live = [value, value]
        self.pieces = {0: value}
        self.count = 0

    def step(self):
        links = self.links
        self.count += 1
        up, down = self.live
        half = up.shape[0] // 32 * 16
        if self.count == links.ahead and half:
            up, down = up[:half], down[half:]
            up = lax.ppermute(up, "dp", links.forward)
            self.live = [up, lax.ppermute(down, "dp", links.backward)]
            return
        up = lax.ppermute(up, "dp", links.forward)
        self.pieces[-self.count] = up
        if self.count <= links.behind:
            down = lax.ppermute(down, "dp", links.backward)
            self.pieces[self.count] = down
        self.live = [up, down]

    def full(self, plan, rows):
        links = self.links
        pieces = [self.pieces[offset] for offset in range(1 - links.ahead, links.behind + 1)]
        halves = self.live if self.live[0].shape[0] < self.pieces[0].shape[0] else self.live[:1]
        return assemble(links.members, halves + pieces, plan, rows)


class ScatterRing:
    def __init__(self, links, groups):
        self.links = links
        self.groups = groups
        self.count = 0
        self.live = ring_call(links, groups, (links.ahead, -links.ahead), (), bf16, first=True)

    def step(self):
        links = self.links
        self.count += 1
        up, down = self.live
        up = lax.ppermute(up, "dp", links.forward)
        down = lax.ppermute(down, "dp", links.backward)
        left = links.ahead - self.count
        if left:
            up, down = ring_call(links, self.groups, (left, -left), (up, down), bf16)
        self.live = [up, down]

    def total(self):
        sources, counts, rows, _ = flatten(self.groups)
        widths = [group[0].shape[2] for group in self.groups]
        return pl.pallas_call(
            functools.partial(total_kernel, counts=counts, place=self.links.ahead),
            out_shape=[
                jax.ShapeDtypeStruct((rows, width), f32 if index == 0 else bf16)
                for index, width in enumerate(widths)
            ],
            in_specs=[SMEM] + [VMEM] * (len(sources) + 2),
            out_specs=[VMEM] * len(widths),
            compiler_params=pltpu.CompilerParams(vmem_limit_bytes=RING_ROOM),
            name="ring_total",
        )(self.links.members, *sources, *self.live)


VMEM = pl.BlockSpec(memory_space=pltpu.VMEM)
SMEM = pl.BlockSpec(memory_space=pltpu.SMEM)


def block_of(sources, member):
    if len(sources) == 1:
        return sources[0][member].astype(f32)
    low, high = sources
    half = low.shape[0]
    lower = low[jnp.minimum(member, half - 1)].astype(f32)
    return jnp.where(member < half, lower, high[jnp.maximum(member - half, 0)].astype(f32))


def ring_sums(members_ref, refs, counts, place):
    member = members_ref[place]
    at = 0
    for count in counts:
        total = None
        for pieces in count:
            made = block_of(refs[at : at + pieces], member)
            total = made if total is None else total + made
            at += pieces
        yield total


def ring_kernel(members_ref, *refs, counts, places, dtype, first):
    size, sends = sum(map(sum, counts)), len(places)
    sources, arrived, outs = refs[:size], refs[size:-sends], refs[-sends:]
    for index, place in enumerate(places):
        column = 0
        out = outs[index]
        mine = arrived if sends == 1 else arrived[index : index + 1]
        for made in ring_sums(members_ref, sources, counts, place):
            rows, width = made.shape
            own = slice(column, column + width)
            column += width
            if first:
                half = out.shape[0]
                out[:, own] = (made[:half] if index == 0 else made[rows - half :]).astype(dtype)
                continue
            whole = [one for one in mine if one.shape[0] == rows]
            for one in whole:
                made = made + one[:, own].astype(f32)
            out[:, own] = made.astype(dtype)
            for one in mine:
                if one.shape[0] < rows:
                    half = one.shape[0]
                    part = slice(0, half) if index == 0 else slice(rows - half, rows)
                    out[part, own] = (made[part] + one[:, own].astype(f32)).astype(dtype)


def total_kernel(members_ref, *refs, counts, place):
    size = sum(map(sum, counts))
    sources, arrived, outs = refs[:size], refs[size : size + 2], refs[size + 2 :]
    column = 0
    for out, made in zip(outs, ring_sums(members_ref, sources, counts, place)):
        own = slice(column, column + out.shape[1])
        for one in arrived:
            made = made + one[:, own].astype(f32)
        out[...] = made.astype(out.dtype)
        column += out.shape[1]


def flatten(groups):
    sources, counts = [], []
    for group in groups:
        pieces = [one if isinstance(one, (list, tuple)) else [one] for one in group]
        counts.append([len(one) for one in pieces])
        sources += [part for one in pieces for part in one]
    widths = [(group[0][0] if isinstance(group[0], (list, tuple)) else group[0]).shape for group in groups]
    return sources, counts, widths[0][1], sum(width[2] for width in widths)


def ring_call(links, groups, offsets, arrived, dtype, first=False):
    sources, counts, rows, columns = flatten(groups)
    size = rows * columns
    return list(
        pl.pallas_call(
            functools.partial(
                ring_kernel,
                counts=counts,
                places=[(offset + links.ahead) % links.dp for offset in offsets],
                dtype=dtype,
                first=first,
            ),
            out_shape=[
                jax.ShapeDtypeStruct((rows // 2 if first else rows, columns), dtype) for _ in offsets
            ],
            in_specs=[SMEM] + [VMEM] * (len(sources) + len(arrived)),
            out_specs=[VMEM] * len(offsets),
            compiler_params=pltpu.CompilerParams(vmem_limit_bytes=RING_ROOM),
            cost_estimate=pl.CostEstimate(
                flops=size * 2, bytes_accessed=6 * size * len(offsets), transcendentals=0
            ),
            name="ring_sum",
        )(links.members, *sources, *arrived)
    )


def finish_kernel(
    members_ref, me_ref, *refs, counts, place, tables
):
    size = sum(map(sum, counts))
    sources, arrived, outs = refs[:size], refs[size : size + 2], refs[size + 2 :]
    (total,) = ring_sums(members_ref, sources, counts, place)
    for one in arrived:
        total = total + one[...].astype(f32)
    rows, group = outs[0].shape
    for index in range(3):
        outs[index][...] = total[:rows, index * group : (index + 1) * group]
    outs[3][...] = total[:rows, 3 * group :].T
    side = total[rows:]
    wide = side.shape[1]
    for out, (line, at, per, full) in zip(outs[4:7], tables):
        turned = pltpu.roll(side, wide - me_ref[0] * per, axis=1)
        for row in range(out.shape[0]):
            start = at + row * full
            out[row : row + 1, :] = turned[line : line + 1, start : start + per]
    share = outs[7].shape[1]
    turned = pltpu.roll(side, wide - me_ref[1] * share, axis=1)
    outs[7][...] = turned[:, 0:share]


def finish(links, ring, places, shapes, tables):
    sources, counts, _, _ = flatten(ring.groups)
    return pl.pallas_call(
        functools.partial(finish_kernel, counts=counts, place=links.ahead, tables=tables),
        out_shape=shapes,
        in_specs=[SMEM] * 2 + [VMEM] * (len(sources) + 2),
        out_specs=[VMEM] * len(shapes),
        compiler_params=pltpu.CompilerParams(vmem_limit_bytes=RING_ROOM),
        name="finish",
    )(links.members, places, *sources, *ring.live)


def assemble_kernel(members_ref, *refs, count, total_rows, plan, rows):
    pieces, outs = refs[:count], refs[count:]
    total, index, done = None, 0, 0
    blocks = 0
    for piece in pieces:
        first = members_ref[index] * rows + done
        own = min(piece.shape[0], rows - done)
        for out, (at, width, _) in zip(outs, plan):
            out[pl.ds(pl.multiple_of(first, 16), own), :] = piece[0:own, at : at + width]
        done += piece.shape[0]
        if done == total_rows:
            if total_rows > rows:
                side = piece[own:, :].astype(f32)
                total = side if total is None else total + side
            index, done, blocks = index + 1, 0, blocks + 1
    for out, (at, width, kept) in zip(outs, plan):
        if kept == "all":
            for index in range(3):
                first = blocks * rows + index * SIDE
                out[first : first + SIDE, :] = total[:, index * width : (index + 1) * width].astype(bf16)
        elif kept is not None:
            out[blocks * rows :, :] = jnp.broadcast_to(
                total[kept : kept + 1, at : at + width], (SIDE, width)
            ).astype(bf16)


def assemble(members, pieces, plan, rows):
    count = members.shape[0]
    full, wide = pieces[-1].shape
    if rows % 16:
        if len(pieces) > count:
            pieces = [jnp.concatenate(pieces[:2])] + pieces[2:]
        stacked = jnp.stack(pieces)
        back = jnp.zeros((count,), jnp.int32).at[members].set(jnp.arange(count, dtype=jnp.int32))
        stacked = jnp.take(stacked, back, axis=0)
        weights = stacked[:, :rows].reshape(count * rows, -1)
        total = jnp.sum(stacked[:, rows:].astype(f32), axis=0)
        outs = []
        for at, width, kept in plan:
            out = weights[:, at : at + width]
            if kept == "all":
                parts = [total[:, i * width : (i + 1) * width].astype(bf16) for i in range(3)]
                out = jnp.concatenate([out] + parts)
            elif kept is not None:
                row = jnp.broadcast_to(total[kept : kept + 1, at : at + width], (SIDE, width))
                out = jnp.concatenate([out, row.astype(bf16)])
            outs.append(out)
        return outs
    shapes = [
        jax.ShapeDtypeStruct(
            (count * rows + SIDE * {None: 0, "all": 3}.get(kept, 1), width), bf16
        )
        for _, width, kept in plan
    ]
    return pl.pallas_call(
        functools.partial(
            assemble_kernel, count=len(pieces), total_rows=full, plan=plan, rows=rows
        ),
        out_shape=shapes,
        in_specs=[SMEM] + [VMEM] * len(pieces),
        out_specs=[VMEM] * len(shapes),
        compiler_params=pltpu.CompilerParams(vmem_limit_bytes=RING_ROOM),
        cost_estimate=pl.CostEstimate(
            flops=0, bytes_accessed=4 * count * full * wide, transcendentals=0
        ),
        name="assemble",
    )(members, *pieces)


def one_hot(first, rows, size):
    hit = lax.broadcasted_iota(jnp.int32, (rows, size), 1) == (
        lax.broadcasted_iota(jnp.int32, (rows, size), 0) + first
    )
    return jnp.where(hit, 1.0, 0.0).astype(bf16)


def placed(table, me, dp):
    count, per = table.shape
    spread = contract(table, one_hot(me * per, per, per * dp), ((1,), (0,)))
    return [spread[row : row + 1] for row in range(count)]


def only_row(row, at):
    line = lax.broadcasted_iota(jnp.int32, (SIDE, row.shape[1]), 0)
    return jnp.where(line == at, row, 0.0)


def pack_kernel(me_ref, *refs, dp):
    sources, out_ref, held, sems = refs[:5], refs[5], refs[6:11], refs[11]
    copies = [
        pltpu.make_async_copy(source, target, sems.at[index])
        for index, (source, target) in enumerate(zip(sources, held))
    ]
    for copy in copies:
        copy.start()
    for copy in copies:
        copy.wait()
    query_ref, key_ref, value_ref, b_query_ref, b_value_ref = held
    rows, group = query_ref.shape
    out_ref[0:rows, 0:group] = query_ref[...]
    out_ref[0:rows, group : 2 * group] = key_ref[...]
    out_ref[0:rows, 2 * group :] = value_ref[...]
    me = me_ref[0]
    row = jnp.concatenate(
        placed(b_query_ref[...], me, dp)
        + [jnp.zeros((1, group), f32)]
        + placed(b_value_ref[...], me, dp),
        axis=1,
    )
    out_ref[rows:, :] = only_row(row, 0).astype(bf16)


def pack_late_kernel(me_ref, w_out_ref, w_down_ref, vectors_ref, out_ref, down_ref, *, dp):
    rows, hidden = w_down_ref.shape
    out_ref[...] = w_out_ref[...].T
    down_ref[0:rows, :] = w_down_ref[...]
    left = vectors_ref[...]
    share = left.shape[1]
    place = one_hot(me_ref[0] * share, share, share * dp)
    spread = []
    for _ in range(3):
        part = left.astype(bf16)
        left = left - part.astype(f32)
        spread.append(contract(part, place, ((1,), (0,))))
    row = jnp.concatenate(spread, axis=1)
    blank = jnp.zeros((SIDE, hidden - row.shape[1]), f32)
    down_ref[rows:, :] = jnp.concatenate([row, blank], axis=1).astype(bf16)


def pack_up_kernel(
    me_ref, out_ref, far_out_ref, w_up_ref, down_ref, far_down_ref, b_up_ref, up_ref, pair_ref, *, dp
):
    rows, hidden = w_up_ref.shape
    group = out_ref.shape[1]
    up_ref[0:rows, 0:group] = out_ref[...]
    up_ref[0:rows, group : 2 * group] = far_out_ref[...]
    up_ref[0:rows, 2 * group :] = w_up_ref[...]
    pair_ref[:, 0:hidden] = down_ref[0:rows, :]
    pair_ref[:, hidden:] = far_down_ref[0:rows, :]
    near = down_ref[rows:, 0 : 3 * group].astype(f32)
    far = far_down_ref[rows:, 0 : 3 * group].astype(f32)
    bias = jnp.concatenate(
        [jnp.zeros((1, 2 * group), f32)] + placed(b_up_ref[...], me_ref[0], dp), axis=1
    )
    side = jnp.concatenate([near, far], axis=1) + only_row(bias, 6)
    up_ref[rows:, :] = side.astype(bf16)


def small_call(kernel, name, links, shapes, *operands, copied=False):
    place = pl.BlockSpec(memory_space=pltpu.HBM) if copied else VMEM
    scratch = []
    if copied:
        operands = [pltpu.with_memory_space_constraint(x, pltpu.HBM) for x in operands]
        scratch = [pltpu.VMEM(x.shape, x.dtype) for x in operands]
        scratch.append(pltpu.SemaphoreType.DMA((len(operands),)))
    return pl.pallas_call(
        functools.partial(kernel, dp=links.dp),
        out_shape=shapes,
        in_specs=[SMEM] + [place] * len(operands),
        out_specs=[VMEM] * len(shapes),
        scratch_shapes=scratch,
        compiler_params=pltpu.CompilerParams(vmem_limit_bytes=RING_ROOM),
        name=name,
    )(links.me.reshape(1), *operands)


def documents_kernel(mine_ref, lengths_ref, span_ref, window_ref, *, block):
    length = span_ref.shape[1]
    count = length // block
    place = lax.broadcasted_iota(jnp.int32, (1, length), 1)
    low = high = jnp.zeros((1, length), jnp.int32)
    begins, ends = [jnp.int32(0)] * count, [jnp.int32(0)] * count
    start = jnp.int32(0)
    for document in range(lengths_ref.shape[1]):
        end = start + lengths_ref[mine_ref[0], document]
        inside = (place >= start) & (place < end)
        low, high = jnp.where(inside, start, low), jnp.where(inside, end, high)
        for index in range(count):
            first, last = index * block, (index + 1) * block - 1
            begins[index] = jnp.where((start <= first) & (first < end), start, begins[index])
            ends[index] = jnp.where((start <= last) & (last < end), end, ends[index])
        start = end
    span_ref[0:1, :] = low
    span_ref[1:2, :] = high
    for index in range(count):
        begin = lax.div(begins[index], jnp.int32(STEP)) * STEP
        window_ref[0, index] = begin
        window_ref[1, index] = lax.div(ends[index] - begin + (STEP - 1), jnp.int32(STEP))


def documents(mine, lengths, length, block):
    return pl.pallas_call(
        functools.partial(documents_kernel, block=block),
        out_shape=[
            jax.ShapeDtypeStruct((2, length), jnp.int32),
            jax.ShapeDtypeStruct((2, length // block), jnp.int32),
        ],
        in_specs=[SMEM, SMEM],
        out_specs=[VMEM, SMEM],
        compiler_params=pltpu.CompilerParams(vmem_limit_bytes=RING_ROOM),
        name="documents",
    )(mine.reshape(1), lengths)


def fill_bias(bias, begin, low, high, size):
    keys = lax.broadcasted_iota(jnp.int32, (size, low.shape[1]), 0) + begin
    bias[0:size, :] = jnp.where((keys >= low) & (keys < high), 0.0, masked_value)


def attend_kernel(
    window_ref, tokens_ref, weight_ref, span_ref, out_ref, log_ref, qkv_ref, keys, values, bias, hold, *, block
):
    length = qkv_ref.shape[1]
    heads = qkv_ref.shape[0] // (3 * HD)
    width = heads * HD
    model = tokens_ref.shape[1]
    made = contract(tokens_ref[...], weight_ref[0:model, :], ((1,), (0,)))
    made = made + weight_ref[model : model + 1, :].astype(f32)
    qkv_ref[...] = made.astype(bf16).T
    tail = jnp.where(lax.broadcasted_iota(jnp.int32, (EXTRA, length), 0) == 0, 1.0, 0.0).astype(bf16)
    for head in range(heads):
        keys[head] = qkv_ref[width + head * HD : width + (head + 1) * HD, :].T
        values[head, 0:HD, :] = qkv_ref[2 * width + head * HD : 2 * width + (head + 1) * HD, :]
        values[head, HD : HD + EXTRA, :] = tail

    def one_block(index, _):
        lanes = pl.ds(pl.multiple_of(index * block, block), block)
        begin = pl.multiple_of(window_ref[0, index], STEP)

        def with_count(count):
            fill_bias(bias, begin, span_ref[0:1, lanes], span_ref[1:2, lanes], count * STEP)
            parts = [(at, min(block, count * STEP - at)) for at in range(0, count * STEP, block)]
            tops = []
            for head in range(heads):
                queries = qkv_ref[head * HD : (head + 1) * HD, lanes] * 0.125
                top = None
                for at, size in parts:
                    own = pl.ds(begin + at, size)
                    scores = contract(keys[head, own, :], queries, ((1,), (0,))) + bias[at : at + size, :]
                    hold[head, at : at + size, :] = scores
                    most = jnp.max(scores.reshape(size // 8, 8, block), axis=0)
                    top = most if top is None else jnp.maximum(top, most)
                tops.append(jnp.max(top, axis=0, keepdims=True))
            for head in range(heads):
                total = None
                for at, size in parts:
                    own = pl.ds(begin + at, size)
                    weights = jnp.exp(hold[head, at : at + size, :] - tops[head]).astype(bf16)
                    made = contract(values[head, :, own], weights, ((1,), (0,)))
                    total = made if total is None else total + made
                mass = total[HD : HD + 1, :]
                out_ref[head * HD : (head + 1) * HD, lanes] = (total[:HD] / mass).astype(bf16)
                log_ref[head : head + 1, lanes] = tops[head] + jnp.log(mass)

        for count in range(1, length // STEP + 1):
            pl.when(window_ref[1, index] == count)(functools.partial(with_count, count))
        return 0

    lax.fori_loop(0, length // block, one_block, 0)


def attend_back_kernel(
    window_ref, half_ref, qkv_ref, span_ref, out_ref, log_ref, weight_ref, one_ref, result_ref, keys, values, bias, grad_key, grad_value, grad_ref, weight, *, block
):
    length = qkv_ref.shape[1]
    model = one_ref.shape[0]
    group = grad_ref.shape[0]
    for half in range(2):

        @pl.when(half_ref[0] == half)
        def _():
            weight[...] = weight_ref[0:model, half * group : (half + 1) * group]

    grad_ref[...] = contract(weight[...], one_ref[...], ((0,), (0,)), bf16)
    heads = qkv_ref.shape[0] // (3 * HD)
    width = heads * HD
    for head in range(heads):
        keys[head] = qkv_ref[width + head * HD : width + (head + 1) * HD, :].T
        values[head] = qkv_ref[2 * width + head * HD : 2 * width + (head + 1) * HD, :].T
    grad_key[...] = jnp.zeros_like(grad_key)
    grad_value[...] = jnp.zeros_like(grad_value)

    def one_block(index, _):
        lanes = pl.ds(pl.multiple_of(index * block, block), block)
        begin = pl.multiple_of(window_ref[0, index], STEP)

        def with_count(count):
            size = count * STEP
            window = pl.ds(begin, size)
            fill_bias(bias, begin, span_ref[0:1, lanes], span_ref[1:2, lanes], size)
            owns = [slice(head * HD, (head + 1) * HD) for head in range(heads)]
            queries = [qkv_ref[own, lanes] * 0.125 for own in owns]
            grads = [grad_ref[own, lanes] for own in owns]
            deltas = [
                jnp.sum(out_ref[own, lanes].astype(f32) * grad.astype(f32), axis=0, keepdims=True)
                for own, grad in zip(owns, grads)
            ]
            made = [None] * heads
            for at in range(0, size, block):
                step = min(block, size - at)
                part = pl.ds(begin + at, step)
                raw = []
                for head in range(heads):
                    scores = contract(keys[head, part, :], queries[head], ((1,), (0,)))
                    grad_prob = contract(values[head, part, :], grads[head], ((1,), (0,)))
                    raw.append((scores + bias[at : at + step, :], grad_prob))
                both = []
                for head, (scores, grad_prob) in enumerate(raw):
                    weights = jnp.exp(scores - log_ref[head : head + 1, lanes])
                    both.append((weights.astype(bf16), (weights * (grad_prob - deltas[head])).astype(bf16)))
                for head, (weights, grad_scores) in enumerate(both):
                    own = owns[head]
                    grad_value[own, part] += contract(grads[head], weights, ((1,), (1,)))
                    grad_key[own, part] += contract(queries[head], grad_scores, ((1,), (1,)))
                    key_cols = qkv_ref[width + head * HD : width + (head + 1) * HD, part]
                    more = contract(key_cols, grad_scores, ((1,), (0,)))
                    made[head] = more if made[head] is None else made[head] + more
            for head, own in enumerate(owns):
                result_ref[own, lanes] = (made[head] * 0.125).astype(bf16)

        for count in range(1, length // STEP + 1):
            pl.when(window_ref[1, index] == count)(functools.partial(with_count, count))
        return 0

    lax.fori_loop(0, length // block, one_block, 0)
    result_ref[width : 2 * width, :] = grad_key[...].astype(bf16)
    result_ref[2 * width :, :] = grad_value[...].astype(bf16)


def attend(tokens, weight, window, span):
    length, model = tokens.shape
    width = weight.shape[1]
    heads = width // (3 * HD)
    return pl.pallas_call(
        functools.partial(attend_kernel, block=BLOCK),
        out_shape=(
            jax.ShapeDtypeStruct((heads * HD, length), bf16),
            jax.ShapeDtypeStruct((8, length), f32),
            jax.ShapeDtypeStruct((width, length), bf16),
        ),
        in_specs=[SMEM] + [VMEM] * 3,
        out_specs=(VMEM,) * 3,
        scratch_shapes=[
            pltpu.VMEM((heads, length, HD), bf16),
            pltpu.VMEM((heads, HD + EXTRA, length), bf16),
            pltpu.VMEM((length, BLOCK), f32),
            pltpu.VMEM((heads, length, BLOCK), f32),
        ],
        compiler_params=pltpu.CompilerParams(vmem_limit_bytes=ATTEND_ROOM),
        cost_estimate=pl.CostEstimate(
            flops=4 * heads * length * length * HD + 2 * length * model * width,
            bytes_accessed=4 * width * length,
            transcendentals=heads * length * length,
        ),
        name="attend",
    )(window, tokens, weight, span)


def attend_back(qkv, out, logs, weight, half, one, window, span):
    width, length = qkv.shape
    heads = width // (3 * HD)
    return pl.pallas_call(
        functools.partial(attend_back_kernel, block=BLOCK),
        out_shape=jax.ShapeDtypeStruct((width, length), bf16),
        in_specs=[SMEM] * 2 + [VMEM] * 6,
        out_specs=VMEM,
        scratch_shapes=[
            pltpu.VMEM((heads, length, HD), bf16),
            pltpu.VMEM((heads, length, HD), bf16),
            pltpu.VMEM((length, BLOCK), f32),
            pltpu.VMEM((heads * HD, length), f32),
            pltpu.VMEM((heads * HD, length), f32),
            pltpu.VMEM((heads * HD, length), bf16),
            pltpu.VMEM((one.shape[0], heads * HD), bf16),
        ],
        compiler_params=pltpu.CompilerParams(vmem_limit_bytes=ATTEND_ROOM),
        cost_estimate=pl.CostEstimate(
            flops=10 * heads * length * length * HD,
            bytes_accessed=6 * width * length,
            transcendentals=heads * length * length,
        ),
        name="attend_back",
    )(window, jnp.full((1,), half, jnp.int32), qkv, span, out, logs, weight, one)


def grad_weight_kernel(tokens_ref, grad_ref, one_ref, mixture_ref, *refs, starts):
    more, out_ref = refs[2:-1], refs[-1]
    up_ref, vectors_ref = refs[0], refs[1]
    dp, full, columns = out_ref.shape
    rows = full - TAIL
    wide = grad_ref.shape[0]
    group = wide // 3
    made = contract(tokens_ref[...], grad_ref[...], ((1,), (1,)))
    out_low = contract(one_ref[...], mixture_ref[...], ((1,), (1,)))
    ones = jnp.ones((TAIL, grad_ref.shape[1]), bf16)
    lane = contract(ones, grad_ref[...], ((1,), (1,)))
    line = lax.broadcasted_iota(jnp.int32, (TAIL, columns), 0)
    bias_row = jnp.concatenate([lane, jnp.zeros((TAIL, columns - wide), f32)], axis=1)
    side = jnp.where(line == 0, bias_row, 0.0) + jnp.where(line == 1, up_ref[0:1, :], 0.0)
    lower = jnp.concatenate([jnp.zeros((2, columns), f32), vectors_ref[0:6, :]], axis=0)
    side = side + lower
    for index in range(dp):
        own = slice(index * rows, (index + 1) * rows)
        left, right, low = made[own], out_low[own], side
        for held, start in zip(more, starts):
            at = index - start
            if not 0 <= at < held.shape[0]:
                continue
            left = left + held[at, 0:rows, 0:wide].astype(f32)
            right = right + held[at, 0:rows, wide:].astype(f32)
            low = low + held[at, rows:, :].astype(f32)
        out_ref[index, 0:rows, 0:wide] = left.astype(bf16)
        out_ref[index, 0:rows, wide:] = right.astype(bf16)
        out_ref[index, rows:, :] = low.astype(bf16)


def grad_weight(dp, tokens, grad, one, mixture, up_row, vectors, more, starts):
    model, length = tokens.shape
    wide, group = grad.shape[0], mixture.shape[0]
    return pl.pallas_call(
        functools.partial(grad_weight_kernel, starts=starts),
        out_shape=jax.ShapeDtypeStruct((dp, model // dp + TAIL, wide + group), bf16),
        in_specs=[VMEM] * (6 + len(more)),
        out_specs=VMEM,
        compiler_params=pltpu.CompilerParams(vmem_limit_bytes=ATTEND_ROOM),
        cost_estimate=pl.CostEstimate(
            flops=2 * length * model * (wide + group),
            bytes_accessed=2 * (length + model) * (wide + group + model),
            transcendentals=0,
        ),
        name="grad_weight",
    )(tokens, grad, one, mixture, up_row, vectors, *more)


def normalize(values):
    average = jnp.mean(values, axis=-1, keepdims=True)
    centred = values - average
    variance = jnp.mean(centred * centred, axis=-1, keepdims=True)
    inv_scale = lax.rsqrt(variance + epsilon)
    return centred * inv_scale, inv_scale


def normalize_back(grad_out, unit_rows, inv_scale, norm_gain):
    grad_unit = grad_out * norm_gain
    middle = grad_unit - jnp.mean(grad_unit, axis=-1, keepdims=True)
    middle = middle - unit_rows * jnp.mean(grad_unit * unit_rows, axis=-1, keepdims=True)
    return inv_scale * middle


def gelu_parts(up_pre):
    normal_cdf = 0.5 * (1.0 + lax.erf(up_pre * root_half))
    return (
        up_pre * normal_cdf,
        normal_cdf + up_pre * inv_root_tau * jnp.exp(-0.5 * up_pre * up_pre),
    )


def tile_kernel(*refs, kernel, steps, tiles):
    def step(index, _):
        views = []
        for ref, tile in zip(refs, tiles):
            if tile is None or steps == 1:
                views.append(ref)
                continue
            size = ref.shape[tile] // steps
            own = pl.ds(pl.multiple_of(index * size, size), size)
            views.append(ref.at[own, :] if tile == 0 else ref.at[:, own])
        kernel(index, *views)
        return 0

    lax.fori_loop(0, steps, step, 0)


def tiled(kernel, name, steps, operands, tiles, shapes, flops):
    shapes, out_tiles = [x for x, _ in shapes], [x for _, x in shapes]
    moved = sum(x.size * x.dtype.itemsize for x in list(operands) + shapes)
    return pl.pallas_call(
        functools.partial(
            tile_kernel, kernel=kernel, steps=steps, tiles=tuple(tiles) + tuple(out_tiles)
        ),
        out_shape=shapes,
        in_specs=[VMEM] * len(operands),
        out_specs=[VMEM] * len(shapes),
        compiler_params=pltpu.CompilerParams(vmem_limit_bytes=TILE_ROOM),
        cost_estimate=pl.CostEstimate(flops=flops, bytes_accessed=moved, transcendentals=0),
        name=name,
    )(*operands)


def shape(*size, dtype=f32):
    return jax.ShapeDtypeStruct(size, dtype)


def vectors_kernel(step, lane_ref, near_ref, far_ref, out_ref):
    model = out_ref.shape[1]
    wide = near_ref.shape[1]
    size = wide // 2
    total = jnp.zeros((SIDE, model), f32)
    lanes = lax.broadcasted_iota(jnp.int32, (size, model), 1)
    for j in range(4):
        held = near_ref if j % 2 == 0 else far_ref
        first = (j // 2) * 3 * size
        place = jnp.where(lanes == lane_ref[:, j : j + 1], 1.0, 0.0).astype(bf16)
        for part in range(3):
            at = first + part * size
            line = model + at // wide * SIDE
            part = held[line : line + SIDE, at % wide : at % wide + size]
            total = total + contract(part, place, ((1,), (0,)))
    out_ref[...] = total


def out_kernel(step, m0, m1, m2, m3, near, far, vectors, tokens, low_ref, turned_ref, unit_ref, scale_ref):
    total = vectors[0:1, :] + tokens[...].astype(f32)
    model, group = total.shape[1], m0.shape[0]
    for index, mixture in enumerate((m0, m1, m2, m3)):
        held = near if index % 2 == 0 else far
        weight = held[0:model, index // 2 * group : (index // 2 + 1) * group]
        total = total + contract(mixture[...], weight, ((0,), (1,)))
    unit, scale = normalize(total)
    unit_ref[...] = unit
    scale_ref[...] = scale
    low = (unit * vectors[2:3, :] + vectors[3:4, :]).astype(bf16)
    low_ref[...] = low
    turned_ref[...] = low.T


def up_kernel(step, low, weight, act_ref, slope_ref):
    model = low.shape[1]
    up_pre = contract(low[...], weight[0:model, :], ((1,), (0,)))
    act, slope = gelu_parts(up_pre + weight[model : model + 1, :].astype(f32))
    act_ref[...] = act.astype(bf16)
    slope_ref[...] = slope.astype(bf16)


def column_sums(step, ref, rows, start=0.0):
    line = lax.broadcasted_iota(jnp.int32, ref.shape, 0)
    made = jnp.zeros(ref.shape, f32)
    for at, values in rows:
        made = made + jnp.where(line == at, jnp.sum(values, axis=0, keepdims=True), 0.0)

    @pl.when(step == 0)
    def _():
        ref[...] = made + start

    @pl.when(step > 0)
    def _():
        ref[...] += made


def down_kernel(
    step, a0, a1, a2, a3, w0, w1, w2, w3, vectors, unit_ref, cotangent, result_ref, grad_ref, low_ref, turned_ref, sums_ref
):
    total = vectors[1:2, :] + unit_ref[...] * vectors[2:3, :] + vectors[3:4, :]
    for act, weight in ((a0, w0), (a1, w1), (a2, w2), (a3, w3)):
        total = total + contract(act[...], weight[...], ((1,), (1,)))
    unit, scale = normalize(total)
    result_ref[...] = (unit * vectors[4:5, :] + vectors[5:6, :]).astype(bf16)
    grad_out = cotangent[...].astype(f32)
    grad = normalize_back(grad_out, unit, scale, vectors[4:5, :])
    grad_ref[...] = grad
    low_ref[...] = grad.astype(bf16)
    turned_ref[...] = grad.astype(bf16).T
    column_sums(step, sums_ref, ((1, grad), (4, grad_out * unit), (5, grad_out)))


def turn_kernel(step, rows, turned_ref):
    turned_ref[...] = rows[...].T


def outer_kernel(turned_ref, right_ref, *refs, added):
    outs = refs[added:]
    at = 0
    for out in outs:
        rows = slice(at, at + out.shape[0])
        made = contract(turned_ref[rows, :], right_ref[...], ((1,), (0,)))
        if added:
            made = made + refs[0][rows, :].astype(f32)
        out[...] = made.astype(bf16)
        at = at + out.shape[0]


def outer(turned, right, cuts=None, arrived=()):
    rows, columns = turned.shape[0], right.shape[1]
    cuts = cuts or [0, rows]
    shapes = [shape(high - low, columns, dtype=bf16) for low, high in zip(cuts, cuts[1:])]
    return pl.pallas_call(
        functools.partial(outer_kernel, added=len(arrived)),
        out_shape=shapes,
        in_specs=[VMEM] * (2 + len(arrived)),
        out_specs=[VMEM] * len(shapes),
        compiler_params=pltpu.CompilerParams(vmem_limit_bytes=TILE_ROOM),
        cost_estimate=pl.CostEstimate(
            flops=2 * turned.size * columns, bytes_accessed=6 * rows * columns, transcendentals=0
        ),
        name="outer",
    )(turned, right, *arrived)


def input_kernel(step, grad, weight, total, out_ref):
    model = total.shape[1]
    made = contract(grad[...], weight[0:model, :], ((0,), (1,)))
    out_ref[...] = (total[...] + made).astype(out_ref.dtype)


def down_end_kernel(own, far, out_ref):
    out_ref[...] = own[...] + far[...].astype(f32)


def slope_kernel(step, low, weight, slope, grad_ref, sums_ref):
    made = contract(low[...], weight[...], ((1,), (0,))) * slope[...].astype(f32)
    made = made.astype(bf16)
    grad_ref[...] = made
    column_sums(step, sums_ref, ((0, made.astype(f32)),))


def first_kernel(
    step, g0, g1, g2, g3, w0, w1, w2, w3, vectors, two, unit_ref, scale, sums_two, grad_ref, turned_ref, sums_ref
):
    total = two[...]
    model = total.shape[1]
    for grad, weight in ((g0, w0), (g1, w1), (g2, w2), (g3, w3)):
        total = total + contract(grad[...], weight[0:model, :], ((1,), (1,)))
    unit = unit_ref[...]
    grad = normalize_back(total, unit, scale[...], vectors[2:3, :])
    grad_ref[...] = grad
    turned_ref[...] = grad.astype(bf16).T
    column_sums(step, sums_ref, ((0, grad), (2, total * unit), (3, total)), sums_two[...])


def per_device(
    tokens,
    doc_lengths,
    w_query,
    w_key,
    w_value,
    w_out,
    w_up,
    w_down,
    b_query,
    b_value,
    b_up,
    b_out,
    b_down,
    gain_one,
    shift_one,
    gain_two,
    shift_two,
    cotangent,
):
    dp, tensor = lax.axis_size("dp"), lax.axis_size("tensor")
    length, model = tokens.shape
    rows = model // dp
    group = w_query.shape[1]
    links = Links(dp, tensor)
    swap = links.swap

    share = b_out.shape[0]
    me = links.me
    mine = lax.axis_index("tensor")
    hidden = w_up.shape[1]
    (packed,) = small_call(
        pack_kernel,
        "pack",
        links,
        [shape(rows + SIDE, 3 * group, dtype=bf16)],
        w_query,
        w_key,
        w_value,
        b_query,
        b_value,
        copied=True,
    )
    ring_attn = GatherRing(links, packed)
    zero = jnp.zeros((share,), f32)
    vectors = jnp.stack([b_out, b_down, gain_one, shift_one, gain_two, shift_two, zero, zero])

    ring_attn.step()
    late_out, late_down = small_call(
        pack_late_kernel,
        "pack_late",
        links,
        [shape(rows, group, dtype=bf16), shape(rows + SIDE, hidden, dtype=bf16)],
        w_out,
        w_down.T,
        vectors,
    )
    late = Box(late_out, late_down, doc_lengths)
    tie(ring_attn, late)
    late_out, late_down, early_lengths = late.live
    ring_attn.step()
    far_late = Box(swap(late_out, 2), swap(late_down, 2))
    span, window = documents(mine, early_lengths, length, BLOCK)
    done = Box(span)
    tie(ring_attn, done)
    span = done.live[0]
    ring_attn.step()
    tie(ring_attn)
    up_chunk, down_chunk = small_call(
        pack_up_kernel,
        "pack_up",
        links,
        [
            shape(rows + SIDE, 2 * group + hidden, dtype=bf16),
            shape(rows, 2 * hidden, dtype=bf16),
        ],
        late_out,
        far_late.live[0],
        w_up,
        late_down,
        far_late.live[1],
        b_up,
    )
    ring_up = GatherRing(links, up_chunk)
    ring_down = GatherRing(links, down_chunk)
    for _ in range(links.ahead - 3):
        ring_attn.step()
    (attn_own,) = ring_attn.full([(0, 3 * group, 0)], rows)

    attn_w = [attn_own, None, None, None]
    qkv, mixture, logs = [None] * 4, [None] * 4, [None] * 4

    def attend_group(j):
        mixture[j], logs[j], qkv[j] = attend(work.live[0], attn_w[j], window, span)
        return Box(mixture[j])

    work = Box(tokens, attn_own)
    tie(ring_attn, ring_up, work)
    attn_w[0] = work.live[1]
    work = Box(work.live[0])
    far = Box(swap(attn_w[0], 2))
    attn_w[1] = swap(attn_w[0], 1)
    ring_up.step()
    done = attend_group(0)
    tie(ring_up, work, done)
    ring_up.step()
    done = attend_group(1)
    tie(ring_up, work, done)
    ring_up.step()
    (tokens_turned,) = tiled(
        turn_kernel, "turn", 4, (work.live[0],), (0,), [(shape(model, length, dtype=bf16), 1)], 0
    )
    turned = Box(tokens_turned)
    tie(ring_up, work, far, turned)
    tokens_turned = turned.live[0]
    attn_w[2] = far.live[0]
    attn_w[3] = swap(attn_w[2], 1)
    for _ in range(links.ahead - 3):
        ring_up.step()
    done = attend_group(2)
    tie(ring_up, work, done, ring_down)
    ring_down.step()
    out_near, up_own = ring_up.full([(0, 2 * group, "all"), (2 * group, hidden, 6)], rows)
    out_far = swap(out_near, 1)
    cuts = [0, model // 3, 2 * model // 3, up_own.shape[0]]
    held, across_up = Box(up_own), []

    def up_across():
        low, high = cuts[len(across_up) : len(across_up) + 2]
        across_up.append(Box(swap(held.live[0][low:high], 2)))
        return across_up[-1]

    moved = up_across()
    done = attend_group(3)
    tie(ring_down, work, done, held, moved)

    ring_down.step()
    moved = up_across()
    count = np.arange(dp * share)
    base = jnp.asarray((count // share * tensor * share + count % share)[:, None], jnp.int32)
    lanes = base + (mine ^ jnp.arange(4, dtype=jnp.int32))[None, :] * share
    (vectors,) = tiled(
        vectors_kernel,
        "vectors",
        1,
        (lanes, out_near, out_far),
        (None,) * 3,
        [(shape(SIDE, model), None)],
        0,
    )
    up_w = [up_own, None, None, None]
    first_low, first_turned, unit_one, scale_one = tiled(
        out_kernel,
        "attention_out",
        1,
        (*mixture, out_near, out_far, vectors, work.live[0]),
        (1,) * 4 + (None,) * 3 + (0,),
        [
            (shape(length, model, dtype=bf16), 0),
            (shape(model, length, dtype=bf16), 1),
            (shape(length, model), 0),
            (shape(length, 1), 0),
        ],
        2 * length * model * model,
    )
    activated, slopes = [None] * 4, [None] * 4

    def up_group(j):
        activated[j], slopes[j] = tiled(
            up_kernel,
            "up",
            1,
            (work.live[0], up_w[j]),
            (0, None),
            [(shape(length, hidden, dtype=bf16), 0)] * 2,
            2 * length * model * hidden,
        )
        return Box(activated[j])

    work = Box(first_low)
    tie(ring_down, work, held, moved)
    up_w[0] = held.live[0]
    moved = up_across()
    up_w[1] = swap(up_w[0], 1)
    ring_down.step()
    done = up_group(0)
    tie(ring_down, work, done, moved)
    for _ in range(links.ahead - 3):
        ring_down.step()
    up_w[2] = jnp.concatenate([box.live[0] for box in across_up])
    up_w[3] = swap(up_w[2], 1)
    done = up_group(1)
    tie(ring_down, work, done)
    down_own, down_across = ring_down.full([(0, hidden, None), (hidden, hidden, None)], rows)
    down_w = [down_own, swap(down_own, 1), down_across, swap(down_across, 1)]
    done = [up_group(2), up_group(3)]
    result, grad_two, grad_two_low, grad_two_turned, sums_two = tiled(
        down_kernel,
        "down",
        2,
        (*activated, *down_w, vectors, unit_one, cotangent),
        (0,) * 4 + (None,) * 5 + (0,) * 2,
        [
            (shape(length, model, dtype=bf16), 0),
            (shape(length, model), 0),
            (shape(length, model, dtype=bf16), 0),
            (shape(model, length, dtype=bf16), 1),
            (shape(SIDE, model), None),
        ],
        8 * length * model * hidden,
    )
    work = Box(grad_two_low)

    def blocks(value):
        return value.reshape(-1, rows, value.shape[-1])

    def grad_down(j):
        return outer(grad_two_turned, activated[j])[0]

    def grad_w_up(j, cuts=None, arrived=()):
        return outer(first_turned, grad_up[j], cuts, arrived)

    grad_up, grad_bias_up = [None] * 4, [None] * 4

    def back_up(j):
        grad_up[j], grad_bias_up[j] = tiled(
            slope_kernel,
            "back_up",
            1,
            (work.live[0], down_w[j], slopes[j]),
            (0, None, 0),
            [(shape(length, hidden, dtype=bf16), 0), (shape(SIDE, hidden), None)],
            2 * length * model * hidden,
        )

    def cuts(total):
        return [0, total * 3 // 8, total * 5 // 8, total]

    sent = Box(grad_down(3), grad_down(1))
    tie(work, sent)
    three, one = (swap(v, 1) for v in sent.live)
    two, zero = grad_down(2), grad_down(0)
    back_up(3)
    three_up = Box(*grad_w_up(3))
    pair = Box(two, zero, three, one)
    tie(work, pair, three_up)
    two, zero, three, one = (blocks(v) for v in pair.live)
    sums_down = ScatterRing(links, [[zero, one], [two, three]])
    sums_down.step()
    three_up = Box(swap(three_up.live[0], 1))
    back_up(2)
    back_up(1)
    back_up(0)
    across = grad_w_up(2, cuts(model), (three_up.live[0],))
    across = Box(*across)
    tie(work, sums_down, across)
    across = across.live
    far_up = [Box(swap(across[0], 2))]
    kept = Box(*grad_w_up(1), *grad_w_up(0), grad_up[0])
    sums_down.step()
    grad_one, grad_one_turned, sums = tiled(
        first_kernel,
        "back_first",
        2,
        (*grad_up, *up_w, vectors, grad_two, unit_one, scale_one, sums_two),
        (0,) * 4 + (None,) * 5 + (0,) * 3 + (None,),
        [
            (shape(length, model), 0),
            (shape(model, length, dtype=bf16), 1),
            (shape(SIDE, model), None),
        ],
        8 * length * model * hidden,
    )
    work = Box(grad_one_turned)
    tie(work, kept, sums_down, far_up[0])
    one_up, zero_up, _ = kept.live
    one_up = Box(swap(one_up, 1))
    far_up.append(Box(swap(across[1], 2)))
    grad_qkv = [None] * 4

    def back_attention(j):
        grad_qkv[j] = attend_back(
            qkv[j],
            mixture[j],
            logs[j],
            out_near if j % 2 == 0 else out_far,
            j // 2,
            work.live[0],
            window,
            span,
        )
        return Box(grad_qkv[j])

    grad_input = Box(grad_one)

    def back_input(j):
        grad_input.live = tiled(
            input_kernel,
            "back_input",
            1,
            (grad_qkv[j], attn_w[j], grad_input.live[0]),
            (1, None, 0),
            [(shape(length, model, dtype=f32 if j else bf16), 0)],
            6 * length * model * group,
        )

    def back_group(j, arrived=(), starts=()):
        return grad_weight(
            dp,
            tokens_turned,
            grad_qkv[j],
            work.live[0],
            mixture[j],
            grad_bias_up[j],
            sums,
            arrived,
            starts,
        )

    sums_down.step()
    back_attention(3)
    three = Box(back_group(3))
    tie(work, three, one_up, far_up[1], sums_down)
    recv = Box(swap(three.live[0], 1))
    far_up.append(Box(swap(across[2], 2)))
    for _ in range(links.ahead - 3):
        sums_down.step()
    done = back_attention(2)
    tie(work, done, recv, far_up[2], sums_down)
    grad_qkv[2] = done.live[0]
    far = blocks(jnp.concatenate([box.live[0] for box in far_up]))
    sums_up = ScatterRing(links, [[blocks(zero_up), blocks(one_up.live[0]), far]])
    sums_up.step()
    down_total, down_far = sums_down.total()
    end_down = Box(swap(down_far, 2))
    two = Box(back_group(2, (recv.live[0],), (0,)))
    back_input(3)
    tie(work, two, sums_up, end_down, grad_input)
    split = cuts(dp)
    far_attn = [Box(swap(two.live[0][split[0] : split[1]], 2))]
    sums_up.step()
    done = back_attention(1)
    tie(work, done, sums_up, far_attn[0])
    grad_qkv[1] = done.live[0]
    far_attn.append(Box(swap(two.live[0][split[1] : split[2]], 2)))
    sums_up.step()
    one = Box(back_group(1))
    back_input(2)
    tie(work, one, far_attn[1], sums_up, grad_input)
    recv = Box(swap(one.live[0], 1))
    far_attn.append(Box(swap(two.live[0][split[2] :], 2)))
    for _ in range(links.ahead - 3):
        sums_up.step()
    done = back_attention(0)
    up_total = Box(*sums_up.total())
    tie(work, done, recv, far_attn[2], up_total)
    grad_qkv[0] = done.live[0]
    arrived = [recv.live[0]] + [box.live[0] for box in far_attn]
    (grad_down_own,) = pl.pallas_call(
        down_end_kernel,
        out_shape=[shape(rows, hidden)],
        in_specs=[VMEM] * 2,
        out_specs=[VMEM],
        compiler_params=pltpu.CompilerParams(vmem_limit_bytes=RING_ROOM),
        name="down_end",
    )(down_total, end_down.live[0])
    ends = Box(grad_down_own, up_total.live[0])
    zero = Box(back_group(0, arrived, (0, *split[:3])), grad_qkv[:2])
    tie(work, zero, ends)
    sums_attn = ScatterRing(links, [[zero.live[0]]])
    grad_qkv[:2] = zero.live[1]
    for j in (1, 0):
        sums_attn.step()
        back_input(j)
        tie(grad_input, sums_attn)
    while sums_attn.count < links.ahead:
        sums_attn.step()
    full = dp * b_query.shape[1]
    full_up = dp * b_up.shape[1]
    *made, held = finish(
        links,
        sums_attn,
        jnp.stack([me, me * tensor + mine]),
        [shape(rows, group)] * 3
        + [shape(group, rows)]
        + [shape(*table.shape) for table in (b_query, b_value, b_up)]
        + [shape(SIDE, share)],
        (
            (0, 0, b_query.shape[1], full),
            (0, 2 * group, b_value.shape[1], full),
            (1, 0, b_up.shape[1], full_up),
        ),
    )
    return (
        result,
        grad_input.live[0],
        *made[:4],
        ends.live[1],
        ends.live[0].T,
        *made[4:],
        *[held[i + 2] for i in range(6)],
    )


def solution(mesh):
    both = P(("dp", "tensor"))
    rows = P(("dp", "tensor"), None)
    down = P("tensor", "dp")
    wide = P("dp", "tensor")
    weights = (wide, wide, wide, down, wide, down, down, down, down)
    return jax.shard_map(
        per_device,
        mesh=mesh,
        in_specs=(rows, P("dp", None)) + weights + (both,) * 6 + (rows,),
        out_specs=(rows, rows) + weights + (both,) * 6,
        check_vma=False,
    )
```
